512 devices in a mesh: vel: 8 (over x, z_hi), sx: 8 (over y), sy: 8 (over z_lo, core).
Axes of the slice: x: 4, y: 8, z: 8 (z_hi: 2, z_lo: 4; z = z_hi * 4 + z_lo), core: 2. Of those that a mesh axis runs over, the one named last changes fastest.
Arguments:
- distribution: bfloat16 [24, 256, 32768], P('sx', 'sy', 'vel'), may hold values from 0.05 to 5, as said below
- plane_weights: bfloat16 [1024, 1024], P(('sx', 'sy')), may hold values from -0.1875 to 0.1875
- depth_weights: bfloat16 [32, 32], replicated, may hold values from -1 to 1
Outputs:
- advanced: bfloat16 [24, 256, 32768], P('sx', 'sy', 'vel')
The draws below stay inside these ranges and needn't reach their ends.
Inputs may be any that keep to these rules, and one draw needn't show every extreme that they name: `distribution`: every entry is positive.
All inputs are finite; a program needn't handle non-finite values.
Results may differ from the reference program's by a relative error of at most 0.0028.
Values may be sent and summed in bfloat16 or wider, within the bound.
No kernel may reach another device: no remote copies, remote signals or barrier semaphores. Data moves between devices by JAX's collectives and lax.ppermute only.
A program may use at most 64 MiB of HBM per device.

```python
import math
import jax
import jax.numpy as jnp
from jax import lax

NVZ = 32
NVX = 32
NVY = 32
NXY = 1024
NVEL = 32768
NROWS = 24
NCOLS = 256


def draw_distribution(key, part):
    full_shape = (NROWS, NCOLS, NVEL)
    depth_share = (jnp.arange(NVEL, dtype=jnp.int32) // (NVX * NVY)).astype(jnp.float32) / (NVZ - 1)
    roughness = jax.random.uniform(key, full_shape, jnp.float32, 0.5, 1.5)
    growth = jnp.exp(math.log(3.0) * depth_share)
    return (roughness * growth).astype(jnp.bfloat16)


def levels(key, dims, shards, low, top_value):
    level, own = 1.0, jax.random.fold_in(key, 6)
    for dim, blocks in shards:
        steps = jnp.exp(jax.random.uniform(jax.random.fold_in(own, dim), (blocks,), jnp.float32, low / len(shards), top_value / len(shards)))
        level = level * jnp.repeat(steps, dims[dim] // blocks).reshape([-1 if axis == dim else 1 for axis in range(len(dims))])
    return level


def normal_values(own_key, extent, scale, limit, cuts=(), kind=jnp.bfloat16):
    drawn = scale * jax.random.normal(own_key, extent, jnp.float32)
    if cuts:
        drawn = drawn * levels(own_key, extent, cuts, -0.22, 0.18)
    return jnp.clip(drawn, -limit, limit).astype(kind)


def setup_inputs(seed: int = 0) -> dict:
    seeds = jax.random.split(jax.random.key(seed), 4)
    distribution = draw_distribution(jax.random.fold_in(seeds[3], 71), 0)
    plane_weights = normal_values(seeds[1], (NXY, NXY), NXY ** -0.5, 0.1875, ((0, 64),))
    depth_weights = normal_values(seeds[2], (NVZ, NVZ), NVZ ** -0.5, 1.0)
    return {"distribution": distribution, "plane_weights": plane_weights, "depth_weights": depth_weights}


COURANT = 0.45
RELAX_RATE = 0.3


def plane_speeds():
    lane_ids = jnp.arange(NVX * NVY, dtype=jnp.int32)
    speed_across = ((lane_ids // NVY).astype(jnp.float32) - (NVX - 1) / 2.0) * (8.0 / NVX)
    speed_along = ((lane_ids % NVY).astype(jnp.float32) - (NVY - 1) / 2.0) * (8.0 / NVY)
    return speed_across, speed_along


def maxwellian(particle_concentration, momentum_across, momentum_along, momentum_depth, motion_work_content, speed_across, speed_along, speed_depth):
    mean_flow_transverse = momentum_across / particle_concentration
    mean_flow_streamwise = momentum_along / particle_concentration
    mean_flow_vertical = momentum_depth / particle_concentration
    cell_heat_level = (motion_work_content / particle_concentration - (mean_flow_transverse ** 2 + mean_flow_streamwise ** 2 + mean_flow_vertical ** 2)) / 3.0
    speed_grid_cell_measure = (8.0 / NVX) * (8.0 / NVY) * (8.0 / NVZ)
    scaling_divisor = particle_concentration * speed_grid_cell_measure / (2.0 * jnp.pi * cell_heat_level) ** 1.5
    maxwellian_width = (speed_across - mean_flow_transverse[:, None, None]) ** 2
    maxwellian_width = maxwellian_width + (speed_along - mean_flow_streamwise[:, None, None]) ** 2
    maxwellian_width = maxwellian_width + (speed_depth[:, None] - mean_flow_vertical[:, None, None]) ** 2
    return scaling_divisor[:, None, None] * jnp.exp(-maxwellian_width / (2.0 * cell_heat_level[:, None, None]))


def reference(distribution, plane_weights, depth_weights):
    speed_across, speed_along = plane_speeds()
    speed_depth = (jnp.arange(NVZ, dtype=jnp.int32).astype(jnp.float32) - (NVZ - 1) / 2.0) * (8.0 / NVZ)
    lanes_total = NVX * NVY
    lattice = distribution.reshape(NROWS, NCOLS, NVZ, lanes_total)
    depth_float = depth_weights.astype(jnp.float32)
    squared = speed_across ** 2 + speed_along ** 2 + speed_depth[:, None] ** 2
    courant_across = COURANT / (4.0 - 4.0 / NVX)
    courant_along = COURANT / (4.0 - 4.0 / NVY)

    def one_row(row_index):
        current = lax.dynamic_index_in_dim(lattice, row_index, 0, keepdims=False).astype(jnp.float32)
        lower_row = lax.dynamic_index_in_dim(lattice, (row_index + NROWS - 1) % NROWS, 0, keepdims=False).astype(jnp.float32)
        upper_row = lax.dynamic_index_in_dim(lattice, (row_index + 1) % NROWS, 0, keepdims=False).astype(jnp.float32)
        particle_concentration = jnp.sum(current, axis=(1, 2))
        momentum_across = jnp.sum(current * speed_across, axis=(1, 2))
        momentum_along = jnp.sum(current * speed_along, axis=(1, 2))
        momentum_depth = jnp.sum(current * speed_depth[:, None], axis=(1, 2))
        motion_work_content = jnp.sum(current * squared, axis=(1, 2))
        equilibrium = maxwellian(particle_concentration, momentum_across, momentum_along, momentum_depth, motion_work_content, speed_across, speed_along, speed_depth)
        deviation = (equilibrium - current).astype(jnp.bfloat16)
        mixed_plane = jnp.dot(deviation.reshape(-1, lanes_total), plane_weights.T, preferred_element_type=jnp.float32)
        mixed_plane = lax.optimization_barrier(mixed_plane.astype(jnp.bfloat16)).astype(jnp.float32)
        mixed_plane = mixed_plane.reshape(NCOLS, NVZ, lanes_total)
        collision = jnp.einsum("zw,cwk->czk", depth_float, mixed_plane, precision=lax.Precision.HIGHEST)
        collision = lax.optimization_barrier(collision.astype(jnp.bfloat16)).astype(jnp.float32)
        left_column = jnp.roll(current, 1, axis=0)
        right_column = jnp.roll(current, -1, axis=0)
        across = jnp.maximum(speed_across, 0.0) * (current - lower_row) + jnp.minimum(speed_across, 0.0) * (upper_row - current)
        along = jnp.maximum(speed_along, 0.0) * (current - left_column) + jnp.minimum(speed_along, 0.0) * (right_column - current)
        advanced = current - (courant_across * across + courant_along * along) + RELAX_RATE * collision
        return advanced.astype(jnp.bfloat16)

    all_rows = lax.map(one_row, jnp.arange(NROWS, dtype=jnp.int32))
    return all_rows.reshape(NROWS, NCOLS, NVZ * lanes_total)
```

```python
import functools

import jax
import jax.numpy as jnp
from jax import lax
from jax.experimental import pallas as pl
from jax.experimental.pallas import tpu as pltpu
from jax.sharding import PartitionSpec as P

NVZ = 32
NVX = 32
NVY = 32
NXY = NVX * NVY
COURANT = 0.45
RELAX_RATE = 0.3
ROWS = 3
COLS = 32
CELLS = ROWS * COLS
PLANES = 4
GROUP = 8
BLOCK = NXY // GROUP
DATA = PLANES * CELLS
CHUNK = DATA + 16
TILE = 16
F32 = jnp.float32
BF16 = jnp.bfloat16


def speed(index, count):
    return (index.astype(F32) - (count - 1) / 2.0) * (8.0 / count)


def lane_speeds(shape, offset):
    lane = lax.broadcasted_iota(jnp.int32, shape, len(shape) - 1) + offset
    return speed(lane // NVY, NVX), speed(lane % NVY, NVY)


def vmem():
    return pl.BlockSpec(memory_space=pltpu.VMEM)


def smem():
    return pl.BlockSpec(memory_space=pltpu.SMEM)


def pack_kernel(place_ref, f_ref, send_ref, low_ref, high_ref, first_ref, last_ref):
    for v in range(GROUP):
        for p in range(PLANES):
            for r in range(ROWS):
                send_ref[v, p * CELLS + r * COLS : p * CELLS + (r + 1) * COLS, :] = f_ref[
                    r, :, p * NXY + v * BLOCK : p * NXY + (v + 1) * BLOCK
                ]
    row = lax.broadcasted_iota(jnp.int32, (16, NXY), 0)
    kind = row % 5
    vx, vy = lane_speeds((16, NXY), 0)
    squared = vx * vx + vy * vy
    rough = squared.astype(BF16).astype(F32)
    one = jnp.ones((16, NXY), F32)
    basis = jnp.where(kind == 1, vx, jnp.where(kind == 2, vy, jnp.where(kind == 4, rough, one)))
    basis = basis.astype(BF16)
    rest = jnp.where(kind == 4, squared - rough, 0.0 * one).astype(BF16)
    contract = (((1,), (1,)), ((), ()))
    column = lax.broadcasted_iota(jnp.int32, (16, CELLS), 0)
    column_kind = column % 5
    total = jnp.zeros((16, CELLS), F32)
    first_plane = place_ref[0] * PLANES
    for p in range(PLANES):
        x = jnp.concatenate([f_ref[r, :, p * NXY : (p + 1) * NXY] for r in range(ROWS)], axis=0)
        sums = lax.dot_general(basis, x, contract, preferred_element_type=F32)
        sums = sums + lax.dot_general(rest, x, contract, preferred_element_type=F32)
        density = lax.dot_general(jnp.ones((16, NXY), BF16), x, contract, preferred_element_type=F32)
        vz = speed(first_plane + p, NVZ)
        total = total + jnp.where(
            column_kind == 3, vz * density, jnp.where(column_kind == 4, sums + vz * vz * density, sums)
        )
    high = total.astype(BF16).astype(F32)
    middle = (total - high).astype(BF16).astype(F32)
    low = (total - high) - middle
    parts = jnp.where(
        column < 5, high, jnp.where(column < 10, middle, jnp.where(column < 15, low, 0.0))
    )
    parts = jnp.concatenate([parts, jnp.zeros((16, 128 - CELLS), F32)], axis=1).astype(BF16)
    for v in range(GROUP):
        send_ref[v, DATA:CHUNK, :] = parts
    for p in range(PLANES):
        half = NXY // 2
        high_ref[:, p * half : (p + 1) * half] = f_ref[ROWS - 1, :, p * NXY + half : (p + 1) * NXY]
        low_ref[:, p * half : (p + 1) * half] = f_ref[0, :, p * NXY : p * NXY + half]
    edge_row = lax.broadcasted_iota(jnp.int32, (8, PLANES * NXY), 0)
    first = jnp.zeros((8, PLANES * NXY), F32)
    last = jnp.zeros((8, PLANES * NXY), F32)
    for r in range(ROWS):
        a = f_ref[r, 0:8, :].astype(F32)[0:1, :]
        b = f_ref[r, COLS - 8 : COLS, :].astype(F32)[7:8, :]
        first = jnp.where(edge_row == r, a, first)
        last = jnp.where(edge_row == r, b, last)
    first_ref[...] = first.astype(BF16)
    last_ref[...] = last.astype(BF16)


def pack(place, f):
    return pl.pallas_call(
        pack_kernel,
        out_shape=(
            jax.ShapeDtypeStruct((GROUP, CHUNK, BLOCK), BF16),
            jax.ShapeDtypeStruct((COLS, PLANES * NXY // 2), BF16),
            jax.ShapeDtypeStruct((COLS, PLANES * NXY // 2), BF16),
            jax.ShapeDtypeStruct((8, PLANES * NXY), BF16),
            jax.ShapeDtypeStruct((8, PLANES * NXY), BF16),
        ),
        in_specs=[smem(), vmem()],
        out_specs=(vmem(),) * 5,
        name="pack",
    )(place, f)


def spread_kernel(depth_ref, out_ref):
    size = NVZ * TILE
    row = lax.broadcasted_iota(jnp.int32, (size, NVZ), 0)
    col = lax.broadcasted_iota(jnp.int32, (size, NVZ), 1)
    pick = jnp.where(row // TILE == col, 1.0, 0.0).astype(BF16)
    left = jnp.dot(pick, depth_ref[...], preferred_element_type=F32).astype(BF16)
    full = lax.dot_general(left, pick, (((1,), (1,)), ((), ())), preferred_element_type=F32)
    i = lax.broadcasted_iota(jnp.int32, (size, size), 0)
    j = lax.broadcasted_iota(jnp.int32, (size, size), 1)
    out_ref[...] = jnp.where(i % TILE == j % TILE, full, 0.0).astype(BF16)


def spread(depth_weights):
    size = NVZ * TILE
    return pl.pallas_call(
        spread_kernel,
        out_shape=jax.ShapeDtypeStruct((size, size), BF16),
        in_specs=[vmem()],
        out_specs=vmem(),
        name="spread",
    )(depth_weights)


def relax_kernel(place_ref, got_ref, mix_ref, send_ref, dev_ref):
    pieces = jnp.concatenate([got_ref[v, DATA:CHUNK, :] for v in range(GROUP)], axis=0)
    i = lax.broadcasted_iota(jnp.int32, (GROUP * 16, 128), 0) % 16
    j = lax.broadcasted_iota(jnp.int32, (GROUP * 16, 128), 1)
    pick = jnp.where((i % 5 == j) & (i < 15), 1.0, 0.0).astype(BF16)
    moments = lax.dot_general(pieces, pick, (((0,), (0,)), ((), ())), preferred_element_type=F32)
    moments = moments[:CELLS, :]
    density = moments[:, 0:1]
    ux = moments[:, 1:2] / density
    uy = moments[:, 2:3] / density
    uz = moments[:, 3:4] / density
    heat = (moments[:, 4:5] / density - (ux * ux + uy * uy + uz * uz)) / 3.0
    measure = (8.0 / NVX) * (8.0 / NVY) * (8.0 / NVZ)
    width = 2.0 * jnp.pi * heat
    scale = density * measure / (width * jnp.sqrt(width))
    inverse = -1.0 / (2.0 * heat)
    vx, vy = lane_speeds((CELLS, BLOCK), place_ref[0] * BLOCK)
    dx = vx - ux
    dy = vy - uy
    plane = scale * jnp.exp((dx * dx + dy * dy) * inverse)
    dz = speed(lax.broadcasted_iota(jnp.int32, (CELLS, 128), 1), NVZ) - uz
    depth = jnp.exp((dz * dz) * inverse)
    for w in range(NVZ):
        v, p = w // PLANES, w % PLANES
        f = got_ref[v, p * CELLS : (p + 1) * CELLS, :].astype(F32)
        deviation = (depth[:, w : w + 1] * plane - f).astype(BF16)
        for t in range(CELLS // TILE):
            dev_ref[w * TILE : (w + 1) * TILE, t * BLOCK : (t + 1) * BLOCK] = deviation[
                t * TILE : (t + 1) * TILE, :
            ]
    mixed = jnp.dot(mix_ref[...], dev_ref[...], preferred_element_type=F32).astype(BF16)
    for w in range(NVZ):
        v, p = w // PLANES, w % PLANES
        for t in range(CELLS // TILE):
            send_ref[v, p * CELLS + t * TILE : p * CELLS + (t + 1) * TILE, :] = mixed[
                w * TILE : (w + 1) * TILE, t * BLOCK : (t + 1) * BLOCK
            ]


def relax(place, got, mix):
    return pl.pallas_call(
        relax_kernel,
        out_shape=jax.ShapeDtypeStruct((GROUP, DATA, BLOCK), BF16),
        in_specs=[smem(), vmem(), vmem()],
        out_specs=vmem(),
        scratch_shapes=[pltpu.VMEM((NVZ * TILE, CELLS // TILE * BLOCK), BF16)],
        name="relax",
    )(place, got, mix)


def advance_kernel(f_ref, back_ref, weights_ref, lower_ref, upper_ref, left_ref, right_ref, out_ref):
    half = NXY // 2
    vx, vy = lane_speeds((COLS, NXY), 0)
    courant_across = COURANT / (4.0 - 4.0 / NVX)
    courant_along = COURANT / (4.0 - 4.0 / NVY)
    cx = courant_across * jnp.abs(vx)
    cy = courant_along * jnp.abs(vy)
    upwind = vy > 0.0
    col = lax.broadcasted_iota(jnp.int32, (COLS, NXY), 0)
    for p in range(PLANES):
        mixed = jnp.concatenate(
            [back_ref[v, p * CELLS : (p + 1) * CELLS, :] for v in range(GROUP)], axis=1
        )
        collision = lax.dot_general(
            mixed, weights_ref[...], (((1,), (1,)), ((), ())), preferred_element_type=F32
        )
        lanes = slice(p * NXY, (p + 1) * NXY)
        first_half = slice(p * NXY, p * NXY + half)
        second_half = slice(p * NXY + half, (p + 1) * NXY)
        packed = slice(p * half, (p + 1) * half)
        for r in range(ROWS):
            current = f_ref[r, :, lanes].astype(F32)
            above = upper_ref[:, packed] if r == ROWS - 1 else f_ref[r + 1, :, first_half]
            below = lower_ref[:, packed] if r == 0 else f_ref[r - 1, :, second_half]
            across = jnp.concatenate([above, below], axis=1).astype(F32)
            left = left_ref[:, lanes].astype(F32)[r : r + 1, :]
            right = right_ref[:, lanes].astype(F32)[r : r + 1, :]
            left = jnp.where(col == 0, left, pltpu.roll(current, 1, 0))
            right = jnp.where(col == COLS - 1, right, pltpu.roll(current, COLS - 1, 0))
            along = jnp.where(upwind, left, right)
            value = current - (cx * (current - across) + cy * (current - along))
            value = value + RELAX_RATE * collision[r * COLS : (r + 1) * COLS, :]
            out_ref[r, :, lanes] = value.astype(BF16)


def advance(f, back, weights, lower, upper, left, right):
    return pl.pallas_call(
        advance_kernel,
        out_shape=jax.ShapeDtypeStruct(f.shape, BF16),
        in_specs=[vmem()] * 7,
        out_specs=vmem(),
        compiler_params=pltpu.CompilerParams(vmem_limit_bytes=48 << 20),
        name="advance",
    )(f, back, weights, lower, upper, left, right)


def ring(axis, step):
    count = lax.axis_size(axis)
    return [(i, (i + step) % count) for i in range(count)]


def local(distribution, plane_weights, depth_weights):
    place = lax.axis_index("vel").astype(jnp.int32).reshape(1)
    send, low, high, first, last = pack(place, distribution)
    got = lax.all_to_all(send, "vel", 0, 0, tiled=True)
    shard = plane_weights.shape[0]
    count = lax.axis_size("sy")
    rows = jnp.broadcast_to(plane_weights[None], (count, shard, NXY))
    rows = lax.all_to_all(rows, "sy", 0, 0, tiled=True).reshape(count * shard, NXY)
    weights = lax.all_gather(rows, "sx", axis=0, tiled=True)
    lower = lax.ppermute(high, "sx", ring("sx", 1))
    upper = lax.ppermute(low, "sx", ring("sx", -1))
    left = lax.ppermute(last, "sy", ring("sy", 1))
    right = lax.ppermute(first, "sy", ring("sy", -1))
    mix = spread(depth_weights)
    back = lax.all_to_all(relax(place, got, mix), "vel", 0, 0, tiled=True)
    return advance(distribution, back, weights, lower, upper, left, right)


def solution(mesh):
    return jax.shard_map(
        local,
        mesh=mesh,
        in_specs=(P("sx", "sy", "vel"), P(("sx", "sy"), None), P()),
        out_specs=P("sx", "sy", "vel"),
        check_vma=False,
    )
```

```python
import jax
import jax.numpy as jnp
import numpy as np
from jax import lax
from jax.experimental import pallas as pl
from jax.experimental.pallas import tpu as pltpu
from jax.sharding import PartitionSpec as P

NVZ = 32
NVX = 32
NVY = 32
NXY = NVX * NVY
COURANT = 0.45
RELAX_RATE = 0.3
ROWS = 3
COLS = 32
CELLS = ROWS * COLS
PLANES = 4
GROUP = 8
BLOCK = NXY // GROUP
DATA = PLANES * CELLS
CHUNK = DATA + 16
TILE = 16
F32 = jnp.float32
BF16 = jnp.bfloat16


def speed(index, count):
    return (index.astype(F32) - (count - 1) / 2.0) * (8.0 / count)


def lane_speeds(shape, offset):
    lane = lax.broadcasted_iota(jnp.int32, shape, len(shape) - 1) + offset
    return speed(lane // NVY, NVX), speed(lane % NVY, NVY)


def vmem():
    return pl.BlockSpec(memory_space=pltpu.VMEM)


def smem():
    return pl.BlockSpec(memory_space=pltpu.SMEM)


def moment_basis():
    lane = np.arange(NXY)
    vx = (lane // NVY - (NVX - 1) / 2.0) * (8.0 / NVX)
    vy = (lane % NVY - (NVY - 1) / 2.0) * (8.0 / NVY)
    squared = (vx * vx + vy * vy).astype(np.float32)
    rough = squared.astype(BF16).astype(np.float32)
    basis = np.zeros((NXY, 128), np.float32)
    for part in range(3):
        basis[:, part * 5] = 1.0
        basis[:, part * 5 + 1] = vx
        basis[:, part * 5 + 2] = vy
        basis[:, part * 5 + 3] = 1.0
        basis[:, part * 5 + 4] = rough
        basis[:, 16 + part * 5 + 4] = squared - rough
        basis[:, 32 + part * 5 + 4] = 1.0
    return basis.astype(BF16)


def pack_kernel(place_ref, f_ref, basis_ref, send_ref):
    lane = lax.broadcasted_iota(jnp.int32, (1, 128), 1)
    first_plane = place_ref[0] * PLANES
    total = jnp.zeros((CELLS, 128), F32)
    for p in range(PLANES):
        x = jnp.concatenate([f_ref[r, :, p * NXY : (p + 1) * NXY] for r in range(ROWS)], axis=0)
        sums = jnp.dot(x, basis_ref[...], preferred_element_type=F32)
        vz = speed(first_plane + p, NVZ)
        factor = jnp.where(lane >= 32, vz * vz, jnp.where((lane < 16) & (lane % 5 == 3), vz, 1.0))
        total = total + sums * factor
        for v in range(GROUP):
            send_ref[v, p * CELLS : (p + 1) * CELLS, :] = x[:, v * BLOCK : (v + 1) * BLOCK]
    total = jnp.transpose(total)
    total = (total[0:16, :] + total[16:32, :]) + total[32:48, :]
    column = lax.broadcasted_iota(jnp.int32, (16, CELLS), 0)
    high = total.astype(BF16).astype(F32)
    middle = (total - high).astype(BF16).astype(F32)
    low = (total - high) - middle
    parts = jnp.where(
        column < 5, high, jnp.where(column < 10, middle, jnp.where(column < 15, low, 0.0))
    )
    parts = jnp.concatenate([parts, jnp.zeros((16, 128 - CELLS), F32)], axis=1).astype(BF16)
    for v in range(GROUP):
        send_ref[v, DATA:CHUNK, :] = parts


def pack(place, f):
    return pl.pallas_call(
        pack_kernel,
        out_shape=jax.ShapeDtypeStruct((GROUP, CHUNK, BLOCK), BF16),
        in_specs=[smem(), vmem(), vmem()],
        out_specs=vmem(),
        name="pack",
    )(place, f, jnp.asarray(moment_basis()))


def edges_kernel(core_ref, f_ref, low_ref, high_ref, inner_ref, outer_ref):
    half = NXY // 2
    for p in range(PLANES):
        rows = slice(p // 2 * COLS, (p // 2 + 1) * COLS)
        lanes = slice(p % 2 * half, (p % 2 + 1) * half)
        high_ref[rows, lanes] = f_ref[ROWS - 1, :, p * NXY + half : (p + 1) * NXY]
        low_ref[rows, lanes] = f_ref[0, :, p * NXY : p * NXY + half]
    edge_row = lax.broadcasted_iota(jnp.int32, (16, NXY), 0)
    first = jnp.zeros((16, NXY), F32)
    last = jnp.zeros((16, NXY), F32)
    for r in range(ROWS):
        for p in range(PLANES):
            lanes = slice(p * NXY, (p + 1) * NXY)
            a = f_ref[r, 0:8, lanes].astype(F32)[0:1, :]
            b = f_ref[r, COLS - 8 : COLS, lanes].astype(F32)[7:8, :]
            first = jnp.where(edge_row == r * PLANES + p, a, first)
            last = jnp.where(edge_row == r * PLANES + p, b, last)
    core = core_ref[0]
    inner_ref[...] = jnp.where(core == 0, last, first).astype(BF16)
    outer_ref[...] = jnp.where(core == 0, first, last).astype(BF16)


def edges(core, f):
    row = jax.ShapeDtypeStruct((2 * COLS, NXY), BF16)
    column = jax.ShapeDtypeStruct((16, NXY), BF16)
    return pl.pallas_call(
        edges_kernel,
        out_shape=(row, row, column, column),
        in_specs=[smem(), vmem()],
        out_specs=(vmem(),) * 4,
        name="edges",
    )(core, f)


def assemble_kernel(where_ref, own_ref, other_ref, out_ref, rows_ref):
    core, z, y = where_ref[0], where_ref[1], where_ref[2]
    far = jnp.where(y % 2 == 0, y + 6, y + 2)
    for m, base in enumerate((y, y + 1, y + 7, far)):
        for i in range(2):
            for j in range(4):
                place = ((base + 4 * i) % 8 * 4 + jnp.bitwise_xor(z, j)) * 2
                block = slice((m * 8 + i * 4 + j) * 16, (m * 8 + i * 4 + j + 1) * 16)
                rows_ref[place + core] = own_ref[block, :]
                rows_ref[place + 1 - core] = other_ref[block, :]
    out_ref[...] = jnp.transpose(rows_ref[...].reshape(NXY, NXY))


def assemble(where, own, other):
    return pl.pallas_call(
        assemble_kernel,
        out_shape=jax.ShapeDtypeStruct((NXY, NXY), BF16),
        in_specs=[smem(), vmem(), vmem()],
        out_specs=vmem(),
        scratch_shapes=[pltpu.VMEM((NXY // 16, 16, NXY), BF16)],
        compiler_params=pltpu.CompilerParams(vmem_limit_bytes=32 << 20),
        name="assemble",
    )(where, own, other)


def spread_kernel(depth_ref, out_ref):
    size = NVZ * TILE
    row = lax.broadcasted_iota(jnp.int32, (size, NVZ), 0)
    col = lax.broadcasted_iota(jnp.int32, (size, NVZ), 1)
    pick = jnp.where(row // TILE == col, 1.0, 0.0).astype(BF16)
    left = jnp.dot(pick, depth_ref[...], preferred_element_type=F32).astype(BF16)
    full = lax.dot_general(left, pick, (((1,), (1,)), ((), ())), preferred_element_type=F32)
    i = lax.broadcasted_iota(jnp.int32, (size, size), 0)
    j = lax.broadcasted_iota(jnp.int32, (size, size), 1)
    out_ref[...] = jnp.where(i % TILE == j % TILE, full, 0.0).astype(BF16)


def spread(depth_weights):
    size = NVZ * TILE
    return pl.pallas_call(
        spread_kernel,
        out_shape=jax.ShapeDtypeStruct((size, size), BF16),
        in_specs=[vmem()],
        out_specs=vmem(),
        name="spread",
    )(depth_weights)


def relax_kernel(place_ref, got_ref, mix_ref, send_ref, dev_ref):
    pieces = jnp.concatenate([got_ref[v, DATA:CHUNK, :] for v in range(GROUP)], axis=0)
    i = lax.broadcasted_iota(jnp.int32, (GROUP * 16, 128), 0) % 16
    j = lax.broadcasted_iota(jnp.int32, (GROUP * 16, 128), 1)
    pick = jnp.where((i % 5 == j) & (i < 15), 1.0, 0.0).astype(BF16)
    moments = lax.dot_general(pieces, pick, (((0,), (0,)), ((), ())), preferred_element_type=F32)
    moments = moments[:CELLS, :]
    density = moments[:, 0:1]
    ux = moments[:, 1:2] / density
    uy = moments[:, 2:3] / density
    uz = moments[:, 3:4] / density
    heat = (moments[:, 4:5] / density - (ux * ux + uy * uy + uz * uz)) / 3.0
    measure = (8.0 / NVX) * (8.0 / NVY) * (8.0 / NVZ)
    width = 2.0 * jnp.pi * heat
    scale = density * measure / (width * jnp.sqrt(width))
    inverse = -1.0 / (2.0 * heat)
    vx, vy = lane_speeds((CELLS, BLOCK), place_ref[0] * BLOCK)
    dx = vx - ux
    dy = vy - uy
    plane = scale * jnp.exp((dx * dx + dy * dy) * inverse)
    dz = speed(lax.broadcasted_iota(jnp.int32, (CELLS, 128), 1), NVZ) - uz
    depth = jnp.exp((dz * dz) * inverse)
    for w in range(NVZ):
        v, p = w // PLANES, w % PLANES
        f = got_ref[v, p * CELLS : (p + 1) * CELLS, :].astype(F32)
        deviation = (depth[:, w : w + 1] * plane - f).astype(BF16)
        for t in range(CELLS // TILE):
            dev_ref[w * TILE : (w + 1) * TILE, t * BLOCK : (t + 1) * BLOCK] = deviation[
                t * TILE : (t + 1) * TILE, :
            ]
    mixed = jnp.dot(mix_ref[...], dev_ref[...], preferred_element_type=F32).astype(BF16)
    for w in range(NVZ):
        v, p = w // PLANES, w % PLANES
        for t in range(CELLS // TILE):
            send_ref[v, p * CELLS + t * TILE : p * CELLS + (t + 1) * TILE, :] = mixed[
                w * TILE : (w + 1) * TILE, t * BLOCK : (t + 1) * BLOCK
            ]


def relax(place, got, mix):
    return pl.pallas_call(
        relax_kernel,
        out_shape=jax.ShapeDtypeStruct((GROUP, DATA, BLOCK), BF16),
        in_specs=[smem(), vmem(), vmem()],
        out_specs=vmem(),
        scratch_shapes=[pltpu.VMEM((NVZ * TILE, CELLS // TILE * BLOCK), BF16)],
        name="relax",
    )(place, got, mix)


def advance_kernel(
    core_ref, f_ref, back_ref, weights_ref, lower_ref, upper_ref, inner_ref, outer_ref, out_ref, mixed_ref
):
    half = NXY // 2
    vx, vy = lane_speeds((COLS, NXY), 0)
    courant_across = COURANT / (4.0 - 4.0 / NVX)
    courant_along = COURANT / (4.0 - 4.0 / NVY)
    cx = courant_across * jnp.abs(vx)
    cy = courant_along * jnp.abs(vy)
    upwind = vy > 0.0
    inner = inner_ref[...].astype(F32)
    outer = outer_ref[...].astype(F32)
    core = core_ref[0]
    left_edge = jnp.where(core == 0, outer, inner)
    right_edge = jnp.where(core == 0, inner, outer)
    col = lax.broadcasted_iota(jnp.int32, (COLS, NXY), 0)
    mixed = jnp.concatenate([back_ref[v] for v in range(GROUP)], axis=1)
    mixed_ref[...] = jnp.dot(mixed, weights_ref[...], preferred_element_type=F32)
    for p in range(PLANES):
        lanes = slice(p * NXY, (p + 1) * NXY)
        first_half = slice(p * NXY, p * NXY + half)
        second_half = slice(p * NXY + half, (p + 1) * NXY)
        rows = slice(p // 2 * COLS, (p // 2 + 1) * COLS)
        packed = slice(p % 2 * half, (p % 2 + 1) * half)
        for r in range(ROWS):
            current = f_ref[r, :, lanes].astype(F32)
            above = upper_ref[rows, packed] if r == ROWS - 1 else f_ref[r + 1, :, first_half]
            below = lower_ref[rows, packed] if r == 0 else f_ref[r - 1, :, second_half]
            across = jnp.concatenate([above, below], axis=1).astype(F32)
            left = left_edge[r * PLANES + p : r * PLANES + p + 1, :]
            right = right_edge[r * PLANES + p : r * PLANES + p + 1, :]
            left = jnp.where(col == 0, left, pltpu.roll(current, 1, 0))
            right = jnp.where(col == COLS - 1, right, pltpu.roll(current, COLS - 1, 0))
            along = jnp.where(upwind, left, right)
            value = current - (cx * (current - across) + cy * (current - along))
            start = p * CELLS + r * COLS
            value = value + RELAX_RATE * mixed_ref[start : start + COLS, :]
            out_ref[r, :, lanes] = value.astype(BF16)


def advance(core, f, back, weights, lower, upper, inner, outer):
    return pl.pallas_call(
        advance_kernel,
        out_shape=jax.ShapeDtypeStruct(f.shape, BF16),
        in_specs=[smem()] + [vmem()] * 7,
        out_specs=vmem(),
        scratch_shapes=[pltpu.VMEM((DATA, NXY), F32)],
        compiler_params=pltpu.CompilerParams(vmem_limit_bytes=48 << 20),
        name="advance",
    )(core, f, back, weights, lower, upper, inner, outer)


def ring(axis, step):
    count = lax.axis_size(axis)
    return [(i, (i + step) % count) for i in range(count)]


def local(distribution, plane_weights, depth_weights):
    place = lax.axis_index("vel").astype(jnp.int32).reshape(1)
    along = lax.axis_index("sy").astype(jnp.int32)
    core = jnp.bitwise_and(along, 1).reshape(1)
    where = jnp.stack([jnp.bitwise_and(along, 1), along >> 1, lax.axis_index("sx").astype(jnp.int32)])
    send = pack(place, distribution)
    got = lax.all_to_all(send, "vel", 0, 0, tiled=True)
    mix = spread(depth_weights)
    low, high, inner, outer = edges(core, distribution)
    flip = lambda bit: [(i, i ^ bit) for i in range(8)]
    held = jnp.concatenate([plane_weights, lax.ppermute(plane_weights, "sy", flip(2))])
    held = jnp.concatenate([held, lax.ppermute(held, "sy", flip(4))])
    held = jnp.concatenate([held, lax.ppermute(held, "sx", flip(4))])
    size = held.shape[0]
    above = lax.ppermute(jnp.concatenate([held, low]), "sx", ring("sx", -1))
    below = lax.ppermute(jnp.concatenate([held, high]), "sx", ring("sx", 1))
    across = lax.ppermute(held, "sx", [(i, (i + 2) % 8 if i % 2 == 0 else (i - 2) % 8) for i in range(8)])
    outer = lax.ppermute(outer, "sy", [(i, (i + 1) % 8 if i % 2 else (i - 1) % 8) for i in range(8)])
    own = jnp.concatenate([held, above[:size], below[:size], across, inner])
    other = lax.ppermute(own, "sy", flip(1))
    weights = assemble(where, own, other)
    back = lax.all_to_all(relax(place, got, mix), "vel", 0, 0, tiled=True)
    return advance(
        core, distribution, back, weights, below[size:], above[size:], other[4 * size :], outer
    )


def solution(mesh):
    return jax.shard_map(
        local,
        mesh=mesh,
        in_specs=(P("sx", "sy", "vel"), P(("sx", "sy"), None), P()),
        out_specs=P("sx", "sy", "vel"),
        check_vma=False,
    )
```

```python
import jax
import jax.numpy as jnp
import numpy as np
from jax import lax
from jax.experimental import pallas as pl
from jax.experimental.pallas import tpu as pltpu
from jax.sharding import PartitionSpec as P

NVZ = 32
NVX = 32
NVY = 32
NXY = NVX * NVY
COURANT = 0.45
RELAX_RATE = 0.3
ROWS = 3
COLS = 32
CELLS = ROWS * COLS
PLANES = 4
GROUP = 8
BLOCK = NXY // GROUP
DATA = PLANES * CELLS
CHUNK = DATA + 16
TILE = 16
LIMIT = 16 << 20
F32 = jnp.float32
BF16 = jnp.bfloat16


def speed(index, count):
    return (index.astype(F32) - (count - 1) / 2.0) * (8.0 / count)


def lane_speeds(shape, offset):
    lane = lax.broadcasted_iota(jnp.int32, shape, len(shape) - 1) + offset
    return speed(lane // NVY, NVX), speed(lane % NVY, NVY)


def vmem():
    return pl.BlockSpec(memory_space=pltpu.VMEM)


def smem():
    return pl.BlockSpec(memory_space=pltpu.SMEM)


def moment_basis():
    lane = np.arange(NXY)
    vx = (lane // NVY - (NVX - 1) / 2.0) * (8.0 / NVX)
    vy = (lane % NVY - (NVY - 1) / 2.0) * (8.0 / NVY)
    squared = (vx * vx + vy * vy).astype(np.float32)
    rough = squared.astype(BF16).astype(np.float32)
    basis = np.zeros((NXY, 128), np.float32)
    for part in range(3):
        basis[:, part * 5] = 1.0
        basis[:, part * 5 + 1] = vx
        basis[:, part * 5 + 2] = vy
        basis[:, part * 5 + 3] = 1.0
        basis[:, part * 5 + 4] = rough
        basis[:, 16 + part * 5 + 4] = squared - rough
        basis[:, 32 + part * 5 + 4] = 1.0
    return basis.astype(BF16)


def pack_kernel(place_ref, f_ref, basis_ref, send_ref):
    lane = lax.broadcasted_iota(jnp.int32, (1, 128), 1)
    first_plane = place_ref[0] * PLANES
    total = jnp.zeros((CELLS, 128), F32)
    for p in range(PLANES):
        x = jnp.concatenate([f_ref[r, :, p * NXY : (p + 1) * NXY] for r in range(ROWS)], axis=0)
        sums = jnp.dot(x, basis_ref[...], preferred_element_type=F32)
        vz = speed(first_plane + p, NVZ)
        factor = jnp.where(lane >= 32, vz * vz, jnp.where((lane < 16) & (lane % 5 == 3), vz, 1.0))
        total = total + sums * factor
        for v in range(GROUP):
            send_ref[v, p * CELLS : (p + 1) * CELLS, :] = x[:, v * BLOCK : (v + 1) * BLOCK]
    total = jnp.transpose(total)
    total = (total[0:16, :] + total[16:32, :]) + total[32:48, :]
    column = lax.broadcasted_iota(jnp.int32, (16, CELLS), 0)
    high = total.astype(BF16).astype(F32)
    middle = (total - high).astype(BF16).astype(F32)
    low = (total - high) - middle
    parts = jnp.where(
        column < 5, high, jnp.where(column < 10, middle, jnp.where(column < 15, low, 0.0))
    )
    parts = jnp.concatenate([parts, jnp.zeros((16, 128 - CELLS), F32)], axis=1).astype(BF16)
    for v in range(GROUP):
        send_ref[v, DATA:CHUNK, :] = parts


def pack(place, f):
    return pl.pallas_call(
        pack_kernel,
        out_shape=jax.ShapeDtypeStruct((GROUP, CHUNK, BLOCK), BF16),
        in_specs=[smem(), vmem(), vmem()],
        out_specs=vmem(),
        compiler_params=pltpu.CompilerParams(vmem_limit_bytes=LIMIT),
        name="pack",
    )(place, f, jnp.asarray(moment_basis()))


def edges_kernel(core_ref, f_ref, low_ref, high_ref, inner_ref, outer_ref):
    half = NXY // 2
    for p in range(PLANES):
        rows = slice(p // 2 * COLS, (p // 2 + 1) * COLS)
        lanes = slice(p % 2 * half, (p % 2 + 1) * half)
        high_ref[rows, lanes] = f_ref[ROWS - 1, :, p * NXY + half : (p + 1) * NXY]
        low_ref[rows, lanes] = f_ref[0, :, p * NXY : p * NXY + half]
    edge_row = lax.broadcasted_iota(jnp.int32, (16, NXY), 0)
    first = jnp.zeros((16, NXY), F32)
    last = jnp.zeros((16, NXY), F32)
    for r in range(ROWS):
        for p in range(PLANES):
            lanes = slice(p * NXY, (p + 1) * NXY)
            a = f_ref[r, 0:8, lanes].astype(F32)[0:1, :]
            b = f_ref[r, COLS - 8 : COLS, lanes].astype(F32)[7:8, :]
            first = jnp.where(edge_row == r * PLANES + p, a, first)
            last = jnp.where(edge_row == r * PLANES + p, b, last)
    core = core_ref[0]
    inner_ref[...] = jnp.where(core == 0, last, first).astype(BF16)
    outer_ref[...] = jnp.where(core == 0, first, last).astype(BF16)


def edges(core, f):
    row = jax.ShapeDtypeStruct((2 * COLS, NXY), BF16)
    column = jax.ShapeDtypeStruct((16, NXY), BF16)
    return pl.pallas_call(
        edges_kernel,
        out_shape=(row, row, column, column),
        in_specs=[smem(), vmem()],
        out_specs=(vmem(),) * 4,
        compiler_params=pltpu.CompilerParams(vmem_limit_bytes=LIMIT),
        name="edges",
    )(core, f)


def assemble_kernel(where_ref, own_ref, other_ref, out_ref, inner_ref, rows_ref):
    core, z, y = where_ref[0], where_ref[1], where_ref[2]
    far = jnp.where(y % 2 == 0, y + 6, y + 2)
    for m, base in enumerate((y, y + 1, y + 7, far)):
        for i in range(2):
            for j in range(4):
                place = ((base + 4 * i) % 8 * 4 + jnp.bitwise_xor(z, j)) * 2
                block = slice((m * 8 + i * 4 + j) * 16, (m * 8 + i * 4 + j + 1) * 16)
                rows_ref[place + core] = own_ref[block, :]
                rows_ref[place + 1 - core] = other_ref[block, :]
    inner_ref[...] = other_ref[NXY // 2 : NXY // 2 + 16, :]
    out_ref[...] = jnp.transpose(rows_ref[...].reshape(NXY, NXY))


def assemble(where, own, other):
    return pl.pallas_call(
        assemble_kernel,
        out_shape=(
            jax.ShapeDtypeStruct((NXY, NXY), BF16),
            jax.ShapeDtypeStruct((16, NXY), BF16),
        ),
        in_specs=[smem(), vmem(), vmem()],
        out_specs=(vmem(), vmem()),
        scratch_shapes=[pltpu.VMEM((NXY // 16, 16, NXY), BF16)],
        compiler_params=pltpu.CompilerParams(vmem_limit_bytes=LIMIT),
        name="assemble",
    )(where, own, other)


def spread_kernel(depth_ref, out_ref):
    size = NVZ * TILE
    row = lax.broadcasted_iota(jnp.int32, (size, NVZ), 0)
    col = lax.broadcasted_iota(jnp.int32, (size, NVZ), 1)
    pick = jnp.where(row // TILE == col, 1.0, 0.0).astype(BF16)
    left = jnp.dot(pick, depth_ref[...], preferred_element_type=F32).astype(BF16)
    full = lax.dot_general(left, pick, (((1,), (1,)), ((), ())), preferred_element_type=F32)
    i = lax.broadcasted_iota(jnp.int32, (size, size), 0)
    j = lax.broadcasted_iota(jnp.int32, (size, size), 1)
    out_ref[...] = jnp.where(i % TILE == j % TILE, full, 0.0).astype(BF16)


def spread(depth_weights):
    size = NVZ * TILE
    return pl.pallas_call(
        spread_kernel,
        out_shape=jax.ShapeDtypeStruct((size, size), BF16),
        in_specs=[vmem()],
        out_specs=vmem(),
        compiler_params=pltpu.CompilerParams(vmem_limit_bytes=LIMIT),
        name="spread",
    )(depth_weights)


def relax_kernel(place_ref, got_ref, mix_ref, send_ref, dev_ref):
    pieces = jnp.concatenate([got_ref[v, DATA:CHUNK, :] for v in range(GROUP)], axis=0)
    i = lax.broadcasted_iota(jnp.int32, (GROUP * 16, 128), 0) % 16
    j = lax.broadcasted_iota(jnp.int32, (GROUP * 16, 128), 1)
    pick = jnp.where((i % 5 == j) & (i < 15), 1.0, 0.0).astype(BF16)
    moments = lax.dot_general(pieces, pick, (((0,), (0,)), ((), ())), preferred_element_type=F32)
    moments = moments[:CELLS, :]
    density = moments[:, 0:1]
    ux = moments[:, 1:2] / density
    uy = moments[:, 2:3] / density
    uz = moments[:, 3:4] / density
    heat = (moments[:, 4:5] / density - (ux * ux + uy * uy + uz * uz)) / 3.0
    measure = (8.0 / NVX) * (8.0 / NVY) * (8.0 / NVZ)
    width = 2.0 * jnp.pi * heat
    scale = density * measure / (width * jnp.sqrt(width))
    inverse = -1.0 / (2.0 * heat)
    vx, vy = lane_speeds((CELLS, BLOCK), place_ref[0] * BLOCK)
    dx = vx - ux
    dy = vy - uy
    plane = scale * jnp.exp((dx * dx + dy * dy) * inverse)
    dz = speed(lax.broadcasted_iota(jnp.int32, (CELLS, 128), 1), NVZ) - uz
    depth = jnp.exp((dz * dz) * inverse)
    for w in range(NVZ):
        v, p = w // PLANES, w % PLANES
        f = got_ref[v, p * CELLS : (p + 1) * CELLS, :].astype(F32)
        deviation = (depth[:, w : w + 1] * plane - f).astype(BF16)
        for t in range(CELLS // TILE):
            dev_ref[w * TILE : (w + 1) * TILE, t * BLOCK : (t + 1) * BLOCK] = deviation[
                t * TILE : (t + 1) * TILE, :
            ]
    mixed = jnp.dot(mix_ref[...], dev_ref[...], preferred_element_type=F32).astype(BF16)
    for w in range(NVZ):
        v, p = w // PLANES, w % PLANES
        for t in range(CELLS // TILE):
            send_ref[v, p * CELLS + t * TILE : p * CELLS + (t + 1) * TILE, :] = mixed[
                w * TILE : (w + 1) * TILE, t * BLOCK : (t + 1) * BLOCK
            ]


def relax(place, got, mix):
    return pl.pallas_call(
        relax_kernel,
        out_shape=jax.ShapeDtypeStruct((GROUP, DATA, BLOCK), BF16),
        in_specs=[smem(), vmem(), vmem()],
        out_specs=vmem(),
        scratch_shapes=[pltpu.VMEM((NVZ * TILE, CELLS // TILE * BLOCK), BF16)],
        compiler_params=pltpu.CompilerParams(vmem_limit_bytes=LIMIT),
        name="relax",
    )(place, got, mix)


def advance_kernel(
    core_ref, f_ref, back_ref, weights_ref, lower_ref, upper_ref, inner_ref, outer_ref, out_ref, mixed_ref
):
    half = NXY // 2
    vx, vy = lane_speeds((COLS, NXY), 0)
    courant_across = COURANT / (4.0 - 4.0 / NVX)
    courant_along = COURANT / (4.0 - 4.0 / NVY)
    cx = courant_across * jnp.abs(vx)
    cy = courant_along * jnp.abs(vy)
    upwind = vy > 0.0
    edge = lower_ref.shape[0] - 2 * COLS
    inner = inner_ref[...].astype(F32)
    outer = outer_ref[...].astype(F32)
    core = core_ref[0]
    left_edge = jnp.where(core == 0, outer, inner)
    right_edge = jnp.where(core == 0, inner, outer)
    col = lax.broadcasted_iota(jnp.int32, (COLS, NXY), 0)
    mixed = jnp.concatenate([back_ref[v] for v in range(GROUP)], axis=1)
    mixed_ref[...] = jnp.dot(mixed, weights_ref[...], preferred_element_type=F32)
    for p in range(PLANES):
        lanes = slice(p * NXY, (p + 1) * NXY)
        first_half = slice(p * NXY, p * NXY + half)
        second_half = slice(p * NXY + half, (p + 1) * NXY)
        rows = slice(edge + p // 2 * COLS, edge + (p // 2 + 1) * COLS)
        packed = slice(p % 2 * half, (p % 2 + 1) * half)
        for r in range(ROWS):
            current = f_ref[r, :, lanes].astype(F32)
            above = upper_ref[rows, packed] if r == ROWS - 1 else f_ref[r + 1, :, first_half]
            below = lower_ref[rows, packed] if r == 0 else f_ref[r - 1, :, second_half]
            across = jnp.concatenate([above, below], axis=1).astype(F32)
            left = left_edge[r * PLANES + p : r * PLANES + p + 1, :]
            right = right_edge[r * PLANES + p : r * PLANES + p + 1, :]
            left = jnp.where(col == 0, left, pltpu.roll(current, 1, 0))
            right = jnp.where(col == COLS - 1, right, pltpu.roll(current, COLS - 1, 0))
            along = jnp.where(upwind, left, right)
            value = current - (cx * (current - across) + cy * (current - along))
            start = p * CELLS + r * COLS
            value = value + RELAX_RATE * mixed_ref[start : start + COLS, :]
            out_ref[r, :, lanes] = value.astype(BF16)


def advance(core, f, back, weights, lower, upper, inner, outer):
    return pl.pallas_call(
        advance_kernel,
        out_shape=jax.ShapeDtypeStruct(f.shape, BF16),
        in_specs=[smem()] + [vmem()] * 7,
        out_specs=vmem(),
        scratch_shapes=[pltpu.VMEM((DATA, NXY), F32)],
        compiler_params=pltpu.CompilerParams(vmem_limit_bytes=LIMIT),
        name="advance",
    )(core, f, back, weights, lower, upper, inner, outer)


def ring(axis, step):
    count = lax.axis_size(axis)
    return [(i, (i + step) % count) for i in range(count)]


def local(distribution, plane_weights, depth_weights):
    place = lax.axis_index("vel").astype(jnp.int32).reshape(1)
    along = lax.axis_index("sy").astype(jnp.int32)
    core = jnp.bitwise_and(along, 1).reshape(1)
    where = jnp.stack([jnp.bitwise_and(along, 1), along >> 1, lax.axis_index("sx").astype(jnp.int32)])
    flip = lambda bit: [(i, i ^ bit) for i in range(8)]
    send = pack(place, distribution)
    held = jnp.concatenate([plane_weights, lax.ppermute(plane_weights, "sy", flip(2))])
    send, held = lax.optimization_barrier((send, held))
    held = jnp.concatenate([held, lax.ppermute(held, "sy", flip(4))])
    send, held = lax.optimization_barrier((send, held))
    got = lax.all_to_all(send, "vel", 0, 0, tiled=True)
    mix = spread(depth_weights)
    low, high, inner, outer = edges(core, distribution)
    held = jnp.concatenate([held, lax.ppermute(held, "sx", flip(4))])
    size = held.shape[0]
    above = lax.ppermute(jnp.concatenate([held, low]), "sx", ring("sx", -1))
    below = lax.ppermute(jnp.concatenate([held, high]), "sx", ring("sx", 1))
    across = lax.ppermute(held, "sx", [(i, (i + 2) % 8 if i % 2 == 0 else (i - 2) % 8) for i in range(8)])
    outer = lax.ppermute(outer, "sy", [(i, (i + 1) % 8 if i % 2 else (i - 1) % 8) for i in range(8)])
    own = jnp.concatenate([held, above[:size], below[:size], across, inner])
    other = lax.ppermute(own, "sy", flip(1))
    weights, inner = assemble(where, own, other)
    back = lax.all_to_all(relax(place, got, mix), "vel", 0, 0, tiled=True)
    return advance(
        core, distribution, back, weights, below, above, inner, outer
    )


def solution(mesh):
    return jax.shard_map(
        local,
        mesh=mesh,
        in_specs=(P("sx", "sy", "vel"), P(("sx", "sy"), None), P()),
        out_specs=P("sx", "sy", "vel"),
        check_vma=False,
    )
```

```python
import jax
import jax.numpy as jnp
import numpy as np
from jax import lax
from jax.experimental import pallas as pl
from jax.experimental.pallas import tpu as pltpu
from jax.sharding import PartitionSpec as P

NVZ = 32
NVX = 32
NVY = 32
NXY = NVX * NVY
COURANT = 0.45
RELAX_RATE = 0.3
ROWS = 3
COLS = 32
CELLS = ROWS * COLS
PLANES = 4
GROUP = 8
BLOCK = NXY // GROUP
DATA = PLANES * CELLS
CHUNK = DATA + 16
TILE = 16
LIMIT = 16 << 20
F32 = jnp.float32
BF16 = jnp.bfloat16


def speed(index, count):
    return (index.astype(F32) - (count - 1) / 2.0) * (8.0 / count)


def lane_speeds(shape, offset):
    lane = lax.broadcasted_iota(jnp.int32, shape, len(shape) - 1) + offset
    return speed(lane // NVY, NVX), speed(lane % NVY, NVY)


def vmem():
    return pl.BlockSpec(memory_space=pltpu.VMEM)


def hbm():
    return pl.BlockSpec(memory_space=pltpu.HBM)


def smem():
    return pl.BlockSpec(memory_space=pltpu.SMEM)


def moment_basis():
    lane = np.arange(NXY)
    vx = (lane // NVY - (NVX - 1) / 2.0) * (8.0 / NVX)
    vy = (lane % NVY - (NVY - 1) / 2.0) * (8.0 / NVY)
    squared = (vx * vx + vy * vy).astype(np.float32)
    rough = squared.astype(BF16).astype(np.float32)
    basis = np.zeros((NXY, 128), np.float32)
    for part in range(3):
        basis[:, part * 5] = 1.0
        basis[:, part * 5 + 1] = vx
        basis[:, part * 5 + 2] = vy
        basis[:, part * 5 + 3] = 1.0
        basis[:, part * 5 + 4] = rough
        basis[:, 16 + part * 5 + 4] = squared - rough
        basis[:, 32 + part * 5 + 4] = 1.0
    return basis.astype(BF16)


def pack_kernel(place_ref, f_ref, basis_ref, send_ref, x_ref, base_ref, out_ref, in_sem, base_sem, out_sem):
    def load(p):
        lanes = pl.ds(p * NXY, NXY)
        return pltpu.make_async_copy(f_ref.at[:, :, lanes], x_ref.at[p], in_sem.at[p])

    def store(p):
        rows = pl.ds(p * CELLS, CELLS)
        return pltpu.make_async_copy(out_ref.at[:, rows, :], send_ref.at[:, rows, :], out_sem.at[p])

    base = pltpu.make_async_copy(basis_ref, base_ref, base_sem)
    load(0).start()
    base.start()
    for p in range(1, PLANES):
        load(p).start()
    lane = lax.broadcasted_iota(jnp.int32, (1, 128), 1)
    first_plane = place_ref[0] * PLANES
    total = jnp.zeros((CELLS, 128), F32)
    for p in range(PLANES):
        load(p).wait()
        x = x_ref[p].reshape(CELLS, NXY)
        for v in range(GROUP):
            out_ref[v, p * CELLS : (p + 1) * CELLS, :] = x[:, v * BLOCK : (v + 1) * BLOCK]
        store(p).start()
        if p == 0:
            base.wait()
        sums = jnp.dot(x, base_ref[...], preferred_element_type=F32)
        vz = speed(first_plane + p, NVZ)
        factor = jnp.where(lane >= 32, vz * vz, jnp.where((lane < 16) & (lane % 5 == 3), vz, 1.0))
        total = total + sums * factor
    total = jnp.transpose(total)
    total = (total[0:16, :] + total[16:32, :]) + total[32:48, :]
    column = lax.broadcasted_iota(jnp.int32, (16, CELLS), 0)
    high = total.astype(BF16).astype(F32)
    middle = (total - high).astype(BF16).astype(F32)
    low = (total - high) - middle
    parts = jnp.where(
        column < 5, high, jnp.where(column < 10, middle, jnp.where(column < 15, low, 0.0))
    )
    parts = jnp.concatenate([parts, jnp.zeros((16, 128 - CELLS), F32)], axis=1).astype(BF16)
    for v in range(GROUP):
        out_ref[v, DATA:CHUNK, :] = parts
    tail = pl.ds(DATA, CHUNK - DATA)
    last = pltpu.make_async_copy(
        out_ref.at[:, tail, :], send_ref.at[:, tail, :], out_sem.at[PLANES]
    )
    last.start()
    for p in range(PLANES):
        store(p).wait()
    last.wait()


def pack(place, f):
    basis = jnp.asarray(moment_basis())
    f, basis = (pltpu.with_memory_space_constraint(x, pltpu.HBM) for x in (f, basis))
    return pl.pallas_call(
        pack_kernel,
        out_shape=jax.ShapeDtypeStruct((GROUP, CHUNK, BLOCK), BF16),
        in_specs=[smem(), hbm(), hbm()],
        out_specs=hbm(),
        scratch_shapes=[
            pltpu.VMEM((PLANES, ROWS, COLS, NXY), BF16),
            pltpu.VMEM((NXY, 128), BF16),
            pltpu.VMEM((GROUP, CHUNK, BLOCK), BF16),
            pltpu.SemaphoreType.DMA((PLANES,)),
            pltpu.SemaphoreType.DMA(()),
            pltpu.SemaphoreType.DMA((PLANES + 1,)),
        ],
        compiler_params=pltpu.CompilerParams(vmem_limit_bytes=LIMIT),
        name="pack",
    )(place, f, basis)


def edges_kernel(core_ref, f_ref, low_ref, high_ref, inner_ref, outer_ref):
    half = NXY // 2
    for p in range(PLANES):
        rows = slice(p // 2 * COLS, (p // 2 + 1) * COLS)
        lanes = slice(p % 2 * half, (p % 2 + 1) * half)
        high_ref[rows, lanes] = f_ref[ROWS - 1, :, p * NXY + half : (p + 1) * NXY]
        low_ref[rows, lanes] = f_ref[0, :, p * NXY : p * NXY + half]
    edge_row = lax.broadcasted_iota(jnp.int32, (16, NXY), 0)
    first = jnp.zeros((16, NXY), F32)
    last = jnp.zeros((16, NXY), F32)
    for r in range(ROWS):
        for p in range(PLANES):
            lanes = slice(p * NXY, (p + 1) * NXY)
            a = f_ref[r, 0:8, lanes].astype(F32)[0:1, :]
            b = f_ref[r, COLS - 8 : COLS, lanes].astype(F32)[7:8, :]
            first = jnp.where(edge_row == r * PLANES + p, a, first)
            last = jnp.where(edge_row == r * PLANES + p, b, last)
    core = core_ref[0]
    inner_ref[...] = jnp.where(core == 0, last, first).astype(BF16)
    outer_ref[...] = jnp.where(core == 0, first, last).astype(BF16)


def edges(core, f):
    row = jax.ShapeDtypeStruct((2 * COLS, NXY), BF16)
    column = jax.ShapeDtypeStruct((16, NXY), BF16)
    return pl.pallas_call(
        edges_kernel,
        out_shape=(row, row, column, column),
        in_specs=[smem(), vmem()],
        out_specs=(vmem(),) * 4,
        compiler_params=pltpu.CompilerParams(vmem_limit_bytes=LIMIT),
        name="edges",
    )(core, f)


def join_kernel(held_ref, above_ref, below_ref, across_ref, inner_ref, out_ref, sem):
    size = held_ref.shape[0]
    copies = []
    for m, ref in enumerate((held_ref, above_ref, below_ref, across_ref)):
        copies.append(
            pltpu.make_async_copy(
                ref.at[pl.ds(0, size)], out_ref.at[pl.ds(m * size, size)], sem.at[m]
            )
        )
    copies.append(
        pltpu.make_async_copy(inner_ref, out_ref.at[pl.ds(4 * size, 16)], sem.at[4])
    )
    for copy in copies:
        copy.start()
    for copy in copies:
        copy.wait()


def join(held, above, below, across, inner):
    return pl.pallas_call(
        join_kernel,
        out_shape=jax.ShapeDtypeStruct((4 * held.shape[0] + 16, NXY), BF16),
        in_specs=[hbm()] * 5,
        out_specs=hbm(),
        scratch_shapes=[pltpu.SemaphoreType.DMA((5,))],
        compiler_params=pltpu.CompilerParams(vmem_limit_bytes=LIMIT),
        name="join",
    )(held, above, below, across, inner)


def assemble_kernel(where_ref, own_ref, other_ref, out_hbm, inner_hbm, rows_ref, turned_ref, sem):
    half = NXY // 2
    edge = pltpu.make_async_copy(other_ref.at[pl.ds(half, 16)], inner_hbm, sem.at[1])
    edge.start()
    core, z, y = where_ref[0], where_ref[1], where_ref[2]
    far = jnp.where(y % 2 == 0, y + 6, y + 2)
    for m, base in enumerate((y, y + 1, y + 7, far)):
        for i in range(2):
            for j in range(4):
                place = ((base + 4 * i) % 8 * 4 + jnp.bitwise_xor(z, j)) * 2
                block = slice((m * 8 + j * 2 + i) * 16, (m * 8 + j * 2 + i + 1) * 16)
                rows_ref[place + core] = own_ref[block, :]
                rows_ref[place + 1 - core] = other_ref[block, :]
    turned_ref[...] = jnp.transpose(rows_ref[...].reshape(NXY, NXY))
    copy = pltpu.make_async_copy(turned_ref, out_hbm, sem.at[0])
    copy.start()
    edge.wait()
    copy.wait()


def assemble(where, own, other):
    return pl.pallas_call(
        assemble_kernel,
        out_shape=(pltpu.HBM((NXY, NXY), BF16), jax.ShapeDtypeStruct((16, NXY), BF16)),
        in_specs=[smem(), vmem(), vmem()],
        out_specs=(hbm(), hbm()),
        scratch_shapes=[
            pltpu.VMEM((NXY // 16, 16, NXY), BF16),
            pltpu.VMEM((NXY, NXY), BF16),
            pltpu.SemaphoreType.DMA((2,)),
        ],
        compiler_params=pltpu.CompilerParams(vmem_limit_bytes=LIMIT),
        name="assemble",
    )(where, own, other)


def spread_kernel(depth_ref, out_ref):
    size = NVZ * TILE
    row = lax.broadcasted_iota(jnp.int32, (size, NVZ), 0)
    col = lax.broadcasted_iota(jnp.int32, (size, NVZ), 1)
    pick = jnp.where(row // TILE == col, 1.0, 0.0).astype(BF16)
    left = jnp.dot(pick, depth_ref[...], preferred_element_type=F32).astype(BF16)
    full = lax.dot_general(left, pick, (((1,), (1,)), ((), ())), preferred_element_type=F32)
    i = lax.broadcasted_iota(jnp.int32, (size, size), 0)
    j = lax.broadcasted_iota(jnp.int32, (size, size), 1)
    out_ref[...] = jnp.where(i % TILE == j % TILE, full, 0.0).astype(BF16)


def spread(depth_weights):
    size = NVZ * TILE
    return pl.pallas_call(
        spread_kernel,
        out_shape=jax.ShapeDtypeStruct((size, size), BF16),
        in_specs=[vmem()],
        out_specs=vmem(),
        compiler_params=pltpu.CompilerParams(vmem_limit_bytes=LIMIT),
        name="spread",
    )(depth_weights)


def relax_kernel(place_ref, got_ref, mix_ref, send_ref, dev_ref):
    pieces = jnp.concatenate([got_ref[v, DATA:CHUNK, :] for v in range(GROUP)], axis=0)
    i = lax.broadcasted_iota(jnp.int32, (GROUP * 16, 128), 0) % 16
    j = lax.broadcasted_iota(jnp.int32, (GROUP * 16, 128), 1)
    pick = jnp.where((i % 5 == j) & (i < 15), 1.0, 0.0).astype(BF16)
    moments = lax.dot_general(pieces, pick, (((0,), (0,)), ((), ())), preferred_element_type=F32)
    moments = moments[:CELLS, :]
    density = moments[:, 0:1]
    ux = moments[:, 1:2] / density
    uy = moments[:, 2:3] / density
    uz = moments[:, 3:4] / density
    heat = (moments[:, 4:5] / density - (ux * ux + uy * uy + uz * uz)) / 3.0
    measure = (8.0 / NVX) * (8.0 / NVY) * (8.0 / NVZ)
    width = 2.0 * jnp.pi * heat
    scale = density * measure / (width * jnp.sqrt(width))
    inverse = -1.0 / (2.0 * heat)
    vx, vy = lane_speeds((CELLS, BLOCK), place_ref[0] * BLOCK)
    dx = vx - ux
    dy = vy - uy
    plane = scale * jnp.exp((dx * dx + dy * dy) * inverse)
    dz = speed(lax.broadcasted_iota(jnp.int32, (CELLS, 128), 1), NVZ) - uz
    depth = jnp.exp((dz * dz) * inverse)
    for w in range(NVZ):
        v, p = w // PLANES, w % PLANES
        f = got_ref[v, p * CELLS : (p + 1) * CELLS, :].astype(F32)
        deviation = (depth[:, w : w + 1] * plane - f).astype(BF16)
        for t in range(CELLS // TILE):
            dev_ref[w * TILE : (w + 1) * TILE, t * BLOCK : (t + 1) * BLOCK] = deviation[
                t * TILE : (t + 1) * TILE, :
            ]
    mixed = jnp.dot(mix_ref[...], dev_ref[...], preferred_element_type=F32).astype(BF16)
    for w in range(NVZ):
        v, p = w // PLANES, w % PLANES
        for t in range(CELLS // TILE):
            send_ref[v, p * CELLS + t * TILE : p * CELLS + (t + 1) * TILE, :] = mixed[
                w * TILE : (w + 1) * TILE, t * BLOCK : (t + 1) * BLOCK
            ]


def relax(place, got, mix):
    return pl.pallas_call(
        relax_kernel,
        out_shape=jax.ShapeDtypeStruct((GROUP, DATA, BLOCK), BF16),
        in_specs=[smem(), vmem(), vmem()],
        out_specs=vmem(),
        scratch_shapes=[pltpu.VMEM((NVZ * TILE, CELLS // TILE * BLOCK), BF16)],
        compiler_params=pltpu.CompilerParams(vmem_limit_bytes=LIMIT),
        name="relax",
    )(place, got, mix)


def advance_kernel(
    core_ref,
    f_hbm,
    back_hbm,
    weights_hbm,
    below_hbm,
    above_hbm,
    inner_hbm,
    outer_hbm,
    out_hbm,
    f_ref,
    back_ref,
    weights_ref,
    lower_ref,
    upper_ref,
    inner_ref,
    outer_ref,
    moved_ref,
    out_ref,
    sem,
    out_sem,
):
    edge = pl.ds(below_hbm.shape[0] - 2 * COLS, 2 * COLS)
    first = [
        pltpu.make_async_copy(below_hbm.at[edge], lower_ref, sem.at[0]),
        pltpu.make_async_copy(above_hbm.at[edge], upper_ref, sem.at[1]),
        pltpu.make_async_copy(inner_hbm, inner_ref, sem.at[2]),
        pltpu.make_async_copy(outer_hbm, outer_ref, sem.at[3]),
        pltpu.make_async_copy(f_hbm, f_ref, sem.at[4]),
    ]
    second = [
        pltpu.make_async_copy(back_hbm, back_ref, sem.at[5]),
        pltpu.make_async_copy(weights_hbm, weights_ref, sem.at[6]),
    ]
    for copy in first + second:
        copy.start()
    half = NXY // 2
    vx, vy = lane_speeds((COLS, NXY), 0)
    courant_across = COURANT / (4.0 - 4.0 / NVX)
    courant_along = COURANT / (4.0 - 4.0 / NVY)
    cx = courant_across * jnp.abs(vx)
    cy = courant_along * jnp.abs(vy)
    upwind = vy > 0.0
    col = lax.broadcasted_iota(jnp.int32, (COLS, NXY), 0)
    core = core_ref[0]
    for copy in first:
        copy.wait()
    inner = inner_ref[...].astype(F32)
    outer = outer_ref[...].astype(F32)
    left_edge = jnp.where(core == 0, outer, inner)
    right_edge = jnp.where(core == 0, inner, outer)
    for p in range(PLANES):
        lanes = slice(p * NXY, (p + 1) * NXY)
        first_half = slice(p * NXY, p * NXY + half)
        second_half = slice(p * NXY + half, (p + 1) * NXY)
        rows = slice(p // 2 * COLS, (p // 2 + 1) * COLS)
        packed = slice(p % 2 * half, (p % 2 + 1) * half)
        for r in range(ROWS):
            current = f_ref[r, :, lanes].astype(F32)
            above = upper_ref[rows, packed] if r == ROWS - 1 else f_ref[r + 1, :, first_half]
            below = lower_ref[rows, packed] if r == 0 else f_ref[r - 1, :, second_half]
            across = jnp.concatenate([above, below], axis=1).astype(F32)
            left = left_edge[r * PLANES + p : r * PLANES + p + 1, :]
            right = right_edge[r * PLANES + p : r * PLANES + p + 1, :]
            left = jnp.where(col == 0, left, pltpu.roll(current, 1, 0))
            right = jnp.where(col == COLS - 1, right, pltpu.roll(current, COLS - 1, 0))
            along = jnp.where(upwind, left, right)
            start = p * CELLS + r * COLS
            moved_ref[start : start + COLS, :] = current - (
                cx * (current - across) + cy * (current - along)
            )
    for copy in second:
        copy.wait()
    mixed = jnp.concatenate([back_ref[v] for v in range(GROUP)], axis=1)
    collision = jnp.dot(mixed, weights_ref[...], preferred_element_type=F32)
    stores = []
    for p in range(PLANES):
        for r in range(ROWS):
            start = p * CELLS + r * COLS
            value = moved_ref[start : start + COLS, :] + RELAX_RATE * collision[start : start + COLS, :]
            out_ref[r, :, p * NXY : (p + 1) * NXY] = value.astype(BF16)
        lanes = pl.ds(p * NXY, NXY)
        stores.append(
            pltpu.make_async_copy(
                out_ref.at[:, :, lanes], out_hbm.at[:, :, lanes], out_sem.at[p]
            )
        )
        stores[-1].start()
    for copy in stores:
        copy.wait()


def advance(core, f, back, weights, below, above, inner, outer):
    weights = pltpu.with_memory_space_constraint(weights, pltpu.HBM)
    return pl.pallas_call(
        advance_kernel,
        out_shape=jax.ShapeDtypeStruct(f.shape, BF16),
        in_specs=[smem()] + [hbm()] * 7,
        out_specs=hbm(),
        scratch_shapes=[
            pltpu.VMEM(f.shape, BF16),
            pltpu.VMEM(back.shape, BF16),
            pltpu.VMEM(weights.shape, BF16),
            pltpu.VMEM((2 * COLS, NXY), BF16),
            pltpu.VMEM((2 * COLS, NXY), BF16),
            pltpu.VMEM(inner.shape, BF16),
            pltpu.VMEM(outer.shape, BF16),
            pltpu.VMEM((DATA, NXY), F32),
            pltpu.VMEM(f.shape, BF16),
            pltpu.SemaphoreType.DMA((7,)),
            pltpu.SemaphoreType.DMA((PLANES,)),
        ],
        compiler_params=pltpu.CompilerParams(vmem_limit_bytes=LIMIT),
        name="advance",
    )(core, f, back, weights, below, above, inner, outer)


def ring(axis, step):
    count = lax.axis_size(axis)
    return [(i, (i + step) % count) for i in range(count)]


def local(distribution, plane_weights, depth_weights):
    place = lax.axis_index("vel").astype(jnp.int32).reshape(1)
    along = lax.axis_index("sy").astype(jnp.int32)
    core = jnp.bitwise_and(along, 1).reshape(1)
    where = jnp.stack([jnp.bitwise_and(along, 1), along >> 1, lax.axis_index("sx").astype(jnp.int32)])
    flip = lambda bit: [(i, i ^ bit) for i in range(8)]
    pair = jnp.concatenate([plane_weights, lax.ppermute(plane_weights, "sx", flip(4))])
    low, high, inner, outer = edges(core, distribution)
    mix = spread(depth_weights)
    spot, pair = lax.optimization_barrier((place, pair))
    held = jnp.concatenate(
        [pair] + [lax.ppermute(pair, "sy", flip(2 * step)) for step in (1, 2, 3)]
    )
    send, held = lax.optimization_barrier((pack(spot, distribution), held))
    got = lax.all_to_all(send, "vel", 0, 0, tiled=True)
    above = lax.ppermute(jnp.concatenate([held, low]), "sx", ring("sx", -1))
    below = lax.ppermute(jnp.concatenate([held, high]), "sx", ring("sx", 1))
    across = lax.ppermute(held, "sx", [(i, (i + 2) % 8 if i % 2 == 0 else (i - 2) % 8) for i in range(8)])
    outer = lax.ppermute(outer, "sy", [(i, (i + 1) % 8 if i % 2 else (i - 1) % 8) for i in range(8)])
    own = join(held, above, below, across, inner)
    other = lax.ppermute(own, "sy", flip(1))
    weights, inner = assemble(where, own, other)
    back = lax.all_to_all(relax(place, got, mix), "vel", 0, 0, tiled=True)
    return advance(
        core, distribution, back, weights, below, above, inner, outer
    )


def solution(mesh):
    return jax.shard_map(
        local,
        mesh=mesh,
        in_specs=(P("sx", "sy", "vel"), P(("sx", "sy"), None), P()),
        out_specs=P("sx", "sy", "vel"),
        check_vma=False,
    )
```

```python
import jax
import jax.numpy as jnp
import numpy as np
from jax import lax
from jax.experimental import pallas as pl
from jax.experimental.pallas import tpu as pltpu
from jax.sharding import PartitionSpec as P

NVZ = 32
NVX = 32
NVY = 32
NXY = NVX * NVY
COURANT = 0.45
RELAX_RATE = 0.3
ROWS = 3
COLS = 32
CELLS = ROWS * COLS
PLANES = 4
GROUP = 8
BLOCK = NXY // GROUP
DATA = PLANES * CELLS
CHUNK = DATA + 16
TILE = 16
LIMIT = 16 << 20
F32 = jnp.float32
BF16 = jnp.bfloat16


def speed(index, count):
    return (index.astype(F32) - (count - 1) / 2.0) * (8.0 / count)


def lane_speeds(shape, offset):
    lane = lax.broadcasted_iota(jnp.int32, shape, len(shape) - 1) + offset
    return speed(lane // NVY, NVX), speed(lane % NVY, NVY)


def vmem():
    return pl.BlockSpec(memory_space=pltpu.VMEM)


def hbm():
    return pl.BlockSpec(memory_space=pltpu.HBM)


def smem():
    return pl.BlockSpec(memory_space=pltpu.SMEM)


def moment_basis():
    lane = np.arange(NXY)
    vx = (lane // NVY - (NVX - 1) / 2.0) * (8.0 / NVX)
    vy = (lane % NVY - (NVY - 1) / 2.0) * (8.0 / NVY)
    squared = (vx * vx + vy * vy).astype(np.float32)
    rough = squared.astype(BF16).astype(np.float32)
    basis = np.zeros((NXY, 128), np.float32)
    for part in range(3):
        basis[:, part * 5] = 1.0
        basis[:, part * 5 + 1] = vx
        basis[:, part * 5 + 2] = vy
        basis[:, part * 5 + 3] = 1.0
        basis[:, part * 5 + 4] = rough
        basis[:, 16 + part * 5 + 4] = squared - rough
        basis[:, 32 + part * 5 + 4] = 1.0
    return basis.astype(BF16)


def pack_kernel(place_ref, f_ref, basis_ref, send_ref, x_ref, base_ref, out_ref, in_sem, base_sem, out_sem):
    def load(p):
        lanes = pl.ds(p * NXY, NXY)
        return pltpu.make_async_copy(f_ref.at[:, :, lanes], x_ref.at[p], in_sem.at[p])

    def store(p):
        rows = pl.ds(p * CELLS, CELLS)
        return pltpu.make_async_copy(out_ref.at[:, rows, :], send_ref.at[:, rows, :], out_sem.at[p])

    base = pltpu.make_async_copy(basis_ref, base_ref, base_sem)
    load(0).start()
    base.start()
    for p in range(1, PLANES):
        load(p).start()
    lane = lax.broadcasted_iota(jnp.int32, (1, 128), 1)
    first_plane = place_ref[0] * PLANES
    total = jnp.zeros((CELLS, 128), F32)
    for p in range(PLANES):
        load(p).wait()
        x = x_ref[p].reshape(CELLS, NXY)
        for v in range(GROUP):
            out_ref[v, p * CELLS : (p + 1) * CELLS, :] = x[:, v * BLOCK : (v + 1) * BLOCK]
        store(p).start()
        if p == 0:
            base.wait()
        sums = jnp.dot(x, base_ref[...], preferred_element_type=F32)
        vz = speed(first_plane + p, NVZ)
        factor = jnp.where(lane >= 32, vz * vz, jnp.where((lane < 16) & (lane % 5 == 3), vz, 1.0))
        total = total + sums * factor
    total = jnp.transpose(total)
    total = (total[0:16, :] + total[16:32, :]) + total[32:48, :]
    column = lax.broadcasted_iota(jnp.int32, (16, CELLS), 0)
    high = total.astype(BF16).astype(F32)
    middle = (total - high).astype(BF16).astype(F32)
    low = (total - high) - middle
    parts = jnp.where(
        column < 5, high, jnp.where(column < 10, middle, jnp.where(column < 15, low, 0.0))
    )
    parts = jnp.concatenate([parts, jnp.zeros((16, 128 - CELLS), F32)], axis=1).astype(BF16)
    for v in range(GROUP):
        out_ref[v, DATA:CHUNK, :] = parts
    tail = pl.ds(DATA, CHUNK - DATA)
    last = pltpu.make_async_copy(
        out_ref.at[:, tail, :], send_ref.at[:, tail, :], out_sem.at[PLANES]
    )
    last.start()
    for p in range(PLANES):
        store(p).wait()
    last.wait()


def pack(place, f):
    basis = jnp.asarray(moment_basis())
    f, basis = (pltpu.with_memory_space_constraint(x, pltpu.HBM) for x in (f, basis))
    return pl.pallas_call(
        pack_kernel,
        out_shape=jax.ShapeDtypeStruct((GROUP, CHUNK, BLOCK), BF16),
        in_specs=[smem(), hbm(), hbm()],
        out_specs=hbm(),
        scratch_shapes=[
            pltpu.VMEM((PLANES, ROWS, COLS, NXY), BF16),
            pltpu.VMEM((NXY, 128), BF16),
            pltpu.VMEM((GROUP, CHUNK, BLOCK), BF16),
            pltpu.SemaphoreType.DMA((PLANES,)),
            pltpu.SemaphoreType.DMA(()),
            pltpu.SemaphoreType.DMA((PLANES + 1,)),
        ],
        compiler_params=pltpu.CompilerParams(vmem_limit_bytes=LIMIT),
        name="pack",
    )(place, f, basis)


def edges_kernel(core_ref, f_ref, low_ref, high_ref, inner_ref, outer_ref):
    half = NXY // 2
    for p in range(PLANES):
        rows = slice(p // 2 * COLS, (p // 2 + 1) * COLS)
        lanes = slice(p % 2 * half, (p % 2 + 1) * half)
        high_ref[rows, lanes] = f_ref[ROWS - 1, :, p * NXY + half : (p + 1) * NXY]
        low_ref[rows, lanes] = f_ref[0, :, p * NXY : p * NXY + half]
    edge_row = lax.broadcasted_iota(jnp.int32, (16, NXY), 0)
    first = jnp.zeros((16, NXY), F32)
    last = jnp.zeros((16, NXY), F32)
    for r in range(ROWS):
        for p in range(PLANES):
            lanes = slice(p * NXY, (p + 1) * NXY)
            a = f_ref[r, 0:8, lanes].astype(F32)[0:1, :]
            b = f_ref[r, COLS - 8 : COLS, lanes].astype(F32)[7:8, :]
            first = jnp.where(edge_row == r * PLANES + p, a, first)
            last = jnp.where(edge_row == r * PLANES + p, b, last)
    core = core_ref[0]
    inner_ref[...] = jnp.where(core == 0, last, first).astype(BF16)
    outer_ref[...] = jnp.where(core == 0, first, last).astype(BF16)


def edges(core, f):
    row = jax.ShapeDtypeStruct((2 * COLS, NXY), BF16)
    column = jax.ShapeDtypeStruct((16, NXY), BF16)
    return pl.pallas_call(
        edges_kernel,
        out_shape=(row, row, column, column),
        in_specs=[smem(), vmem()],
        out_specs=(vmem(),) * 4,
        compiler_params=pltpu.CompilerParams(vmem_limit_bytes=LIMIT),
        name="edges",
    )(core, f)


def spread_kernel(depth_ref, out_ref):
    size = NVZ * TILE
    row = lax.broadcasted_iota(jnp.int32, (size, NVZ), 0)
    col = lax.broadcasted_iota(jnp.int32, (size, NVZ), 1)
    pick = jnp.where(row // TILE == col, 1.0, 0.0).astype(BF16)
    left = jnp.dot(pick, depth_ref[...], preferred_element_type=F32).astype(BF16)
    full = lax.dot_general(left, pick, (((1,), (1,)), ((), ())), preferred_element_type=F32)
    i = lax.broadcasted_iota(jnp.int32, (size, size), 0)
    j = lax.broadcasted_iota(jnp.int32, (size, size), 1)
    out_ref[...] = jnp.where(i % TILE == j % TILE, full, 0.0).astype(BF16)


def spread(depth_weights):
    size = NVZ * TILE
    return pl.pallas_call(
        spread_kernel,
        out_shape=jax.ShapeDtypeStruct((size, size), BF16),
        in_specs=[vmem()],
        out_specs=vmem(),
        compiler_params=pltpu.CompilerParams(vmem_limit_bytes=LIMIT),
        name="spread",
    )(depth_weights)


def relax_kernel(place_ref, got_ref, mix_ref, send_ref, dev_ref):
    pieces = jnp.concatenate([got_ref[v, DATA:CHUNK, :] for v in range(GROUP)], axis=0)
    i = lax.broadcasted_iota(jnp.int32, (GROUP * 16, 128), 0) % 16
    j = lax.broadcasted_iota(jnp.int32, (GROUP * 16, 128), 1)
    pick = jnp.where((i % 5 == j) & (i < 15), 1.0, 0.0).astype(BF16)
    moments = lax.dot_general(pieces, pick, (((0,), (0,)), ((), ())), preferred_element_type=F32)
    moments = moments[:CELLS, :]
    density = moments[:, 0:1]
    ux = moments[:, 1:2] / density
    uy = moments[:, 2:3] / density
    uz = moments[:, 3:4] / density
    heat = (moments[:, 4:5] / density - (ux * ux + uy * uy + uz * uz)) / 3.0
    measure = (8.0 / NVX) * (8.0 / NVY) * (8.0 / NVZ)
    width = 2.0 * jnp.pi * heat
    scale = density * measure / (width * jnp.sqrt(width))
    inverse = -1.0 / (2.0 * heat)
    vx, vy = lane_speeds((CELLS, BLOCK), place_ref[0] * BLOCK)
    dx = vx - ux
    dy = vy - uy
    plane = scale * jnp.exp((dx * dx + dy * dy) * inverse)
    dz = speed(lax.broadcasted_iota(jnp.int32, (CELLS, 128), 1), NVZ) - uz
    depth = jnp.exp((dz * dz) * inverse)
    for w in range(NVZ):
        v, p = w // PLANES, w % PLANES
        f = got_ref[v, p * CELLS : (p + 1) * CELLS, :].astype(F32)
        deviation = (depth[:, w : w + 1] * plane - f).astype(BF16)
        for t in range(CELLS // TILE):
            dev_ref[w * TILE : (w + 1) * TILE, t * BLOCK : (t + 1) * BLOCK] = deviation[
                t * TILE : (t + 1) * TILE, :
            ]
    mixed = jnp.dot(mix_ref[...], dev_ref[...], preferred_element_type=F32).astype(BF16)
    for w in range(NVZ):
        v, p = w // PLANES, w % PLANES
        for t in range(CELLS // TILE):
            send_ref[v, p * CELLS + t * TILE : p * CELLS + (t + 1) * TILE, :] = mixed[
                w * TILE : (w + 1) * TILE, t * BLOCK : (t + 1) * BLOCK
            ]


def relax(place, got, mix):
    return pl.pallas_call(
        relax_kernel,
        out_shape=jax.ShapeDtypeStruct((GROUP, DATA, BLOCK), BF16),
        in_specs=[smem(), vmem(), vmem()],
        out_specs=vmem(),
        scratch_shapes=[pltpu.VMEM((NVZ * TILE, CELLS // TILE * BLOCK), BF16)],
        compiler_params=pltpu.CompilerParams(vmem_limit_bytes=LIMIT),
        name="relax",
    )(place, got, mix)


def advance_kernel(
    core_ref,
    f_hbm,
    back_hbm,
    weights_hbm,
    below_hbm,
    above_hbm,
    inner_hbm,
    outer_hbm,
    out_hbm,
    f_ref,
    back_ref,
    weights_ref,
    lower_ref,
    upper_ref,
    inner_ref,
    outer_ref,
    moved_ref,
    out_ref,
    sem,
    out_sem,
):
    first = [
        pltpu.make_async_copy(below_hbm, lower_ref, sem.at[0]),
        pltpu.make_async_copy(above_hbm, upper_ref, sem.at[1]),
        pltpu.make_async_copy(inner_hbm, inner_ref, sem.at[2]),
        pltpu.make_async_copy(outer_hbm, outer_ref, sem.at[3]),
        pltpu.make_async_copy(f_hbm, f_ref, sem.at[4]),
    ]
    second = [
        pltpu.make_async_copy(back_hbm, back_ref, sem.at[5]),
        pltpu.make_async_copy(weights_hbm, weights_ref, sem.at[6]),
    ]
    for copy in first + second:
        copy.start()
    half = NXY // 2
    vx, vy = lane_speeds((COLS, NXY), 0)
    courant_across = COURANT / (4.0 - 4.0 / NVX)
    courant_along = COURANT / (4.0 - 4.0 / NVY)
    cx = courant_across * jnp.abs(vx)
    cy = courant_along * jnp.abs(vy)
    upwind = vy > 0.0
    col = lax.broadcasted_iota(jnp.int32, (COLS, NXY), 0)
    core = core_ref[0]
    for copy in first:
        copy.wait()
    inner = inner_ref[...].astype(F32)
    outer = outer_ref[...].astype(F32)
    left_edge = jnp.where(core == 0, outer, inner)
    right_edge = jnp.where(core == 0, inner, outer)
    for p in range(PLANES):
        lanes = slice(p * NXY, (p + 1) * NXY)
        first_half = slice(p * NXY, p * NXY + half)
        second_half = slice(p * NXY + half, (p + 1) * NXY)
        rows = slice(p // 2 * COLS, (p // 2 + 1) * COLS)
        packed = slice(p % 2 * half, (p % 2 + 1) * half)
        for r in range(ROWS):
            current = f_ref[r, :, lanes].astype(F32)
            above = upper_ref[rows, packed] if r == ROWS - 1 else f_ref[r + 1, :, first_half]
            below = lower_ref[rows, packed] if r == 0 else f_ref[r - 1, :, second_half]
            across = jnp.concatenate([above, below], axis=1).astype(F32)
            left = left_edge[r * PLANES + p : r * PLANES + p + 1, :]
            right = right_edge[r * PLANES + p : r * PLANES + p + 1, :]
            left = jnp.where(col == 0, left, pltpu.roll(current, 1, 0))
            right = jnp.where(col == COLS - 1, right, pltpu.roll(current, COLS - 1, 0))
            along = jnp.where(upwind, left, right)
            start = p * CELLS + r * COLS
            moved_ref[start : start + COLS, :] = current - (
                cx * (current - across) + cy * (current - along)
            )
    for copy in second:
        copy.wait()
    mixed = jnp.concatenate([back_ref[v] for v in range(GROUP)], axis=1)
    collision = lax.dot_general(
        mixed, weights_ref[...], (((1,), (1,)), ((), ())), preferred_element_type=F32
    )
    stores = []
    for p in range(PLANES):
        for r in range(ROWS):
            start = p * CELLS + r * COLS
            value = moved_ref[start : start + COLS, :] + RELAX_RATE * collision[start : start + COLS, :]
            out_ref[r, :, p * NXY : (p + 1) * NXY] = value.astype(BF16)
        lanes = pl.ds(p * NXY, NXY)
        stores.append(
            pltpu.make_async_copy(
                out_ref.at[:, :, lanes], out_hbm.at[:, :, lanes], out_sem.at[p]
            )
        )
        stores[-1].start()
    for copy in stores:
        copy.wait()


def advance(core, f, back, weights, below, above, inner, outer):
    weights = pltpu.with_memory_space_constraint(weights, pltpu.HBM)
    return pl.pallas_call(
        advance_kernel,
        out_shape=jax.ShapeDtypeStruct(f.shape, BF16),
        in_specs=[smem()] + [hbm()] * 7,
        out_specs=hbm(),
        scratch_shapes=[
            pltpu.VMEM(f.shape, BF16),
            pltpu.VMEM(back.shape, BF16),
            pltpu.VMEM(weights.shape, BF16),
            pltpu.VMEM((2 * COLS, NXY), BF16),
            pltpu.VMEM((2 * COLS, NXY), BF16),
            pltpu.VMEM(inner.shape, BF16),
            pltpu.VMEM(outer.shape, BF16),
            pltpu.VMEM((DATA, NXY), F32),
            pltpu.VMEM(f.shape, BF16),
            pltpu.SemaphoreType.DMA((7,)),
            pltpu.SemaphoreType.DMA((PLANES,)),
        ],
        compiler_params=pltpu.CompilerParams(vmem_limit_bytes=LIMIT),
        name="advance",
    )(core, f, back, weights, below, above, inner, outer)


def ring(axis, step):
    count = lax.axis_size(axis)
    return [(i, (i + step) % count) for i in range(count)]


def local(distribution, plane_weights, depth_weights):
    place = lax.axis_index("vel").astype(jnp.int32).reshape(1)
    core = jnp.bitwise_and(lax.axis_index("sy").astype(jnp.int32), 1).reshape(1)
    shard, width = plane_weights.shape
    count = lax.axis_size("sy")
    rows = jnp.broadcast_to(plane_weights[None], (count, shard, width))
    rows = lax.all_to_all(rows, "sy", 0, 0, tiled=True).reshape(count * shard, width)
    send, rows = lax.optimization_barrier((pack(place, distribution), rows))
    weights = lax.all_gather(rows, "sx", axis=0, tiled=True)
    got = lax.all_to_all(send, "vel", 0, 0, tiled=True)
    low, high, inner, outer = edges(core, distribution)
    mix = spread(depth_weights)
    above = lax.ppermute(low, "sx", ring("sx", -1))
    below = lax.ppermute(high, "sx", ring("sx", 1))
    inner = lax.ppermute(inner, "sy", [(i, i ^ 1) for i in range(count)])
    outer = lax.ppermute(
        outer, "sy", [(i, (i + 1) % count if i % 2 else (i - 1) % count) for i in range(count)]
    )
    back = lax.all_to_all(relax(place, got, mix), "vel", 0, 0, tiled=True)
    return advance(core, distribution, back, weights, below, above, inner, outer)


def solution(mesh):
    return jax.shard_map(
        local,
        mesh=mesh,
        in_specs=(P("sx", "sy", "vel"), P(("sx", "sy"), None), P()),
        out_specs=P("sx", "sy", "vel"),
        check_vma=False,
    )
```

```python
import jax
import jax.numpy as jnp
import numpy as np
from jax import lax
from jax.experimental import pallas as pl
from jax.experimental.pallas import tpu as pltpu
from jax.sharding import PartitionSpec as P

NVZ = 32
NVX = 32
NVY = 32
NXY = NVX * NVY
COURANT = 0.45
RELAX_RATE = 0.3
ROWS = 3
COLS = 32
CELLS = ROWS * COLS
PLANES = 4
GROUP = 8
BLOCK = NXY // GROUP
DATA = PLANES * CELLS
CHUNK = DATA + 16
TILE = 16
LIMIT = 16 << 20
F32 = jnp.float32
BF16 = jnp.bfloat16


def speed(index, count):
    return (index.astype(F32) - (count - 1) / 2.0) * (8.0 / count)


def lane_speeds(shape, offset):
    lane = lax.broadcasted_iota(jnp.int32, shape, len(shape) - 1) + offset
    return speed(lane // NVY, NVX), speed(lane % NVY, NVY)


def vmem():
    return pl.BlockSpec(memory_space=pltpu.VMEM)


def hbm():
    return pl.BlockSpec(memory_space=pltpu.HBM)


def smem():
    return pl.BlockSpec(memory_space=pltpu.SMEM)


def moment_basis():
    lane = np.arange(NXY)
    vx = (lane // NVY - (NVX - 1) / 2.0) * (8.0 / NVX)
    vy = (lane % NVY - (NVY - 1) / 2.0) * (8.0 / NVY)
    squared = (vx * vx + vy * vy).astype(np.float32)
    rough = squared.astype(BF16).astype(np.float32)
    basis = np.zeros((NXY, 128), np.float32)
    for part in range(3):
        basis[:, part * 5] = 1.0
        basis[:, part * 5 + 1] = vx
        basis[:, part * 5 + 2] = vy
        basis[:, part * 5 + 3] = 1.0
        basis[:, part * 5 + 4] = rough
        basis[:, 16 + part * 5 + 4] = squared - rough
        basis[:, 32 + part * 5 + 4] = 1.0
    return basis.astype(BF16)


def pack_kernel(place_ref, f_ref, basis_ref, send_ref, x_ref, base_ref, out_ref, in_sem, base_sem, out_sem):
    def load(p):
        lanes = pl.ds(p * NXY, NXY)
        return pltpu.make_async_copy(f_ref.at[:, :, lanes], x_ref.at[p], in_sem.at[p])

    def store(p):
        rows = pl.ds(p * CELLS, CELLS)
        return pltpu.make_async_copy(out_ref.at[:, rows, :], send_ref.at[:, rows, :], out_sem.at[p])

    base = pltpu.make_async_copy(basis_ref, base_ref, base_sem)
    load(0).start()
    base.start()
    for p in range(1, PLANES):
        load(p).start()
    lane = lax.broadcasted_iota(jnp.int32, (1, 128), 1)
    first_plane = place_ref[0] * PLANES
    total = jnp.zeros((CELLS, 128), F32)
    for p in range(PLANES):
        load(p).wait()
        x = x_ref[p].reshape(CELLS, NXY)
        for v in range(GROUP):
            out_ref[v, p * CELLS : (p + 1) * CELLS, :] = x[:, v * BLOCK : (v + 1) * BLOCK]
        store(p).start()
        if p == 0:
            base.wait()
        sums = jnp.dot(x, base_ref[...], preferred_element_type=F32)
        vz = speed(first_plane + p, NVZ)
        factor = jnp.where(lane >= 32, vz * vz, jnp.where((lane < 16) & (lane % 5 == 3), vz, 1.0))
        total = total + sums * factor
    total = jnp.transpose(total)
    total = (total[0:16, :] + total[16:32, :]) + total[32:48, :]
    column = lax.broadcasted_iota(jnp.int32, (16, CELLS), 0)
    high = total.astype(BF16).astype(F32)
    middle = (total - high).astype(BF16).astype(F32)
    low = (total - high) - middle
    parts = jnp.where(
        column < 5, high, jnp.where(column < 10, middle, jnp.where(column < 15, low, 0.0))
    )
    parts = jnp.concatenate([parts, jnp.zeros((16, 128 - CELLS), F32)], axis=1).astype(BF16)
    for v in range(GROUP):
        out_ref[v, DATA:CHUNK, :] = parts
    tail = pl.ds(DATA, CHUNK - DATA)
    last = pltpu.make_async_copy(
        out_ref.at[:, tail, :], send_ref.at[:, tail, :], out_sem.at[PLANES]
    )
    last.start()
    for p in range(PLANES):
        store(p).wait()
    last.wait()


def pack(place, f):
    basis = jnp.asarray(moment_basis())
    f, basis = (pltpu.with_memory_space_constraint(x, pltpu.HBM) for x in (f, basis))
    return pl.pallas_call(
        pack_kernel,
        out_shape=jax.ShapeDtypeStruct((GROUP, CHUNK, BLOCK), BF16),
        in_specs=[smem(), hbm(), hbm()],
        out_specs=hbm(),
        scratch_shapes=[
            pltpu.VMEM((PLANES, ROWS, COLS, NXY), BF16),
            pltpu.VMEM((NXY, 128), BF16),
            pltpu.VMEM((GROUP, CHUNK, BLOCK), BF16),
            pltpu.SemaphoreType.DMA((PLANES,)),
            pltpu.SemaphoreType.DMA(()),
            pltpu.SemaphoreType.DMA((PLANES + 1,)),
        ],
        compiler_params=pltpu.CompilerParams(vmem_limit_bytes=LIMIT),
        name="pack",
    )(place, f, basis)


def columns_kernel(core_ref, f_hbm, shard_hbm, pack_ref, inner_ref, first_ref, last_ref, sem):
    shard = shard_hbm.shape[0]
    copies = [
        pltpu.make_async_copy(f_hbm.at[:, pl.ds(0, 8), :], first_ref, sem.at[0]),
        pltpu.make_async_copy(f_hbm.at[:, pl.ds(COLS - 8, 8), :], last_ref, sem.at[1]),
        pltpu.make_async_copy(shard_hbm, pack_ref.at[pl.ds(0, shard)], sem.at[2]),
    ]
    for copy in copies:
        copy.start()
    edge_row = lax.broadcasted_iota(jnp.int32, (16, NXY), 0)
    first = jnp.zeros((16, NXY), F32)
    last = jnp.zeros((16, NXY), F32)
    for copy in copies:
        copy.wait()
    for r in range(ROWS):
        for p in range(PLANES):
            lanes = slice(p * NXY, (p + 1) * NXY)
            a = first_ref[r, :, lanes].astype(F32)[0:1, :]
            b = last_ref[r, :, lanes].astype(F32)[7:8, :]
            first = jnp.where(edge_row == r * PLANES + p, a, first)
            last = jnp.where(edge_row == r * PLANES + p, b, last)
    core = core_ref[0]
    inner_ref[...] = jnp.where(core == 0, last, first).astype(BF16)
    pack_ref[shard : shard + 16, :] = jnp.where(core == 0, first, last).astype(BF16)


def columns(core, f, shard):
    f, shard = (pltpu.with_memory_space_constraint(x, pltpu.HBM) for x in (f, shard))
    return pl.pallas_call(
        columns_kernel,
        out_shape=(
            jax.ShapeDtypeStruct((shard.shape[0] + 16, NXY), BF16),
            jax.ShapeDtypeStruct((16, NXY), BF16),
        ),
        in_specs=[smem(), hbm(), hbm()],
        out_specs=(vmem(), vmem()),
        scratch_shapes=[
            pltpu.VMEM((ROWS, 8, PLANES * NXY), BF16),
            pltpu.VMEM((ROWS, 8, PLANES * NXY), BF16),
            pltpu.SemaphoreType.DMA((3,)),
        ],
        compiler_params=pltpu.CompilerParams(vmem_limit_bytes=LIMIT),
        name="columns",
    )(core, f, shard)


def edges_kernel(held_ref, f_ref, low_ref, high_ref):
    half = NXY // 2
    size = held_ref.shape[0]
    low_ref[0:size, :] = held_ref[...]
    high_ref[0:size, :] = held_ref[...]
    for p in range(PLANES):
        rows = slice(size + p // 2 * COLS, size + (p // 2 + 1) * COLS)
        lanes = slice(p % 2 * half, (p % 2 + 1) * half)
        high_ref[rows, lanes] = f_ref[ROWS - 1, :, p * NXY + half : (p + 1) * NXY]
        low_ref[rows, lanes] = f_ref[0, :, p * NXY : p * NXY + half]


def edges(held, f):
    row = jax.ShapeDtypeStruct((held.shape[0] + 2 * COLS, NXY), BF16)
    return pl.pallas_call(
        edges_kernel,
        out_shape=(row, row),
        in_specs=[vmem(), vmem()],
        out_specs=(vmem(), vmem()),
        compiler_params=pltpu.CompilerParams(vmem_limit_bytes=LIMIT),
        name="edges",
    )(held, f)


def join_kernel(held_ref, above_ref, below_ref, across_ref, inner_ref, out_ref, sem):
    size = held_ref.shape[0]
    copies = []
    for m, ref in enumerate((held_ref, above_ref, below_ref, across_ref)):
        copies.append(
            pltpu.make_async_copy(
                ref.at[pl.ds(0, size)], out_ref.at[pl.ds(m * size, size)], sem.at[m]
            )
        )
    copies.append(
        pltpu.make_async_copy(inner_ref, out_ref.at[pl.ds(4 * size, 16)], sem.at[4])
    )
    for copy in copies:
        copy.start()
    for copy in copies:
        copy.wait()


def join(held, above, below, across, inner):
    return pl.pallas_call(
        join_kernel,
        out_shape=jax.ShapeDtypeStruct((4 * held.shape[0] + 16, NXY), BF16),
        in_specs=[hbm()] * 5,
        out_specs=hbm(),
        scratch_shapes=[pltpu.SemaphoreType.DMA((5,))],
        compiler_params=pltpu.CompilerParams(vmem_limit_bytes=LIMIT),
        name="join",
    )(held, above, below, across, inner)


def assemble_kernel(where_ref, own_ref, other_ref, out_hbm, inner_hbm, rows_ref, turned_ref, sem):
    half = NXY // 2
    edge = pltpu.make_async_copy(other_ref.at[pl.ds(half, 16)], inner_hbm, sem.at[1])
    edge.start()
    mine, y = where_ref[0], where_ref[1]
    far = jnp.where(y % 2 == 0, y + 6, y + 2)
    for side, ref in ((mine, own_ref), (jnp.bitwise_xor(mine, 1), other_ref)):
        turn = jnp.bitwise_xor(side, 4)
        step = jnp.where(side % 2 == 1, 1, 7)
        places = (side, (side + step) % 8, turn, (turn + step) % 8)
        for m, base in enumerate((y, y + 1, y + 7, far)):
            for i in range(2):
                for j in range(4):
                    block = slice((m * 8 + i * 4 + j) * 16, (m * 8 + i * 4 + j + 1) * 16)
                    rows_ref[(base + 4 * i) % 8 * 8 + places[j]] = ref[block, :]
    turned_ref[...] = jnp.transpose(rows_ref[...].reshape(NXY, NXY))
    copy = pltpu.make_async_copy(turned_ref, out_hbm, sem.at[0])
    copy.start()
    edge.wait()
    copy.wait()


def assemble(where, own, other):
    return pl.pallas_call(
        assemble_kernel,
        out_shape=(pltpu.HBM((NXY, NXY), BF16), jax.ShapeDtypeStruct((16, NXY), BF16)),
        in_specs=[smem(), vmem(), vmem()],
        out_specs=(hbm(), hbm()),
        scratch_shapes=[
            pltpu.VMEM((NXY // 16, 16, NXY), BF16),
            pltpu.VMEM((NXY, NXY), BF16),
            pltpu.SemaphoreType.DMA((2,)),
        ],
        compiler_params=pltpu.CompilerParams(vmem_limit_bytes=LIMIT),
        name="assemble",
    )(where, own, other)


def spread_kernel(depth_ref, out_ref):
    size = NVZ * TILE
    row = lax.broadcasted_iota(jnp.int32, (size, NVZ), 0)
    col = lax.broadcasted_iota(jnp.int32, (size, NVZ), 1)
    pick = jnp.where(row // TILE == col, 1.0, 0.0).astype(BF16)
    left = jnp.dot(pick, depth_ref[...], preferred_element_type=F32).astype(BF16)
    full = lax.dot_general(left, pick, (((1,), (1,)), ((), ())), preferred_element_type=F32)
    i = lax.broadcasted_iota(jnp.int32, (size, size), 0)
    j = lax.broadcasted_iota(jnp.int32, (size, size), 1)
    out_ref[...] = jnp.where(i % TILE == j % TILE, full, 0.0).astype(BF16)


def spread(depth_weights):
    size = NVZ * TILE
    return pl.pallas_call(
        spread_kernel,
        out_shape=jax.ShapeDtypeStruct((size, size), BF16),
        in_specs=[vmem()],
        out_specs=vmem(),
        compiler_params=pltpu.CompilerParams(vmem_limit_bytes=LIMIT),
        name="spread",
    )(depth_weights)


def relax_kernel(place_ref, got_ref, mix_ref, send_ref, dev_ref):
    pieces = jnp.concatenate([got_ref[v, DATA:CHUNK, :] for v in range(GROUP)], axis=0)
    i = lax.broadcasted_iota(jnp.int32, (GROUP * 16, 128), 0) % 16
    j = lax.broadcasted_iota(jnp.int32, (GROUP * 16, 128), 1)
    pick = jnp.where((i % 5 == j) & (i < 15), 1.0, 0.0).astype(BF16)
    moments = lax.dot_general(pieces, pick, (((0,), (0,)), ((), ())), preferred_element_type=F32)
    moments = moments[:CELLS, :]
    density = moments[:, 0:1]
    ux = moments[:, 1:2] / density
    uy = moments[:, 2:3] / density
    uz = moments[:, 3:4] / density
    heat = (moments[:, 4:5] / density - (ux * ux + uy * uy + uz * uz)) / 3.0
    measure = (8.0 / NVX) * (8.0 / NVY) * (8.0 / NVZ)
    width = 2.0 * jnp.pi * heat
    scale = density * measure / (width * jnp.sqrt(width))
    inverse = -1.0 / (2.0 * heat)
    vx, vy = lane_speeds((CELLS, BLOCK), place_ref[0] * BLOCK)
    dx = vx - ux
    dy = vy - uy
    plane = scale * jnp.exp((dx * dx + dy * dy) * inverse)
    dz = speed(lax.broadcasted_iota(jnp.int32, (CELLS, 128), 1), NVZ) - uz
    depth = jnp.exp((dz * dz) * inverse)
    for w in range(NVZ):
        v, p = w // PLANES, w % PLANES
        f = got_ref[v, p * CELLS : (p + 1) * CELLS, :].astype(F32)
        deviation = (depth[:, w : w + 1] * plane - f).astype(BF16)
        for t in range(CELLS // TILE):
            dev_ref[w * TILE : (w + 1) * TILE, t * BLOCK : (t + 1) * BLOCK] = deviation[
                t * TILE : (t + 1) * TILE, :
            ]
    mixed = jnp.dot(mix_ref[...], dev_ref[...], preferred_element_type=F32).astype(BF16)
    for w in range(NVZ):
        v, p = w // PLANES, w % PLANES
        for t in range(CELLS // TILE):
            send_ref[v, p * CELLS + t * TILE : p * CELLS + (t + 1) * TILE, :] = mixed[
                w * TILE : (w + 1) * TILE, t * BLOCK : (t + 1) * BLOCK
            ]


def relax(place, got, mix):
    return pl.pallas_call(
        relax_kernel,
        out_shape=jax.ShapeDtypeStruct((GROUP, DATA, BLOCK), BF16),
        in_specs=[smem(), vmem(), vmem()],
        out_specs=vmem(),
        scratch_shapes=[pltpu.VMEM((NVZ * TILE, CELLS // TILE * BLOCK), BF16)],
        compiler_params=pltpu.CompilerParams(vmem_limit_bytes=LIMIT),
        name="relax",
    )(place, got, mix)


def advance_kernel(
    core_ref,
    f_hbm,
    back_hbm,
    weights_hbm,
    below_hbm,
    above_hbm,
    inner_hbm,
    outer_hbm,
    out_hbm,
    f_ref,
    back_ref,
    weights_ref,
    lower_ref,
    upper_ref,
    inner_ref,
    outer_ref,
    moved_ref,
    out_ref,
    sem,
    out_sem,
):
    edge = pl.ds(below_hbm.shape[0] - 2 * COLS, 2 * COLS)
    first = [
        pltpu.make_async_copy(below_hbm.at[edge], lower_ref, sem.at[0]),
        pltpu.make_async_copy(above_hbm.at[edge], upper_ref, sem.at[1]),
        pltpu.make_async_copy(inner_hbm, inner_ref, sem.at[2]),
        pltpu.make_async_copy(outer_hbm.at[pl.ds(outer_hbm.shape[0] - 16, 16)], outer_ref, sem.at[3]),
        pltpu.make_async_copy(f_hbm, f_ref, sem.at[4]),
    ]
    second = [
        pltpu.make_async_copy(back_hbm, back_ref, sem.at[5]),
        pltpu.make_async_copy(weights_hbm, weights_ref, sem.at[6]),
    ]
    for copy in first + second:
        copy.start()
    half = NXY // 2
    vx, vy = lane_speeds((COLS, NXY), 0)
    courant_across = COURANT / (4.0 - 4.0 / NVX)
    courant_along = COURANT / (4.0 - 4.0 / NVY)
    cx = courant_across * jnp.abs(vx)
    cy = courant_along * jnp.abs(vy)
    upwind = vy > 0.0
    col = lax.broadcasted_iota(jnp.int32, (COLS, NXY), 0)
    core = core_ref[0]
    for copy in first:
        copy.wait()
    inner = inner_ref[...].astype(F32)
    outer = outer_ref[...].astype(F32)
    left_edge = jnp.where(core == 0, outer, inner)
    right_edge = jnp.where(core == 0, inner, outer)
    for p in range(PLANES):
        lanes = slice(p * NXY, (p + 1) * NXY)
        first_half = slice(p * NXY, p * NXY + half)
        second_half = slice(p * NXY + half, (p + 1) * NXY)
        rows = slice(p // 2 * COLS, (p // 2 + 1) * COLS)
        packed = slice(p % 2 * half, (p % 2 + 1) * half)
        for r in range(ROWS):
            current = f_ref[r, :, lanes].astype(F32)
            above = upper_ref[rows, packed] if r == ROWS - 1 else f_ref[r + 1, :, first_half]
            below = lower_ref[rows, packed] if r == 0 else f_ref[r - 1, :, second_half]
            across = jnp.concatenate([above, below], axis=1).astype(F32)
            left = left_edge[r * PLANES + p : r * PLANES + p + 1, :]
            right = right_edge[r * PLANES + p : r * PLANES + p + 1, :]
            left = jnp.where(col == 0, left, pltpu.roll(current, 1, 0))
            right = jnp.where(col == COLS - 1, right, pltpu.roll(current, COLS - 1, 0))
            along = jnp.where(upwind, left, right)
            start = p * CELLS + r * COLS
            moved_ref[start : start + COLS, :] = current - (
                cx * (current - across) + cy * (current - along)
            )
    for copy in second:
        copy.wait()
    mixed = jnp.concatenate([back_ref[v] for v in range(GROUP)], axis=1)
    collision = jnp.dot(mixed, weights_ref[...], preferred_element_type=F32)
    stores = []
    for p in range(PLANES):
        for r in range(ROWS):
            start = p * CELLS + r * COLS
            value = moved_ref[start : start + COLS, :] + RELAX_RATE * collision[start : start + COLS, :]
            out_ref[r, :, p * NXY : (p + 1) * NXY] = value.astype(BF16)
        lanes = pl.ds(p * NXY, NXY)
        stores.append(
            pltpu.make_async_copy(
                out_ref.at[:, :, lanes], out_hbm.at[:, :, lanes], out_sem.at[p]
            )
        )
        stores[-1].start()
    for copy in stores:
        copy.wait()


def advance(core, f, back, weights, below, above, inner, outer):
    weights = pltpu.with_memory_space_constraint(weights, pltpu.HBM)
    return pl.pallas_call(
        advance_kernel,
        out_shape=jax.ShapeDtypeStruct(f.shape, BF16),
        in_specs=[smem()] + [hbm()] * 7,
        out_specs=hbm(),
        scratch_shapes=[
            pltpu.VMEM(f.shape, BF16),
            pltpu.VMEM(back.shape, BF16),
            pltpu.VMEM(weights.shape, BF16),
            pltpu.VMEM((2 * COLS, NXY), BF16),
            pltpu.VMEM((2 * COLS, NXY), BF16),
            pltpu.VMEM(inner.shape, BF16),
            pltpu.VMEM((16, NXY), BF16),
            pltpu.VMEM((DATA, NXY), F32),
            pltpu.VMEM(f.shape, BF16),
            pltpu.SemaphoreType.DMA((7,)),
            pltpu.SemaphoreType.DMA((PLANES,)),
        ],
        compiler_params=pltpu.CompilerParams(vmem_limit_bytes=LIMIT),
        name="advance",
    )(core, f, back, weights, below, above, inner, outer)


def ring(axis, step):
    count = lax.axis_size(axis)
    return [(i, (i + step) % count) for i in range(count)]


def local(distribution, plane_weights, depth_weights):
    place = lax.axis_index("vel").astype(jnp.int32).reshape(1)
    along = lax.axis_index("sy").astype(jnp.int32)
    core = jnp.bitwise_and(along, 1).reshape(1)
    where = jnp.stack([along, lax.axis_index("sx").astype(jnp.int32)])
    flip = lambda bit: [(i, i ^ bit) for i in range(8)]
    bundle, inner = columns(core, distribution, plane_weights)
    outer = lax.ppermute(bundle, "sy", [(i, (i + 1) % 8 if i % 2 else (i - 1) % 8) for i in range(8)])
    held = jnp.concatenate([plane_weights, outer[: plane_weights.shape[0]]])
    held = jnp.concatenate([held, lax.ppermute(held, "sy", flip(4))])
    send, held = lax.optimization_barrier((pack(place, distribution), held))
    got = lax.all_to_all(send, "vel", 0, 0, tiled=True)
    held = jnp.concatenate([held, lax.ppermute(held, "sx", flip(4))])
    low, high = edges(held, distribution)
    mix = spread(depth_weights)
    above = lax.ppermute(low, "sx", ring("sx", -1))
    below = lax.ppermute(high, "sx", ring("sx", 1))
    across = lax.ppermute(held, "sx", [(i, (i + 2) % 8 if i % 2 == 0 else (i - 2) % 8) for i in range(8)])
    own = join(held, above, below, across, inner)
    other = lax.ppermute(own, "sy", flip(1))
    weights, inner = assemble(where, own, other)
    back = lax.all_to_all(relax(place, got, mix), "vel", 0, 0, tiled=True)
    return advance(core, distribution, back, weights, below, above, inner, outer)


def solution(mesh):
    return jax.shard_map(
        local,
        mesh=mesh,
        in_specs=(P("sx", "sy", "vel"), P(("sx", "sy"), None), P()),
        out_specs=P("sx", "sy", "vel"),
        check_vma=False,
    )
```

```python
import jax
import jax.numpy as jnp
import numpy as np
from jax import lax
from jax.experimental import pallas as pl
from jax.experimental.pallas import tpu as pltpu
from jax.sharding import PartitionSpec as P

NVZ = 32
NVX = 32
NVY = 32
NXY = NVX * NVY
COURANT = 0.45
RELAX_RATE = 0.3
ROWS = 3
COLS = 32
CELLS = ROWS * COLS
PLANES = 4
GROUP = 8
BLOCK = NXY // GROUP
DATA = PLANES * CELLS
CHUNK = DATA + 16
TILE = 16
LIMIT = 16 << 20
F32 = jnp.float32
BF16 = jnp.bfloat16


def speed(index, count):
    return (index.astype(F32) - (count - 1) / 2.0) * (8.0 / count)


def lane_speeds(shape, offset):
    lane = lax.broadcasted_iota(jnp.int32, shape, len(shape) - 1) + offset
    return speed(lane // NVY, NVX), speed(lane % NVY, NVY)


def vmem():
    return pl.BlockSpec(memory_space=pltpu.VMEM)


def hbm():
    return pl.BlockSpec(memory_space=pltpu.HBM)


def smem():
    return pl.BlockSpec(memory_space=pltpu.SMEM)


def moment_basis():
    lane = np.arange(NXY)
    vx = (lane // NVY - (NVX - 1) / 2.0) * (8.0 / NVX)
    vy = (lane % NVY - (NVY - 1) / 2.0) * (8.0 / NVY)
    squared = (vx * vx + vy * vy).astype(np.float32)
    rough = squared.astype(BF16).astype(np.float32)
    basis = np.zeros((NXY, 128), np.float32)
    for part in range(3):
        basis[:, part * 5] = 1.0
        basis[:, part * 5 + 1] = vx
        basis[:, part * 5 + 2] = vy
        basis[:, part * 5 + 3] = 1.0
        basis[:, part * 5 + 4] = rough
        basis[:, 16 + part * 5 + 4] = squared - rough
        basis[:, 32 + part * 5 + 4] = 1.0
    return basis.astype(BF16)


def pack_kernel(place_ref, f_ref, basis_ref, send_ref, x_ref, base_ref, out_ref, in_sem, base_sem, out_sem):
    def load(p):
        lanes = pl.ds(p * NXY, NXY)
        return pltpu.make_async_copy(f_ref.at[:, :, lanes], x_ref.at[p], in_sem.at[p])

    def store(p):
        rows = pl.ds(p * CELLS, CELLS)
        return pltpu.make_async_copy(out_ref.at[:, rows, :], send_ref.at[:, rows, :], out_sem.at[p])

    base = pltpu.make_async_copy(basis_ref, base_ref, base_sem)
    load(0).start()
    base.start()
    for p in range(1, PLANES):
        load(p).start()
    lane = lax.broadcasted_iota(jnp.int32, (1, 128), 1)
    first_plane = place_ref[0] * PLANES
    total = jnp.zeros((CELLS, 128), F32)
    for p in range(PLANES):
        load(p).wait()
        x = x_ref[p].reshape(CELLS, NXY)
        for v in range(GROUP):
            out_ref[v, p * CELLS : (p + 1) * CELLS, :] = x[:, v * BLOCK : (v + 1) * BLOCK]
        store(p).start()
        if p == 0:
            base.wait()
        sums = jnp.dot(x, base_ref[...], preferred_element_type=F32)
        vz = speed(first_plane + p, NVZ)
        factor = jnp.where(lane >= 32, vz * vz, jnp.where((lane < 16) & (lane % 5 == 3), vz, 1.0))
        total = total + sums * factor
    total = jnp.transpose(total)
    total = (total[0:16, :] + total[16:32, :]) + total[32:48, :]
    column = lax.broadcasted_iota(jnp.int32, (16, CELLS), 0)
    high = total.astype(BF16).astype(F32)
    middle = (total - high).astype(BF16).astype(F32)
    low = (total - high) - middle
    parts = jnp.where(
        column < 5, high, jnp.where(column < 10, middle, jnp.where(column < 15, low, 0.0))
    )
    parts = jnp.concatenate([parts, jnp.zeros((16, 128 - CELLS), F32)], axis=1).astype(BF16)
    for v in range(GROUP):
        out_ref[v, DATA:CHUNK, :] = parts
    tail = pl.ds(DATA, CHUNK - DATA)
    last = pltpu.make_async_copy(
        out_ref.at[:, tail, :], send_ref.at[:, tail, :], out_sem.at[PLANES]
    )
    last.start()
    for p in range(PLANES):
        store(p).wait()
    last.wait()


def pack(place, f):
    basis = jnp.asarray(moment_basis())
    f, basis = (pltpu.with_memory_space_constraint(x, pltpu.HBM) for x in (f, basis))
    return pl.pallas_call(
        pack_kernel,
        out_shape=jax.ShapeDtypeStruct((GROUP, CHUNK, BLOCK), BF16),
        in_specs=[smem(), hbm(), hbm()],
        out_specs=hbm(),
        scratch_shapes=[
            pltpu.VMEM((PLANES, ROWS, COLS, NXY), BF16),
            pltpu.VMEM((NXY, 128), BF16),
            pltpu.VMEM((GROUP, CHUNK, BLOCK), BF16),
            pltpu.SemaphoreType.DMA((PLANES,)),
            pltpu.SemaphoreType.DMA(()),
            pltpu.SemaphoreType.DMA((PLANES + 1,)),
        ],
        compiler_params=pltpu.CompilerParams(vmem_limit_bytes=LIMIT),
        name="pack",
    )(place, f, basis)


def columns_kernel(core_ref, f_hbm, shard_hbm, pack_ref, inner_ref, first_ref, last_ref, sem):
    shard = shard_hbm.shape[0]
    copies = [
        pltpu.make_async_copy(f_hbm.at[:, pl.ds(0, 8), :], first_ref, sem.at[0]),
        pltpu.make_async_copy(f_hbm.at[:, pl.ds(COLS - 8, 8), :], last_ref, sem.at[1]),
        pltpu.make_async_copy(shard_hbm, pack_ref.at[pl.ds(0, shard)], sem.at[2]),
    ]
    for copy in copies:
        copy.start()
    edge_row = lax.broadcasted_iota(jnp.int32, (16, NXY), 0)
    first = jnp.zeros((16, NXY), F32)
    last = jnp.zeros((16, NXY), F32)
    for copy in copies:
        copy.wait()
    for r in range(ROWS):
        for p in range(PLANES):
            lanes = slice(p * NXY, (p + 1) * NXY)
            a = first_ref[r, :, lanes].astype(F32)[0:1, :]
            b = last_ref[r, :, lanes].astype(F32)[7:8, :]
            first = jnp.where(edge_row == r * PLANES + p, a, first)
            last = jnp.where(edge_row == r * PLANES + p, b, last)
    core = core_ref[0]
    inner_ref[...] = jnp.where(core == 0, last, first).astype(BF16)
    pack_ref[shard : shard + 16, :] = jnp.where(core == 0, first, last).astype(BF16)


def columns(core, f, shard):
    f, shard = (pltpu.with_memory_space_constraint(x, pltpu.HBM) for x in (f, shard))
    return pl.pallas_call(
        columns_kernel,
        out_shape=(
            jax.ShapeDtypeStruct((shard.shape[0] + 16, NXY), BF16),
            jax.ShapeDtypeStruct((16, NXY), BF16),
        ),
        in_specs=[smem(), hbm(), hbm()],
        out_specs=(vmem(), vmem()),
        scratch_shapes=[
            pltpu.VMEM((ROWS, 8, PLANES * NXY), BF16),
            pltpu.VMEM((ROWS, 8, PLANES * NXY), BF16),
            pltpu.SemaphoreType.DMA((3,)),
        ],
        compiler_params=pltpu.CompilerParams(vmem_limit_bytes=LIMIT),
        name="columns",
    )(core, f, shard)


def edges_kernel(held_ref, f_ref, low_ref, high_ref):
    half = NXY // 2
    size = held_ref.shape[0]
    low_ref[0:size, :] = held_ref[...]
    high_ref[0:size, :] = held_ref[...]
    for p in range(PLANES):
        rows = slice(size + p // 2 * COLS, size + (p // 2 + 1) * COLS)
        lanes = slice(p % 2 * half, (p % 2 + 1) * half)
        high_ref[rows, lanes] = f_ref[ROWS - 1, :, p * NXY + half : (p + 1) * NXY]
        low_ref[rows, lanes] = f_ref[0, :, p * NXY : p * NXY + half]


def edges(held, f):
    row = jax.ShapeDtypeStruct((held.shape[0] + 2 * COLS, NXY), BF16)
    return pl.pallas_call(
        edges_kernel,
        out_shape=(row, row),
        in_specs=[vmem(), vmem()],
        out_specs=(vmem(), vmem()),
        compiler_params=pltpu.CompilerParams(vmem_limit_bytes=LIMIT),
        name="edges",
    )(held, f)


def join_kernel(*refs):
    *parts, inner_ref, out_ref, sem = refs
    size = (out_ref.shape[0] - 16) // len(parts)
    copies = []
    for m, ref in enumerate(parts):
        copies.append(
            pltpu.make_async_copy(
                ref.at[pl.ds(0, size)], out_ref.at[pl.ds(m * size, size)], sem.at[m]
            )
        )
    copies.append(
        pltpu.make_async_copy(inner_ref, out_ref.at[pl.ds(len(parts) * size, 16)], sem.at[len(parts)])
    )
    for copy in copies:
        copy.start()
    for copy in copies:
        copy.wait()


def join(parts, inner):
    return pl.pallas_call(
        join_kernel,
        out_shape=jax.ShapeDtypeStruct((len(parts) * parts[0].shape[0] + 16, NXY), BF16),
        in_specs=[hbm()] * (len(parts) + 1),
        out_specs=hbm(),
        scratch_shapes=[pltpu.SemaphoreType.DMA((len(parts) + 1,))],
        compiler_params=pltpu.CompilerParams(vmem_limit_bytes=LIMIT),
        name="join",
    )(*parts, inner)


def assemble_kernel(where_ref, own_ref, other_ref, out_hbm, inner_hbm, rows_ref, turned_ref, sem):
    half = NXY // 2
    edge = pltpu.make_async_copy(other_ref.at[pl.ds(half, 16)], inner_hbm, sem.at[1])
    edge.start()
    mine, y = where_ref[0], where_ref[1]
    for side, ref in ((mine, own_ref), (jnp.bitwise_xor(mine, 1), other_ref)):
        turn = jnp.bitwise_xor(side, 4)
        step = jnp.where(side % 2 == 1, 1, 7)
        places = (side, (side + step) % 8, turn, (turn + step) % 8)
        for m, away in enumerate((0, 1, 7, 2, 6, 3, 5, 4)):
            for j in range(4):
                block = slice((m * 4 + j) * 16, (m * 4 + j + 1) * 16)
                rows_ref[(y + away) % 8 * 8 + places[j]] = ref[block, :]
    turned_ref[...] = jnp.transpose(rows_ref[...].reshape(NXY, NXY))
    copy = pltpu.make_async_copy(turned_ref, out_hbm, sem.at[0])
    copy.start()
    edge.wait()
    copy.wait()


def assemble(where, own, other):
    return pl.pallas_call(
        assemble_kernel,
        out_shape=(pltpu.HBM((NXY, NXY), BF16), jax.ShapeDtypeStruct((16, NXY), BF16)),
        in_specs=[smem(), vmem(), vmem()],
        out_specs=(hbm(), hbm()),
        scratch_shapes=[
            pltpu.VMEM((NXY // 16, 16, NXY), BF16),
            pltpu.VMEM((NXY, NXY), BF16),
            pltpu.SemaphoreType.DMA((2,)),
        ],
        compiler_params=pltpu.CompilerParams(vmem_limit_bytes=LIMIT),
        name="assemble",
    )(where, own, other)


def spread_kernel(depth_ref, out_ref):
    size = NVZ * TILE
    row = lax.broadcasted_iota(jnp.int32, (size, NVZ), 0)
    col = lax.broadcasted_iota(jnp.int32, (size, NVZ), 1)
    pick = jnp.where(row // TILE == col, 1.0, 0.0).astype(BF16)
    left = jnp.dot(pick, depth_ref[...], preferred_element_type=F32).astype(BF16)
    full = lax.dot_general(left, pick, (((1,), (1,)), ((), ())), preferred_element_type=F32)
    i = lax.broadcasted_iota(jnp.int32, (size, size), 0)
    j = lax.broadcasted_iota(jnp.int32, (size, size), 1)
    out_ref[...] = jnp.where(i % TILE == j % TILE, full, 0.0).astype(BF16)


def spread(depth_weights):
    size = NVZ * TILE
    return pl.pallas_call(
        spread_kernel,
        out_shape=jax.ShapeDtypeStruct((size, size), BF16),
        in_specs=[vmem()],
        out_specs=vmem(),
        compiler_params=pltpu.CompilerParams(vmem_limit_bytes=LIMIT),
        name="spread",
    )(depth_weights)


def relax_kernel(place_ref, got_ref, mix_ref, send_ref, dev_ref):
    pieces = jnp.concatenate([got_ref[v, DATA:CHUNK, :] for v in range(GROUP)], axis=0)
    i = lax.broadcasted_iota(jnp.int32, (GROUP * 16, 128), 0) % 16
    j = lax.broadcasted_iota(jnp.int32, (GROUP * 16, 128), 1)
    pick = jnp.where((i % 5 == j) & (i < 15), 1.0, 0.0).astype(BF16)
    moments = lax.dot_general(pieces, pick, (((0,), (0,)), ((), ())), preferred_element_type=F32)
    moments = moments[:CELLS, :]
    density = moments[:, 0:1]
    ux = moments[:, 1:2] / density
    uy = moments[:, 2:3] / density
    uz = moments[:, 3:4] / density
    heat = (moments[:, 4:5] / density - (ux * ux + uy * uy + uz * uz)) / 3.0
    measure = (8.0 / NVX) * (8.0 / NVY) * (8.0 / NVZ)
    width = 2.0 * jnp.pi * heat
    scale = density * measure / (width * jnp.sqrt(width))
    inverse = -1.0 / (2.0 * heat)
    vx, vy = lane_speeds((CELLS, BLOCK), place_ref[0] * BLOCK)
    dx = vx - ux
    dy = vy - uy
    plane = scale * jnp.exp((dx * dx + dy * dy) * inverse)
    dz = speed(lax.broadcasted_iota(jnp.int32, (CELLS, 128), 1), NVZ) - uz
    depth = jnp.exp((dz * dz) * inverse)
    for w in range(NVZ):
        v, p = w // PLANES, w % PLANES
        f = got_ref[v, p * CELLS : (p + 1) * CELLS, :].astype(F32)
        deviation = (depth[:, w : w + 1] * plane - f).astype(BF16)
        for t in range(CELLS // TILE):
            dev_ref[w * TILE : (w + 1) * TILE, t * BLOCK : (t + 1) * BLOCK] = deviation[
                t * TILE : (t + 1) * TILE, :
            ]
    mixed = jnp.dot(mix_ref[...], dev_ref[...], preferred_element_type=F32).astype(BF16)
    for w in range(NVZ):
        v, p = w // PLANES, w % PLANES
        for t in range(CELLS // TILE):
            send_ref[v, p * CELLS + t * TILE : p * CELLS + (t + 1) * TILE, :] = mixed[
                w * TILE : (w + 1) * TILE, t * BLOCK : (t + 1) * BLOCK
            ]


def relax(place, got, mix):
    return pl.pallas_call(
        relax_kernel,
        out_shape=jax.ShapeDtypeStruct((GROUP, DATA, BLOCK), BF16),
        in_specs=[smem(), vmem(), vmem()],
        out_specs=vmem(),
        scratch_shapes=[pltpu.VMEM((NVZ * TILE, CELLS // TILE * BLOCK), BF16)],
        compiler_params=pltpu.CompilerParams(vmem_limit_bytes=LIMIT),
        name="relax",
    )(place, got, mix)


def advance_kernel(
    core_ref,
    f_hbm,
    back_hbm,
    weights_hbm,
    below_hbm,
    above_hbm,
    inner_hbm,
    outer_hbm,
    out_hbm,
    f_ref,
    back_ref,
    weights_ref,
    lower_ref,
    upper_ref,
    inner_ref,
    outer_ref,
    moved_ref,
    out_ref,
    sem,
    out_sem,
):
    edge = pl.ds(below_hbm.shape[0] - 2 * COLS, 2 * COLS)
    first = [
        pltpu.make_async_copy(below_hbm.at[edge], lower_ref, sem.at[0]),
        pltpu.make_async_copy(above_hbm.at[edge], upper_ref, sem.at[1]),
        pltpu.make_async_copy(inner_hbm, inner_ref, sem.at[2]),
        pltpu.make_async_copy(outer_hbm.at[pl.ds(outer_hbm.shape[0] - 16, 16)], outer_ref, sem.at[3]),
        pltpu.make_async_copy(f_hbm, f_ref, sem.at[4]),
    ]
    second = [
        pltpu.make_async_copy(back_hbm, back_ref, sem.at[5]),
        pltpu.make_async_copy(weights_hbm, weights_ref, sem.at[6]),
    ]
    for copy in first + second:
        copy.start()
    half = NXY // 2
    vx, vy = lane_speeds((COLS, NXY), 0)
    courant_across = COURANT / (4.0 - 4.0 / NVX)
    courant_along = COURANT / (4.0 - 4.0 / NVY)
    cx = courant_across * jnp.abs(vx)
    cy = courant_along * jnp.abs(vy)
    upwind = vy > 0.0
    col = lax.broadcasted_iota(jnp.int32, (COLS, NXY), 0)
    core = core_ref[0]
    for copy in first:
        copy.wait()
    inner = inner_ref[...].astype(F32)
    outer = outer_ref[...].astype(F32)
    left_edge = jnp.where(core == 0, outer, inner)
    right_edge = jnp.where(core == 0, inner, outer)
    for p in range(PLANES):
        lanes = slice(p * NXY, (p + 1) * NXY)
        first_half = slice(p * NXY, p * NXY + half)
        second_half = slice(p * NXY + half, (p + 1) * NXY)
        rows = slice(p // 2 * COLS, (p // 2 + 1) * COLS)
        packed = slice(p % 2 * half, (p % 2 + 1) * half)
        for r in range(ROWS):
            current = f_ref[r, :, lanes].astype(F32)
            above = upper_ref[rows, packed] if r == ROWS - 1 else f_ref[r + 1, :, first_half]
            below = lower_ref[rows, packed] if r == 0 else f_ref[r - 1, :, second_half]
            across = jnp.concatenate([above, below], axis=1).astype(F32)
            left = left_edge[r * PLANES + p : r * PLANES + p + 1, :]
            right = right_edge[r * PLANES + p : r * PLANES + p + 1, :]
            left = jnp.where(col == 0, left, pltpu.roll(current, 1, 0))
            right = jnp.where(col == COLS - 1, right, pltpu.roll(current, COLS - 1, 0))
            along = jnp.where(upwind, left, right)
            start = p * CELLS + r * COLS
            moved_ref[start : start + COLS, :] = current - (
                cx * (current - across) + cy * (current - along)
            )
    for copy in second:
        copy.wait()
    mixed = jnp.concatenate([back_ref[v] for v in range(GROUP)], axis=1)
    collision = jnp.dot(mixed, weights_ref[...], preferred_element_type=F32)
    stores = []
    for p in range(PLANES):
        for r in range(ROWS):
            start = p * CELLS + r * COLS
            value = moved_ref[start : start + COLS, :] + RELAX_RATE * collision[start : start + COLS, :]
            out_ref[r, :, p * NXY : (p + 1) * NXY] = value.astype(BF16)
        lanes = pl.ds(p * NXY, NXY)
        stores.append(
            pltpu.make_async_copy(
                out_ref.at[:, :, lanes], out_hbm.at[:, :, lanes], out_sem.at[p]
            )
        )
        stores[-1].start()
    for copy in stores:
        copy.wait()


def advance(core, f, back, weights, below, above, inner, outer):
    weights = pltpu.with_memory_space_constraint(weights, pltpu.HBM)
    return pl.pallas_call(
        advance_kernel,
        out_shape=jax.ShapeDtypeStruct(f.shape, BF16),
        in_specs=[smem()] + [hbm()] * 7,
        out_specs=hbm(),
        scratch_shapes=[
            pltpu.VMEM(f.shape, BF16),
            pltpu.VMEM(back.shape, BF16),
            pltpu.VMEM(weights.shape, BF16),
            pltpu.VMEM((2 * COLS, NXY), BF16),
            pltpu.VMEM((2 * COLS, NXY), BF16),
            pltpu.VMEM(inner.shape, BF16),
            pltpu.VMEM((16, NXY), BF16),
            pltpu.VMEM((DATA, NXY), F32),
            pltpu.VMEM(f.shape, BF16),
            pltpu.SemaphoreType.DMA((7,)),
            pltpu.SemaphoreType.DMA((PLANES,)),
        ],
        compiler_params=pltpu.CompilerParams(vmem_limit_bytes=LIMIT),
        name="advance",
    )(core, f, back, weights, below, above, inner, outer)


def ring(axis, step):
    count = lax.axis_size(axis)
    return [(i, (i + step) % count) for i in range(count)]


def local(distribution, plane_weights, depth_weights):
    place = lax.axis_index("vel").astype(jnp.int32).reshape(1)
    along = lax.axis_index("sy").astype(jnp.int32)
    core = jnp.bitwise_and(along, 1).reshape(1)
    where = jnp.stack([along, lax.axis_index("sx").astype(jnp.int32)])
    flip = lambda bit: [(i, i ^ bit) for i in range(8)]
    bundle, inner = columns(core, distribution, plane_weights)
    outer = lax.ppermute(bundle, "sy", [(i, (i + 1) % 8 if i % 2 else (i - 1) % 8) for i in range(8)])
    held = jnp.concatenate([plane_weights, outer[: plane_weights.shape[0]]])
    held = jnp.concatenate([held, lax.ppermute(held, "sy", flip(4))])
    send, held = lax.optimization_barrier((pack(place, distribution), held))
    got = lax.all_to_all(send, "vel", 0, 0, tiled=True)
    far = [lax.ppermute(held, "sx", ring("sx", -away)) for away in (2, 6, 3, 5, 4)]
    low, high = edges(held, distribution)
    mix = spread(depth_weights)
    above = lax.ppermute(low, "sx", ring("sx", -1))
    below = lax.ppermute(high, "sx", ring("sx", 1))
    send = relax(place, got, mix)
    send, *far = lax.optimization_barrier((send, *far))
    own = join([held, above, below] + far, inner)
    other = lax.ppermute(own, "sy", flip(1))
    weights, inner = assemble(where, own, other)
    back = lax.all_to_all(send, "vel", 0, 0, tiled=True)
    return advance(core, distribution, back, weights, below, above, inner, outer)


def solution(mesh):
    return jax.shard_map(
        local,
        mesh=mesh,
        in_specs=(P("sx", "sy", "vel"), P(("sx", "sy"), None), P()),
        out_specs=P("sx", "sy", "vel"),
        check_vma=False,
    )
```

```python
import jax
import jax.numpy as jnp
import numpy as np
from jax import lax
from jax.experimental import pallas as pl
from jax.experimental.pallas import tpu as pltpu
from jax.sharding import PartitionSpec as P

NVZ = 32
NVX = 32
NVY = 32
NXY = NVX * NVY
COURANT = 0.45
RELAX_RATE = 0.3
ROWS = 3
COLS = 32
CELLS = ROWS * COLS
PLANES = 4
GROUP = 8
BLOCK = NXY // GROUP
DATA = PLANES * CELLS
CHUNK = DATA + 16
TILE = 16
LIMIT = 16 << 20
F32 = jnp.float32
BF16 = jnp.bfloat16


def speed(index, count):
    return (index.astype(F32) - (count - 1) / 2.0) * (8.0 / count)


def lane_speeds(shape, offset):
    lane = lax.broadcasted_iota(jnp.int32, shape, len(shape) - 1) + offset
    return speed(lane // NVY, NVX), speed(lane % NVY, NVY)


def vmem():
    return pl.BlockSpec(memory_space=pltpu.VMEM)


def hbm():
    return pl.BlockSpec(memory_space=pltpu.HBM)


def smem():
    return pl.BlockSpec(memory_space=pltpu.SMEM)


def moment_basis():
    lane = np.arange(NXY)
    vx = (lane // NVY - (NVX - 1) / 2.0) * (8.0 / NVX)
    vy = (lane % NVY - (NVY - 1) / 2.0) * (8.0 / NVY)
    squared = (vx * vx + vy * vy).astype(np.float32)
    rough = squared.astype(BF16).astype(np.float32)
    basis = np.zeros((NXY, 128), np.float32)
    for part in range(3):
        basis[:, part * 5] = 1.0
        basis[:, part * 5 + 1] = vx
        basis[:, part * 5 + 2] = vy
        basis[:, part * 5 + 3] = 1.0
        basis[:, part * 5 + 4] = rough
        basis[:, 16 + part * 5 + 4] = squared - rough
        basis[:, 32 + part * 5 + 4] = 1.0
    return basis.astype(BF16)


def pack_kernel(place_ref, f_ref, basis_ref, send_ref, x_ref, base_ref, out_ref, in_sem, base_sem, out_sem):
    def load(p):
        lanes = pl.ds(p * NXY, NXY)
        return pltpu.make_async_copy(f_ref.at[:, :, lanes], x_ref.at[p], in_sem.at[p])

    def store(p):
        rows = pl.ds(p * CELLS, CELLS)
        return pltpu.make_async_copy(out_ref.at[:, rows, :], send_ref.at[:, rows, :], out_sem.at[p])

    base = pltpu.make_async_copy(basis_ref, base_ref, base_sem)
    load(0).start()
    base.start()
    for p in range(1, PLANES):
        load(p).start()
    lane = lax.broadcasted_iota(jnp.int32, (1, 128), 1)
    first_plane = place_ref[0] * PLANES
    total = jnp.zeros((CELLS, 128), F32)
    for p in range(PLANES):
        load(p).wait()
        x = x_ref[p].reshape(CELLS, NXY)
        for v in range(GROUP):
            out_ref[v, p * CELLS : (p + 1) * CELLS, :] = x[:, v * BLOCK : (v + 1) * BLOCK]
        store(p).start()
        if p == 0:
            base.wait()
        sums = jnp.dot(x, base_ref[...], preferred_element_type=F32)
        vz = speed(first_plane + p, NVZ)
        factor = jnp.where(lane >= 32, vz * vz, jnp.where((lane < 16) & (lane % 5 == 3), vz, 1.0))
        total = total + sums * factor
    total = jnp.transpose(total)
    total = (total[0:16, :] + total[16:32, :]) + total[32:48, :]
    column = lax.broadcasted_iota(jnp.int32, (16, CELLS), 0)
    high = total.astype(BF16).astype(F32)
    middle = (total - high).astype(BF16).astype(F32)
    low = (total - high) - middle
    parts = jnp.where(
        column < 5, high, jnp.where(column < 10, middle, jnp.where(column < 15, low, 0.0))
    )
    parts = jnp.concatenate([parts, jnp.zeros((16, 128 - CELLS), F32)], axis=1).astype(BF16)
    for v in range(GROUP):
        out_ref[v, DATA:CHUNK, :] = parts
    tail = pl.ds(DATA, CHUNK - DATA)
    last = pltpu.make_async_copy(
        out_ref.at[:, tail, :], send_ref.at[:, tail, :], out_sem.at[PLANES]
    )
    last.start()
    for p in range(PLANES):
        store(p).wait()
    last.wait()


def pack(place, f):
    basis = jnp.asarray(moment_basis())
    f, basis = (pltpu.with_memory_space_constraint(x, pltpu.HBM) for x in (f, basis))
    return pl.pallas_call(
        pack_kernel,
        out_shape=jax.ShapeDtypeStruct((GROUP, CHUNK, BLOCK), BF16),
        in_specs=[smem(), hbm(), hbm()],
        out_specs=hbm(),
        scratch_shapes=[
            pltpu.VMEM((PLANES, ROWS, COLS, NXY), BF16),
            pltpu.VMEM((NXY, 128), BF16),
            pltpu.VMEM((GROUP, CHUNK, BLOCK), BF16),
            pltpu.SemaphoreType.DMA((PLANES,)),
            pltpu.SemaphoreType.DMA(()),
            pltpu.SemaphoreType.DMA((PLANES + 1,)),
        ],
        compiler_params=pltpu.CompilerParams(vmem_limit_bytes=LIMIT),
        name="pack",
    )(place, f, basis)


def edges_kernel(
    core_ref, f_ref, low_hbm, high_hbm, inner_ref, outer_ref, low_ref, high_ref, sem
):
    half = NXY // 2
    for p in range(PLANES):
        rows = slice(p // 2 * COLS, (p // 2 + 1) * COLS)
        lanes = slice(p % 2 * half, (p % 2 + 1) * half)
        high_ref[rows, lanes] = f_ref[ROWS - 1, :, p * NXY + half : (p + 1) * NXY]
        low_ref[rows, lanes] = f_ref[0, :, p * NXY : p * NXY + half]
    copies = [
        pltpu.make_async_copy(low_ref, low_hbm, sem.at[0]),
        pltpu.make_async_copy(high_ref, high_hbm, sem.at[1]),
    ]
    for copy in copies:
        copy.start()
    edge_row = lax.broadcasted_iota(jnp.int32, (16, NXY), 0)
    first = jnp.zeros((16, NXY), F32)
    last = jnp.zeros((16, NXY), F32)
    for r in range(ROWS):
        for p in range(PLANES):
            lanes = slice(p * NXY, (p + 1) * NXY)
            a = f_ref[r, 0:8, lanes].astype(F32)[0:1, :]
            b = f_ref[r, COLS - 8 : COLS, lanes].astype(F32)[7:8, :]
            first = jnp.where(edge_row == r * PLANES + p, a, first)
            last = jnp.where(edge_row == r * PLANES + p, b, last)
    core = core_ref[0]
    inner_ref[...] = jnp.where(core == 0, last, first).astype(BF16)
    outer_ref[...] = jnp.where(core == 0, first, last).astype(BF16)
    for copy in copies:
        copy.wait()


def edges(core, f):
    row = pltpu.HBM((2 * COLS, NXY), BF16)
    column = jax.ShapeDtypeStruct((16, NXY), BF16)
    return pl.pallas_call(
        edges_kernel,
        out_shape=(row, row, column, column),
        in_specs=[smem(), vmem()],
        out_specs=(hbm(), hbm(), vmem(), vmem()),
        scratch_shapes=[
            pltpu.VMEM((2 * COLS, NXY), BF16),
            pltpu.VMEM((2 * COLS, NXY), BF16),
            pltpu.SemaphoreType.DMA((2,)),
        ],
        compiler_params=pltpu.CompilerParams(vmem_limit_bytes=LIMIT),
        name="edges",
    )(core, f)


def spray_kernel(place_ref, shard_ref, out_ref):
    start = place_ref[0] // 2 * 2 * BLOCK
    for core in range(2):
        offset = pl.multiple_of(start + core * BLOCK, BLOCK)
        part = shard_ref[:, pl.ds(offset, BLOCK)]
        for d in range(core, out_ref.shape[0], 2):
            out_ref[d] = part


def spray(place, shard, count):
    return pl.pallas_call(
        spray_kernel,
        out_shape=jax.ShapeDtypeStruct((count, shard.shape[0], BLOCK), BF16),
        in_specs=[smem(), vmem()],
        out_specs=vmem(),
        compiler_params=pltpu.CompilerParams(vmem_limit_bytes=LIMIT),
        name="spray",
    )(place, shard)


def join_kernel(*refs):
    *parts, inner_ref, out_ref, sem = refs
    size = parts[0].shape[0]
    copies = [
        pltpu.make_async_copy(ref, out_ref.at[pl.ds(m * size, size)], sem.at[m])
        for m, ref in enumerate(parts)
    ]
    for lane in range(NXY // BLOCK):
        rows = pl.ds(len(parts) * size + lane * 16, 16)
        copies.append(
            pltpu.make_async_copy(
                inner_ref.at[:, pl.ds(lane * BLOCK, BLOCK)], out_ref.at[rows], sem.at[len(parts) + lane]
            )
        )
    for copy in copies:
        copy.start()
    for copy in copies:
        copy.wait()


def join(parts, inner):
    size = parts[0].shape[0]
    lanes = NXY // BLOCK
    return pl.pallas_call(
        join_kernel,
        out_shape=pltpu.HBM((len(parts) * size + lanes * 16, BLOCK), BF16),
        in_specs=[hbm()] * (len(parts) + 1),
        out_specs=hbm(),
        scratch_shapes=[pltpu.SemaphoreType.DMA((len(parts) + lanes,))],
        compiler_params=pltpu.CompilerParams(vmem_limit_bytes=LIMIT),
        name="join",
    )(*parts, inner)


def spread_kernel(depth_ref, out_ref):
    size = NVZ * TILE
    row = lax.broadcasted_iota(jnp.int32, (size, NVZ), 0)
    col = lax.broadcasted_iota(jnp.int32, (size, NVZ), 1)
    pick = jnp.where(row // TILE == col, 1.0, 0.0).astype(BF16)
    left = jnp.dot(pick, depth_ref[...], preferred_element_type=F32).astype(BF16)
    full = lax.dot_general(left, pick, (((1,), (1,)), ((), ())), preferred_element_type=F32)
    i = lax.broadcasted_iota(jnp.int32, (size, size), 0)
    j = lax.broadcasted_iota(jnp.int32, (size, size), 1)
    out_ref[...] = jnp.where(i % TILE == j % TILE, full, 0.0).astype(BF16)


def spread(depth_weights):
    size = NVZ * TILE
    return pl.pallas_call(
        spread_kernel,
        out_shape=jax.ShapeDtypeStruct((size, size), BF16),
        in_specs=[vmem()],
        out_specs=vmem(),
        compiler_params=pltpu.CompilerParams(vmem_limit_bytes=LIMIT),
        name="spread",
    )(depth_weights)


def relax_kernel(place_ref, got_ref, mix_ref, send_ref, dev_ref):
    pieces = jnp.concatenate([got_ref[v, DATA:CHUNK, :] for v in range(GROUP)], axis=0)
    i = lax.broadcasted_iota(jnp.int32, (GROUP * 16, 128), 0) % 16
    j = lax.broadcasted_iota(jnp.int32, (GROUP * 16, 128), 1)
    pick = jnp.where((i % 5 == j) & (i < 15), 1.0, 0.0).astype(BF16)
    moments = lax.dot_general(pieces, pick, (((0,), (0,)), ((), ())), preferred_element_type=F32)
    moments = moments[:CELLS, :]
    density = moments[:, 0:1]
    ux = moments[:, 1:2] / density
    uy = moments[:, 2:3] / density
    uz = moments[:, 3:4] / density
    heat = (moments[:, 4:5] / density - (ux * ux + uy * uy + uz * uz)) / 3.0
    measure = (8.0 / NVX) * (8.0 / NVY) * (8.0 / NVZ)
    width = 2.0 * jnp.pi * heat
    scale = density * measure / (width * jnp.sqrt(width))
    inverse = -1.0 / (2.0 * heat)
    vx, vy = lane_speeds((CELLS, BLOCK), place_ref[0] * BLOCK)
    dx = vx - ux
    dy = vy - uy
    plane = scale * jnp.exp((dx * dx + dy * dy) * inverse)
    dz = speed(lax.broadcasted_iota(jnp.int32, (CELLS, 128), 1), NVZ) - uz
    depth = jnp.exp((dz * dz) * inverse)
    for w in range(NVZ):
        v, p = w // PLANES, w % PLANES
        f = got_ref[v, p * CELLS : (p + 1) * CELLS, :].astype(F32)
        deviation = (depth[:, w : w + 1] * plane - f).astype(BF16)
        for t in range(CELLS // TILE):
            dev_ref[w * TILE : (w + 1) * TILE, t * BLOCK : (t + 1) * BLOCK] = deviation[
                t * TILE : (t + 1) * TILE, :
            ]
    mixed = jnp.dot(mix_ref[...], dev_ref[...], preferred_element_type=F32).astype(BF16)
    for w in range(NVZ):
        v, p = w // PLANES, w % PLANES
        for t in range(CELLS // TILE):
            send_ref[v, p * CELLS + t * TILE : p * CELLS + (t + 1) * TILE, :] = mixed[
                w * TILE : (w + 1) * TILE, t * BLOCK : (t + 1) * BLOCK
            ]


def relax(place, got, mix):
    return pl.pallas_call(
        relax_kernel,
        out_shape=jax.ShapeDtypeStruct((GROUP, DATA, BLOCK), BF16),
        in_specs=[smem(), vmem(), vmem()],
        out_specs=vmem(),
        scratch_shapes=[pltpu.VMEM((NVZ * TILE, CELLS // TILE * BLOCK), BF16)],
        compiler_params=pltpu.CompilerParams(vmem_limit_bytes=LIMIT),
        name="relax",
    )(place, got, mix)


def advance_kernel(
    core_ref,
    f_hbm,
    back_hbm,
    own_hbm,
    other_hbm,
    below_hbm,
    above_hbm,
    outer_hbm,
    out_hbm,
    f_ref,
    back_ref,
    weights_ref,
    lower_ref,
    upper_ref,
    inner_ref,
    outer_ref,
    moved_ref,
    out_ref,
    sem,
    out_sem,
):
    first = [
        pltpu.make_async_copy(below_hbm, lower_ref, sem.at[0]),
        pltpu.make_async_copy(above_hbm, upper_ref, sem.at[1]),
        pltpu.make_async_copy(outer_hbm, outer_ref, sem.at[3]),
        pltpu.make_async_copy(f_hbm, f_ref, sem.at[4]),
    ]
    second = [pltpu.make_async_copy(back_hbm, back_ref, sem.at[5])]
    core, place = core_ref[0], core_ref[1]
    for m in range(4):
        column = jnp.bitwise_xor(place // 2, m) * 2
        block = pl.ds(m * NXY, NXY)
        second.append(
            pltpu.make_async_copy(own_hbm.at[block], weights_ref.at[column + core], sem.at[6 + m])
        )
        second.append(
            pltpu.make_async_copy(
                other_hbm.at[block], weights_ref.at[column + 1 - core], sem.at[10 + m]
            )
        )
    lanes_of = NXY // BLOCK
    for lane in range(lanes_of):
        first.append(
            pltpu.make_async_copy(
                other_hbm.at[pl.ds(4 * NXY + lane * 16, 16)],
                inner_ref.at[:, pl.ds(lane * BLOCK, BLOCK)],
                sem.at[14 + lane],
            )
        )
    for copy in first + second:
        copy.start()
    half = NXY // 2
    vx, vy = lane_speeds((COLS, NXY), 0)
    courant_across = COURANT / (4.0 - 4.0 / NVX)
    courant_along = COURANT / (4.0 - 4.0 / NVY)
    cx = courant_across * jnp.abs(vx)
    cy = courant_along * jnp.abs(vy)
    upwind = vy > 0.0
    col = lax.broadcasted_iota(jnp.int32, (COLS, NXY), 0)
    for copy in first:
        copy.wait()
    inner = inner_ref[...].astype(F32)
    outer = outer_ref[...].astype(F32)
    left_edge = jnp.where(core == 0, outer, inner)
    right_edge = jnp.where(core == 0, inner, outer)
    for p in range(PLANES):
        lanes = slice(p * NXY, (p + 1) * NXY)
        first_half = slice(p * NXY, p * NXY + half)
        second_half = slice(p * NXY + half, (p + 1) * NXY)
        rows = slice(p // 2 * COLS, (p // 2 + 1) * COLS)
        packed = slice(p % 2 * half, (p % 2 + 1) * half)
        for r in range(ROWS):
            current = f_ref[r, :, lanes].astype(F32)
            above = upper_ref[rows, packed] if r == ROWS - 1 else f_ref[r + 1, :, first_half]
            below = lower_ref[rows, packed] if r == 0 else f_ref[r - 1, :, second_half]
            across = jnp.concatenate([above, below], axis=1).astype(F32)
            left = left_edge[r * PLANES + p : r * PLANES + p + 1, :]
            right = right_edge[r * PLANES + p : r * PLANES + p + 1, :]
            left = jnp.where(col == 0, left, pltpu.roll(current, 1, 0))
            right = jnp.where(col == COLS - 1, right, pltpu.roll(current, COLS - 1, 0))
            along = jnp.where(upwind, left, right)
            start = p * CELLS + r * COLS
            moved_ref[start : start + COLS, :] = current - (
                cx * (current - across) + cy * (current - along)
            )
    for copy in second:
        copy.wait()
    mixed = jnp.concatenate([back_ref[v] for v in range(GROUP)], axis=1)
    weights = jnp.concatenate([weights_ref[v] for v in range(GROUP)], axis=1)
    collision = lax.dot_general(
        mixed, weights, (((1,), (1,)), ((), ())), preferred_element_type=F32
    )
    stores = []
    for p in range(PLANES):
        for r in range(ROWS):
            start = p * CELLS + r * COLS
            value = moved_ref[start : start + COLS, :] + RELAX_RATE * collision[start : start + COLS, :]
            out_ref[r, :, p * NXY : (p + 1) * NXY] = value.astype(BF16)
        lanes = pl.ds(p * NXY, NXY)
        stores.append(
            pltpu.make_async_copy(
                out_ref.at[:, :, lanes], out_hbm.at[:, :, lanes], out_sem.at[p]
            )
        )
        stores[-1].start()
    for copy in stores:
        copy.wait()


def advance(where, f, back, own, other, below, above, outer):
    own, other = (pltpu.with_memory_space_constraint(x, pltpu.HBM) for x in (own, other))
    return pl.pallas_call(
        advance_kernel,
        out_shape=jax.ShapeDtypeStruct(f.shape, BF16),
        in_specs=[smem()] + [hbm()] * 7,
        out_specs=hbm(),
        scratch_shapes=[
            pltpu.VMEM(f.shape, BF16),
            pltpu.VMEM(back.shape, BF16),
            pltpu.VMEM((GROUP, NXY, BLOCK), BF16),
            pltpu.VMEM((2 * COLS, NXY), BF16),
            pltpu.VMEM((2 * COLS, NXY), BF16),
            pltpu.VMEM((16, NXY), BF16),
            pltpu.VMEM((16, NXY), BF16),
            pltpu.VMEM((DATA, NXY), F32),
            pltpu.VMEM(f.shape, BF16),
            pltpu.SemaphoreType.DMA((14 + NXY // BLOCK,)),
            pltpu.SemaphoreType.DMA((PLANES,)),
        ],
        compiler_params=pltpu.CompilerParams(vmem_limit_bytes=LIMIT),
        name="advance",
    )(where, f, back, own, other, below, above, outer)


def ring(axis, step):
    count = lax.axis_size(axis)
    return [(i, (i + step) % count) for i in range(count)]


def local(distribution, plane_weights, depth_weights):
    place = lax.axis_index("vel").astype(jnp.int32).reshape(1)
    core = jnp.bitwise_and(lax.axis_index("sy").astype(jnp.int32), 1).reshape(1)
    where = jnp.concatenate([core, place])
    shard, width = plane_weights.shape
    count = lax.axis_size("sy")
    flip = lambda bit: [(i, i ^ bit) for i in range(8)]
    columns = lax.all_to_all(
        spray(place, plane_weights, width // shard), ("sx", "sy"), 0, 0, tiled=True
    ).reshape(width, BLOCK)
    send, columns = lax.optimization_barrier((pack(place, distribution), columns))
    got = lax.all_to_all(send, "vel", 0, 0, tiled=True)
    far = [lax.ppermute(columns, "vel", flip(2 * step)) for step in (1, 2, 3)]
    low, high, inner, outer = edges(core, distribution)
    outer = lax.ppermute(
        outer, "sy", [(i, (i + 1) % count if i % 2 else (i - 1) % count) for i in range(count)]
    )
    send = relax(place, got, spread(depth_weights))
    send, outer, *far = lax.optimization_barrier((send, outer, *far))
    own = join([columns] + far, inner)
    other = lax.ppermute(own, "sy", flip(1))
    above = lax.ppermute(low, "sx", ring("sx", -1))
    below = lax.ppermute(high, "sx", ring("sx", 1))
    back = lax.all_to_all(send, "vel", 0, 0, tiled=True)
    return advance(where, distribution, back, own, other, below, above, outer)


def solution(mesh):
    return jax.shard_map(
        local,
        mesh=mesh,
        in_specs=(P("sx", "sy", "vel"), P(("sx", "sy"), None), P()),
        out_specs=P("sx", "sy", "vel"),
        check_vma=False,
    )
```

```python
import jax
import jax.numpy as jnp
import numpy as np
from jax import lax
from jax.experimental import pallas as pl
from jax.experimental.pallas import tpu as pltpu
from jax.sharding import PartitionSpec as P

NVZ = 32
NVX = 32
NVY = 32
NXY = NVX * NVY
COURANT = 0.45
RELAX_RATE = 0.3
ROWS = 3
COLS = 32
CELLS = ROWS * COLS
PLANES = 4
GROUP = 8
BLOCK = NXY // GROUP
DATA = PLANES * CELLS
CHUNK = DATA + 16
TILE = 16
LIMIT = 16 << 20
F32 = jnp.float32
BF16 = jnp.bfloat16


def speed(index, count):
    return (index.astype(F32) - (count - 1) / 2.0) * (8.0 / count)


def lane_speeds(shape, offset):
    lane = lax.broadcasted_iota(jnp.int32, shape, len(shape) - 1) + offset
    return speed(lane // NVY, NVX), speed(lane % NVY, NVY)


def vmem():
    return pl.BlockSpec(memory_space=pltpu.VMEM)


def hbm():
    return pl.BlockSpec(memory_space=pltpu.HBM)


def smem():
    return pl.BlockSpec(memory_space=pltpu.SMEM)


def moment_basis():
    lane = np.arange(NXY)
    vx = (lane // NVY - (NVX - 1) / 2.0) * (8.0 / NVX)
    vy = (lane % NVY - (NVY - 1) / 2.0) * (8.0 / NVY)
    squared = (vx * vx + vy * vy).astype(np.float32)
    rough = squared.astype(BF16).astype(np.float32)
    basis = np.zeros((NXY, 128), np.float32)
    for part in range(3):
        basis[:, part * 5] = 1.0
        basis[:, part * 5 + 1] = vx
        basis[:, part * 5 + 2] = vy
        basis[:, part * 5 + 3] = 1.0
        basis[:, part * 5 + 4] = rough
        basis[:, 16 + part * 5 + 4] = squared - rough
        basis[:, 32 + part * 5 + 4] = 1.0
    return basis.astype(BF16)


def pack_kernel(place_ref, f_ref, basis_ref, send_ref, x_ref, base_ref, out_ref, in_sem, base_sem, out_sem):
    def load(p):
        lanes = pl.ds(p * NXY, NXY)
        return pltpu.make_async_copy(f_ref.at[:, :, lanes], x_ref.at[p], in_sem.at[p])

    def store(p):
        rows = pl.ds(p * CELLS, CELLS)
        return pltpu.make_async_copy(out_ref.at[:, rows, :], send_ref.at[:, rows, :], out_sem.at[p])

    base = pltpu.make_async_copy(basis_ref, base_ref, base_sem)
    load(0).start()
    base.start()
    for p in range(1, PLANES):
        load(p).start()
    lane = lax.broadcasted_iota(jnp.int32, (1, 128), 1)
    first_plane = place_ref[0] * PLANES
    total = jnp.zeros((CELLS, 128), F32)
    for p in range(PLANES):
        load(p).wait()
        x = x_ref[p].reshape(CELLS, NXY)
        for v in range(GROUP):
            out_ref[v, p * CELLS : (p + 1) * CELLS, :] = x[:, v * BLOCK : (v + 1) * BLOCK]
        store(p).start()
        if p == 0:
            base.wait()
        sums = jnp.dot(x, base_ref[...], preferred_element_type=F32)
        vz = speed(first_plane + p, NVZ)
        factor = jnp.where(lane >= 32, vz * vz, jnp.where((lane < 16) & (lane % 5 == 3), vz, 1.0))
        total = total + sums * factor
    total = jnp.transpose(total)
    total = (total[0:16, :] + total[16:32, :]) + total[32:48, :]
    column = lax.broadcasted_iota(jnp.int32, (16, CELLS), 0)
    high = total.astype(BF16).astype(F32)
    middle = (total - high).astype(BF16).astype(F32)
    low = (total - high) - middle
    parts = jnp.where(
        column < 5, high, jnp.where(column < 10, middle, jnp.where(column < 15, low, 0.0))
    )
    parts = jnp.concatenate([parts, jnp.zeros((16, 128 - CELLS), F32)], axis=1).astype(BF16)
    for v in range(GROUP):
        out_ref[v, DATA:CHUNK, :] = parts
    tail = pl.ds(DATA, CHUNK - DATA)
    last = pltpu.make_async_copy(
        out_ref.at[:, tail, :], send_ref.at[:, tail, :], out_sem.at[PLANES]
    )
    last.start()
    for p in range(PLANES):
        store(p).wait()
    last.wait()


def pack(place, f):
    basis = jnp.asarray(moment_basis())
    f, basis = (pltpu.with_memory_space_constraint(x, pltpu.HBM) for x in (f, basis))
    return pl.pallas_call(
        pack_kernel,
        out_shape=jax.ShapeDtypeStruct((GROUP, CHUNK, BLOCK), BF16),
        in_specs=[smem(), hbm(), hbm()],
        out_specs=hbm(),
        scratch_shapes=[
            pltpu.VMEM((PLANES, ROWS, COLS, NXY), BF16),
            pltpu.VMEM((NXY, 128), BF16),
            pltpu.VMEM((GROUP, CHUNK, BLOCK), BF16),
            pltpu.SemaphoreType.DMA((PLANES,)),
            pltpu.SemaphoreType.DMA(()),
            pltpu.SemaphoreType.DMA((PLANES + 1,)),
        ],
        compiler_params=pltpu.CompilerParams(vmem_limit_bytes=LIMIT),
        name="pack",
    )(place, f, basis)


def edges_kernel(core_ref, held_ref, f_ref, low_ref, high_ref, inner_ref, outer_ref):
    half = NXY // 2
    size = held_ref.shape[0]
    low_ref[0:size, :] = held_ref[...]
    high_ref[0:size, :] = held_ref[...]
    for p in range(PLANES):
        rows = slice(size + p // 2 * COLS, size + (p // 2 + 1) * COLS)
        lanes = slice(p % 2 * half, (p % 2 + 1) * half)
        high_ref[rows, lanes] = f_ref[ROWS - 1, :, p * NXY + half : (p + 1) * NXY]
        low_ref[rows, lanes] = f_ref[0, :, p * NXY : p * NXY + half]
    edge_row = lax.broadcasted_iota(jnp.int32, (16, NXY), 0)
    first = jnp.zeros((16, NXY), F32)
    last = jnp.zeros((16, NXY), F32)
    for r in range(ROWS):
        for p in range(PLANES):
            lanes = slice(p * NXY, (p + 1) * NXY)
            a = f_ref[r, 0:8, lanes].astype(F32)[0:1, :]
            b = f_ref[r, COLS - 8 : COLS, lanes].astype(F32)[7:8, :]
            first = jnp.where(edge_row == r * PLANES + p, a, first)
            last = jnp.where(edge_row == r * PLANES + p, b, last)
    core = core_ref[0]
    inner_ref[...] = jnp.where(core == 0, last, first).astype(BF16)
    outer_ref[...] = jnp.where(core == 0, first, last).astype(BF16)


def edges(core, held, f):
    row = jax.ShapeDtypeStruct((held.shape[0] + 2 * COLS, NXY), BF16)
    column = jax.ShapeDtypeStruct((16, NXY), BF16)
    return pl.pallas_call(
        edges_kernel,
        out_shape=(row, row, column, column),
        in_specs=[smem(), vmem(), vmem()],
        out_specs=(vmem(),) * 4,
        compiler_params=pltpu.CompilerParams(vmem_limit_bytes=LIMIT),
        name="edges",
    )(core, held, f)


def join_kernel(held_ref, above_ref, below_ref, across_ref, inner_ref, out_ref, sem):
    size = held_ref.shape[0]
    copies = []
    for m, ref in enumerate((held_ref, above_ref, below_ref, across_ref)):
        copies.append(
            pltpu.make_async_copy(
                ref.at[pl.ds(0, size)], out_ref.at[pl.ds(m * size, size)], sem.at[m]
            )
        )
    copies.append(
        pltpu.make_async_copy(inner_ref, out_ref.at[pl.ds(4 * size, 16)], sem.at[4])
    )
    for copy in copies:
        copy.start()
    for copy in copies:
        copy.wait()


def join(held, above, below, across, inner):
    return pl.pallas_call(
        join_kernel,
        out_shape=jax.ShapeDtypeStruct((4 * held.shape[0] + 16, NXY), BF16),
        in_specs=[hbm()] * 5,
        out_specs=hbm(),
        scratch_shapes=[pltpu.SemaphoreType.DMA((5,))],
        compiler_params=pltpu.CompilerParams(vmem_limit_bytes=LIMIT),
        name="join",
    )(held, above, below, across, inner)


def assemble_kernel(where_ref, own_ref, other_ref, out_hbm, inner_hbm, rows_ref, turned_ref, sem):
    half = NXY // 2
    edge = pltpu.make_async_copy(other_ref.at[pl.ds(half, 16)], inner_hbm, sem.at[1])
    edge.start()
    mine, y = where_ref[0], where_ref[1]
    far = jnp.where(y % 2 == 0, y + 6, y + 2)
    for side, ref in ((mine, own_ref), (jnp.bitwise_xor(mine, 1), other_ref)):
        places = [jnp.bitwise_xor(side, 2 * step) for step in range(4)]
        for m, base in enumerate((y, y + 1, y + 7, far)):
            for i in range(2):
                for j in range(4):
                    block = slice((m * 8 + i * 4 + j) * 16, (m * 8 + i * 4 + j + 1) * 16)
                    rows_ref[(base + 4 * i) % 8 * 8 + places[j]] = ref[block, :]
    turned_ref[...] = jnp.transpose(rows_ref[...].reshape(NXY, NXY))
    copy = pltpu.make_async_copy(turned_ref, out_hbm, sem.at[0])
    copy.start()
    edge.wait()
    copy.wait()


def assemble(where, own, other):
    return pl.pallas_call(
        assemble_kernel,
        out_shape=(pltpu.HBM((NXY, NXY), BF16), jax.ShapeDtypeStruct((16, NXY), BF16)),
        in_specs=[smem(), vmem(), vmem()],
        out_specs=(hbm(), hbm()),
        scratch_shapes=[
            pltpu.VMEM((NXY // 16, 16, NXY), BF16),
            pltpu.VMEM((NXY, NXY), BF16),
            pltpu.SemaphoreType.DMA((2,)),
        ],
        compiler_params=pltpu.CompilerParams(vmem_limit_bytes=LIMIT),
        name="assemble",
    )(where, own, other)


def spread_kernel(depth_ref, out_ref):
    size = NVZ * TILE
    row = lax.broadcasted_iota(jnp.int32, (size, NVZ), 0)
    col = lax.broadcasted_iota(jnp.int32, (size, NVZ), 1)
    pick = jnp.where(row // TILE == col, 1.0, 0.0).astype(BF16)
    left = jnp.dot(pick, depth_ref[...], preferred_element_type=F32).astype(BF16)
    full = lax.dot_general(left, pick, (((1,), (1,)), ((), ())), preferred_element_type=F32)
    i = lax.broadcasted_iota(jnp.int32, (size, size), 0)
    j = lax.broadcasted_iota(jnp.int32, (size, size), 1)
    out_ref[...] = jnp.where(i % TILE == j % TILE, full, 0.0).astype(BF16)


def spread(depth_weights):
    size = NVZ * TILE
    return pl.pallas_call(
        spread_kernel,
        out_shape=jax.ShapeDtypeStruct((size, size), BF16),
        in_specs=[vmem()],
        out_specs=vmem(),
        compiler_params=pltpu.CompilerParams(vmem_limit_bytes=LIMIT),
        name="spread",
    )(depth_weights)


def relax_kernel(place_ref, got_ref, mix_ref, send_ref, dev_ref):
    pieces = jnp.concatenate([got_ref[v, DATA:CHUNK, :] for v in range(GROUP)], axis=0)
    i = lax.broadcasted_iota(jnp.int32, (GROUP * 16, 128), 0) % 16
    j = lax.broadcasted_iota(jnp.int32, (GROUP * 16, 128), 1)
    pick = jnp.where((i % 5 == j) & (i < 15), 1.0, 0.0).astype(BF16)
    moments = lax.dot_general(pieces, pick, (((0,), (0,)), ((), ())), preferred_element_type=F32)
    moments = moments[:CELLS, :]
    density = moments[:, 0:1]
    ux = moments[:, 1:2] / density
    uy = moments[:, 2:3] / density
    uz = moments[:, 3:4] / density
    heat = (moments[:, 4:5] / density - (ux * ux + uy * uy + uz * uz)) / 3.0
    measure = (8.0 / NVX) * (8.0 / NVY) * (8.0 / NVZ)
    width = 2.0 * jnp.pi * heat
    scale = density * measure / (width * jnp.sqrt(width))
    inverse = -1.0 / (2.0 * heat)
    vx, vy = lane_speeds((CELLS, BLOCK), place_ref[0] * BLOCK)
    dx = vx - ux
    dy = vy - uy
    plane = scale * jnp.exp((dx * dx + dy * dy) * inverse)
    dz = speed(lax.broadcasted_iota(jnp.int32, (CELLS, 128), 1), NVZ) - uz
    depth = jnp.exp((dz * dz) * inverse)
    for w in range(NVZ):
        v, p = w // PLANES, w % PLANES
        f = got_ref[v, p * CELLS : (p + 1) * CELLS, :].astype(F32)
        deviation = (depth[:, w : w + 1] * plane - f).astype(BF16)
        for t in range(CELLS // TILE):
            dev_ref[w * TILE : (w + 1) * TILE, t * BLOCK : (t + 1) * BLOCK] = deviation[
                t * TILE : (t + 1) * TILE, :
            ]
    mixed = jnp.dot(mix_ref[...], dev_ref[...], preferred_element_type=F32).astype(BF16)
    for w in range(NVZ):
        v, p = w // PLANES, w % PLANES
        for t in range(CELLS // TILE):
            send_ref[v, p * CELLS + t * TILE : p * CELLS + (t + 1) * TILE, :] = mixed[
                w * TILE : (w + 1) * TILE, t * BLOCK : (t + 1) * BLOCK
            ]


def relax(place, got, mix):
    return pl.pallas_call(
        relax_kernel,
        out_shape=jax.ShapeDtypeStruct((GROUP, DATA, BLOCK), BF16),
        in_specs=[smem(), vmem(), vmem()],
        out_specs=vmem(),
        scratch_shapes=[pltpu.VMEM((NVZ * TILE, CELLS // TILE * BLOCK), BF16)],
        compiler_params=pltpu.CompilerParams(vmem_limit_bytes=LIMIT),
        name="relax",
    )(place, got, mix)


def advance_kernel(
    core_ref,
    f_hbm,
    back_hbm,
    weights_hbm,
    below_hbm,
    above_hbm,
    inner_hbm,
    outer_hbm,
    out_hbm,
    f_ref,
    back_ref,
    weights_ref,
    lower_ref,
    upper_ref,
    inner_ref,
    outer_ref,
    moved_ref,
    out_ref,
    sem,
    out_sem,
):
    edge = pl.ds(below_hbm.shape[0] - 2 * COLS, 2 * COLS)
    first = [
        pltpu.make_async_copy(below_hbm.at[edge], lower_ref, sem.at[0]),
        pltpu.make_async_copy(above_hbm.at[edge], upper_ref, sem.at[1]),
        pltpu.make_async_copy(inner_hbm, inner_ref, sem.at[2]),
        pltpu.make_async_copy(outer_hbm.at[pl.ds(outer_hbm.shape[0] - 16, 16)], outer_ref, sem.at[3]),
        pltpu.make_async_copy(f_hbm, f_ref, sem.at[4]),
    ]
    second = [
        pltpu.make_async_copy(back_hbm, back_ref, sem.at[5]),
        pltpu.make_async_copy(weights_hbm, weights_ref, sem.at[6]),
    ]
    for copy in first + second:
        copy.start()
    half = NXY // 2
    vx, vy = lane_speeds((COLS, NXY), 0)
    courant_across = COURANT / (4.0 - 4.0 / NVX)
    courant_along = COURANT / (4.0 - 4.0 / NVY)
    cx = courant_across * jnp.abs(vx)
    cy = courant_along * jnp.abs(vy)
    upwind = vy > 0.0
    col = lax.broadcasted_iota(jnp.int32, (COLS, NXY), 0)
    core = core_ref[0]
    for copy in first:
        copy.wait()
    inner = inner_ref[...].astype(F32)
    outer = outer_ref[...].astype(F32)
    left_edge = jnp.where(core == 0, outer, inner)
    right_edge = jnp.where(core == 0, inner, outer)
    for p in range(PLANES):
        lanes = slice(p * NXY, (p + 1) * NXY)
        first_half = slice(p * NXY, p * NXY + half)
        second_half = slice(p * NXY + half, (p + 1) * NXY)
        rows = slice(p // 2 * COLS, (p // 2 + 1) * COLS)
        packed = slice(p % 2 * half, (p % 2 + 1) * half)
        for r in range(ROWS):
            current = f_ref[r, :, lanes].astype(F32)
            above = upper_ref[rows, packed] if r == ROWS - 1 else f_ref[r + 1, :, first_half]
            below = lower_ref[rows, packed] if r == 0 else f_ref[r - 1, :, second_half]
            across = jnp.concatenate([above, below], axis=1).astype(F32)
            left = left_edge[r * PLANES + p : r * PLANES + p + 1, :]
            right = right_edge[r * PLANES + p : r * PLANES + p + 1, :]
            left = jnp.where(col == 0, left, pltpu.roll(current, 1, 0))
            right = jnp.where(col == COLS - 1, right, pltpu.roll(current, COLS - 1, 0))
            along = jnp.where(upwind, left, right)
            start = p * CELLS + r * COLS
            moved_ref[start : start + COLS, :] = current - (
                cx * (current - across) + cy * (current - along)
            )
    for copy in second:
        copy.wait()
    mixed = jnp.concatenate([back_ref[v] for v in range(GROUP)], axis=1)
    collision = jnp.dot(mixed, weights_ref[...], preferred_element_type=F32)
    stores = []
    for p in range(PLANES):
        for r in range(ROWS):
            start = p * CELLS + r * COLS
            value = moved_ref[start : start + COLS, :] + RELAX_RATE * collision[start : start + COLS, :]
            out_ref[r, :, p * NXY : (p + 1) * NXY] = value.astype(BF16)
        lanes = pl.ds(p * NXY, NXY)
        stores.append(
            pltpu.make_async_copy(
                out_ref.at[:, :, lanes], out_hbm.at[:, :, lanes], out_sem.at[p]
            )
        )
        stores[-1].start()
    for copy in stores:
        copy.wait()


def advance(core, f, back, weights, below, above, inner, outer):
    weights = pltpu.with_memory_space_constraint(weights, pltpu.HBM)
    return pl.pallas_call(
        advance_kernel,
        out_shape=jax.ShapeDtypeStruct(f.shape, BF16),
        in_specs=[smem()] + [hbm()] * 7,
        out_specs=hbm(),
        scratch_shapes=[
            pltpu.VMEM(f.shape, BF16),
            pltpu.VMEM(back.shape, BF16),
            pltpu.VMEM(weights.shape, BF16),
            pltpu.VMEM((2 * COLS, NXY), BF16),
            pltpu.VMEM((2 * COLS, NXY), BF16),
            pltpu.VMEM(inner.shape, BF16),
            pltpu.VMEM((16, NXY), BF16),
            pltpu.VMEM((DATA, NXY), F32),
            pltpu.VMEM(f.shape, BF16),
            pltpu.SemaphoreType.DMA((7,)),
            pltpu.SemaphoreType.DMA((PLANES,)),
        ],
        compiler_params=pltpu.CompilerParams(vmem_limit_bytes=LIMIT),
        name="advance",
    )(core, f, back, weights, below, above, inner, outer)


def ring(axis, step):
    count = lax.axis_size(axis)
    return [(i, (i + step) % count) for i in range(count)]


def local(distribution, plane_weights, depth_weights):
    place = lax.axis_index("vel").astype(jnp.int32).reshape(1)
    along = lax.axis_index("sy").astype(jnp.int32)
    core = jnp.bitwise_and(along, 1).reshape(1)
    where = jnp.stack([along, lax.axis_index("sx").astype(jnp.int32)])
    flip = lambda bit: [(i, i ^ bit) for i in range(8)]
    held = jnp.concatenate([plane_weights, lax.ppermute(plane_weights, "sy", flip(2))])
    held = jnp.concatenate([held, lax.ppermute(held, "sy", flip(4))])
    send, held = lax.optimization_barrier((pack(place, distribution), held))
    got = lax.all_to_all(send, "vel", 0, 0, tiled=True)
    held = jnp.concatenate([held, lax.ppermute(held, "sx", flip(4))])
    low, high, inner, outer = edges(core, held, distribution)
    above = lax.ppermute(low, "sx", ring("sx", -1))
    below = lax.ppermute(high, "sx", ring("sx", 1))
    across = lax.ppermute(held, "sx", [(i, (i + 2) % 8 if i % 2 == 0 else (i - 2) % 8) for i in range(8)])
    outer = lax.ppermute(outer, "sy", [(i, (i + 1) % 8 if i % 2 else (i - 1) % 8) for i in range(8)])
    send = relax(place, got, spread(depth_weights))
    across = pltpu.with_memory_space_constraint(across, pltpu.HBM)
    send, across = lax.optimization_barrier((send, across))
    own = join(held, above, below, across, inner)
    other = lax.ppermute(own, "sy", flip(1))
    weights, inner = assemble(where, own, other)
    back = lax.all_to_all(send, "vel", 0, 0, tiled=True)
    return advance(core, distribution, back, weights, below, above, inner, outer)


def solution(mesh):
    return jax.shard_map(
        local,
        mesh=mesh,
        in_specs=(P("sx", "sy", "vel"), P(("sx", "sy"), None), P()),
        out_specs=P("sx", "sy", "vel"),
        check_vma=False,
    )
```

```python
import jax
import jax.numpy as jnp
import numpy as np
from jax import lax
from jax.experimental import pallas as pl
from jax.experimental.pallas import tpu as pltpu
from jax.sharding import PartitionSpec as P

NVZ = 32
NVX = 32
NVY = 32
NXY = NVX * NVY
COURANT = 0.45
RELAX_RATE = 0.3
ROWS = 3
COLS = 32
CELLS = ROWS * COLS
PLANES = 4
GROUP = 8
BLOCK = NXY // GROUP
DATA = PLANES * CELLS
CHUNK = DATA + 16
TILE = 16
LIMIT = 16 << 20
F32 = jnp.float32
BF16 = jnp.bfloat16


def speed(index, count):
    return (index.astype(F32) - (count - 1) / 2.0) * (8.0 / count)


def lane_speeds(shape, offset):
    lane = lax.broadcasted_iota(jnp.int32, shape, len(shape) - 1) + offset
    return speed(lane // NVY, NVX), speed(lane % NVY, NVY)


def vmem():
    return pl.BlockSpec(memory_space=pltpu.VMEM)


def hbm():
    return pl.BlockSpec(memory_space=pltpu.HBM)


def smem():
    return pl.BlockSpec(memory_space=pltpu.SMEM)


def moment_basis():
    lane = np.arange(NXY)
    vx = (lane // NVY - (NVX - 1) / 2.0) * (8.0 / NVX)
    vy = (lane % NVY - (NVY - 1) / 2.0) * (8.0 / NVY)
    squared = (vx * vx + vy * vy).astype(np.float32)
    rough = squared.astype(BF16).astype(np.float32)
    basis = np.zeros((NXY, 128), np.float32)
    for part in range(3):
        basis[:, part * 5] = 1.0
        basis[:, part * 5 + 1] = vx
        basis[:, part * 5 + 2] = vy
        basis[:, part * 5 + 3] = 1.0
        basis[:, part * 5 + 4] = rough
        basis[:, 16 + part * 5 + 4] = squared - rough
        basis[:, 32 + part * 5 + 4] = 1.0
    return basis.astype(BF16)


def pack_kernel(place_ref, f_ref, basis_ref, send_ref, x_ref, base_ref, out_ref, in_sem, base_sem, out_sem):
    def load(p):
        lanes = pl.ds(p * NXY, NXY)
        return pltpu.make_async_copy(f_ref.at[:, :, lanes], x_ref.at[p], in_sem.at[p])

    def store(p):
        rows = pl.ds(p * CELLS, CELLS)
        return pltpu.make_async_copy(out_ref.at[:, rows, :], send_ref.at[:, rows, :], out_sem.at[p])

    base = pltpu.make_async_copy(basis_ref, base_ref, base_sem)
    load(0).start()
    base.start()
    for p in range(1, PLANES):
        load(p).start()
    lane = lax.broadcasted_iota(jnp.int32, (1, 128), 1)
    first_plane = place_ref[0] * PLANES
    total = jnp.zeros((CELLS, 128), F32)
    for p in range(PLANES):
        load(p).wait()
        x = x_ref[p].reshape(CELLS, NXY)
        for v in range(GROUP):
            out_ref[v, p * CELLS : (p + 1) * CELLS, :] = x[:, v * BLOCK : (v + 1) * BLOCK]
        store(p).start()
        if p == 0:
            base.wait()
        sums = jnp.dot(x, base_ref[...], preferred_element_type=F32)
        vz = speed(first_plane + p, NVZ)
        factor = jnp.where(lane >= 32, vz * vz, jnp.where((lane < 16) & (lane % 5 == 3), vz, 1.0))
        total = total + sums * factor
    total = jnp.transpose(total)
    total = (total[0:16, :] + total[16:32, :]) + total[32:48, :]
    column = lax.broadcasted_iota(jnp.int32, (16, CELLS), 0)
    high = total.astype(BF16).astype(F32)
    middle = (total - high).astype(BF16).astype(F32)
    low = (total - high) - middle
    parts = jnp.where(
        column < 5, high, jnp.where(column < 10, middle, jnp.where(column < 15, low, 0.0))
    )
    parts = jnp.concatenate([parts, jnp.zeros((16, 128 - CELLS), F32)], axis=1).astype(BF16)
    for v in range(GROUP):
        out_ref[v, DATA:CHUNK, :] = parts
    tail = pl.ds(DATA, CHUNK - DATA)
    last = pltpu.make_async_copy(
        out_ref.at[:, tail, :], send_ref.at[:, tail, :], out_sem.at[PLANES]
    )
    last.start()
    for p in range(PLANES):
        store(p).wait()
    last.wait()


def pack(place, f):
    basis = jnp.asarray(moment_basis())
    f, basis = (pltpu.with_memory_space_constraint(x, pltpu.HBM) for x in (f, basis))
    return pl.pallas_call(
        pack_kernel,
        out_shape=jax.ShapeDtypeStruct((GROUP, CHUNK, BLOCK), BF16),
        in_specs=[smem(), hbm(), hbm()],
        out_specs=hbm(),
        scratch_shapes=[
            pltpu.VMEM((PLANES, ROWS, COLS, NXY), BF16),
            pltpu.VMEM((NXY, 128), BF16),
            pltpu.VMEM((GROUP, CHUNK, BLOCK), BF16),
            pltpu.SemaphoreType.DMA((PLANES,)),
            pltpu.SemaphoreType.DMA(()),
            pltpu.SemaphoreType.DMA((PLANES + 1,)),
        ],
        compiler_params=pltpu.CompilerParams(vmem_limit_bytes=LIMIT),
        name="pack",
    )(place, f, basis)


def edges_kernel(core_ref, held_ref, f_ref, low_ref, high_ref, inner_ref, outer_ref):
    half = NXY // 2
    size = held_ref.shape[0]
    low_ref[0:size, :] = held_ref[...]
    high_ref[0:size, :] = held_ref[...]
    for p in range(PLANES):
        rows = slice(size + p // 2 * COLS, size + (p // 2 + 1) * COLS)
        lanes = slice(p % 2 * half, (p % 2 + 1) * half)
        high_ref[rows, lanes] = f_ref[ROWS - 1, :, p * NXY + half : (p + 1) * NXY]
        low_ref[rows, lanes] = f_ref[0, :, p * NXY : p * NXY + half]
    edge_row = lax.broadcasted_iota(jnp.int32, (16, NXY), 0)
    first = jnp.zeros((16, NXY), F32)
    last = jnp.zeros((16, NXY), F32)
    for r in range(ROWS):
        for p in range(PLANES):
            lanes = slice(p * NXY, (p + 1) * NXY)
            a = f_ref[r, 0:8, lanes].astype(F32)[0:1, :]
            b = f_ref[r, COLS - 8 : COLS, lanes].astype(F32)[7:8, :]
            first = jnp.where(edge_row == r * PLANES + p, a, first)
            last = jnp.where(edge_row == r * PLANES + p, b, last)
    core = core_ref[0]
    inner_ref[...] = jnp.where(core == 0, last, first).astype(BF16)
    outer_ref[...] = jnp.where(core == 0, first, last).astype(BF16)


def edges(core, held, f):
    row = jax.ShapeDtypeStruct((held.shape[0] + 2 * COLS, NXY), BF16)
    column = jax.ShapeDtypeStruct((16, NXY), BF16)
    return pl.pallas_call(
        edges_kernel,
        out_shape=(row, row, column, column),
        in_specs=[smem(), vmem(), vmem()],
        out_specs=(vmem(),) * 4,
        compiler_params=pltpu.CompilerParams(vmem_limit_bytes=LIMIT),
        name="edges",
    )(core, held, f)


def join_kernel(held_ref, above_ref, below_ref, across_ref, inner_ref, out_ref, sem):
    size = held_ref.shape[0]
    copies = []
    for m, ref in enumerate((held_ref, above_ref, below_ref, across_ref)):
        copies.append(
            pltpu.make_async_copy(
                ref.at[pl.ds(0, size)], out_ref.at[pl.ds(m * size, size)], sem.at[m]
            )
        )
    copies.append(
        pltpu.make_async_copy(inner_ref, out_ref.at[pl.ds(4 * size, 16)], sem.at[4])
    )
    for copy in copies:
        copy.start()
    for copy in copies:
        copy.wait()


def join(held, above, below, across, inner):
    return pl.pallas_call(
        join_kernel,
        out_shape=jax.ShapeDtypeStruct((4 * held.shape[0] + 16, NXY), BF16),
        in_specs=[hbm()] * 5,
        out_specs=hbm(),
        scratch_shapes=[pltpu.SemaphoreType.DMA((5,))],
        compiler_params=pltpu.CompilerParams(vmem_limit_bytes=LIMIT),
        name="join",
    )(held, above, below, across, inner)


def assemble_kernel(where_ref, own_ref, other_ref, out_hbm, inner_hbm, rows_ref, turned_ref, sem):
    half = NXY // 2
    edge = pltpu.make_async_copy(other_ref.at[pl.ds(half, 16)], inner_hbm, sem.at[1])
    edge.start()
    mine, y = where_ref[0], where_ref[1]
    far = jnp.where(y % 2 == 0, y + 6, y + 2)
    for side, ref in ((mine, own_ref), (jnp.bitwise_xor(mine, 1), other_ref)):
        places = [jnp.bitwise_xor(side, 2 * step) for step in range(4)]
        for m, base in enumerate((y, y + 1, y + 7, far)):
            for i in range(2):
                for j in range(4):
                    block = slice((m * 8 + i * 4 + j) * 16, (m * 8 + i * 4 + j + 1) * 16)
                    rows_ref[(base + 4 * i) % 8 * 8 + places[j]] = ref[block, :]
    turned_ref[...] = jnp.transpose(rows_ref[...].reshape(NXY, NXY))
    copy = pltpu.make_async_copy(turned_ref, out_hbm, sem.at[0])
    copy.start()
    edge.wait()
    copy.wait()


def assemble(where, own, other):
    return pl.pallas_call(
        assemble_kernel,
        out_shape=(pltpu.HBM((NXY, NXY), BF16), jax.ShapeDtypeStruct((16, NXY), BF16)),
        in_specs=[smem(), vmem(), vmem()],
        out_specs=(hbm(), hbm()),
        scratch_shapes=[
            pltpu.VMEM((NXY // 16, 16, NXY), BF16),
            pltpu.VMEM((NXY, NXY), BF16),
            pltpu.SemaphoreType.DMA((2,)),
        ],
        compiler_params=pltpu.CompilerParams(vmem_limit_bytes=LIMIT),
        name="assemble",
    )(where, own, other)


def spread_kernel(depth_ref, out_ref):
    size = NVZ * TILE
    row = lax.broadcasted_iota(jnp.int32, (size, NVZ), 0)
    col = lax.broadcasted_iota(jnp.int32, (size, NVZ), 1)
    pick = jnp.where(row // TILE == col, 1.0, 0.0).astype(BF16)
    left = jnp.dot(pick, depth_ref[...], preferred_element_type=F32).astype(BF16)
    full = lax.dot_general(left, pick, (((1,), (1,)), ((), ())), preferred_element_type=F32)
    i = lax.broadcasted_iota(jnp.int32, (size, size), 0)
    j = lax.broadcasted_iota(jnp.int32, (size, size), 1)
    out_ref[...] = jnp.where(i % TILE == j % TILE, full, 0.0).astype(BF16)


def spread(depth_weights):
    size = NVZ * TILE
    return pl.pallas_call(
        spread_kernel,
        out_shape=jax.ShapeDtypeStruct((size, size), BF16),
        in_specs=[vmem()],
        out_specs=vmem(),
        compiler_params=pltpu.CompilerParams(vmem_limit_bytes=LIMIT),
        name="spread",
    )(depth_weights)


def relax_kernel(place_ref, got_ref, mix_ref, send_ref, dev_ref):
    pieces = jnp.concatenate([got_ref[v, DATA:CHUNK, :] for v in range(GROUP)], axis=0)
    i = lax.broadcasted_iota(jnp.int32, (GROUP * 16, 128), 0) % 16
    j = lax.broadcasted_iota(jnp.int32, (GROUP * 16, 128), 1)
    pick = jnp.where((i % 5 == j) & (i < 15), 1.0, 0.0).astype(BF16)
    moments = lax.dot_general(pieces, pick, (((0,), (0,)), ((), ())), preferred_element_type=F32)
    moments = moments[:CELLS, :]
    density = moments[:, 0:1]
    ux = moments[:, 1:2] / density
    uy = moments[:, 2:3] / density
    uz = moments[:, 3:4] / density
    heat = (moments[:, 4:5] / density - (ux * ux + uy * uy + uz * uz)) / 3.0
    measure = (8.0 / NVX) * (8.0 / NVY) * (8.0 / NVZ)
    width = 2.0 * jnp.pi * heat
    scale = density * measure / (width * jnp.sqrt(width))
    inverse = -1.0 / (2.0 * heat)
    vx, vy = lane_speeds((CELLS, BLOCK), place_ref[0] * BLOCK)
    dx = vx - ux
    dy = vy - uy
    plane = scale * jnp.exp((dx * dx + dy * dy) * inverse)
    dz = speed(lax.broadcasted_iota(jnp.int32, (CELLS, 128), 1), NVZ) - uz
    depth = jnp.exp((dz * dz) * inverse)
    for w in range(NVZ):
        v, p = w // PLANES, w % PLANES
        f = got_ref[v, p * CELLS : (p + 1) * CELLS, :].astype(F32)
        deviation = (depth[:, w : w + 1] * plane - f).astype(BF16)
        for t in range(CELLS // TILE):
            dev_ref[w * TILE : (w + 1) * TILE, t * BLOCK : (t + 1) * BLOCK] = deviation[
                t * TILE : (t + 1) * TILE, :
            ]
    mixed = jnp.dot(mix_ref[...], dev_ref[...], preferred_element_type=F32).astype(BF16)
    for w in range(NVZ):
        v, p = w // PLANES, w % PLANES
        for t in range(CELLS // TILE):
            send_ref[v, p * CELLS + t * TILE : p * CELLS + (t + 1) * TILE, :] = mixed[
                w * TILE : (w + 1) * TILE, t * BLOCK : (t + 1) * BLOCK
            ]


def relax(place, got, mix):
    return pl.pallas_call(
        relax_kernel,
        out_shape=jax.ShapeDtypeStruct((GROUP, DATA, BLOCK), BF16),
        in_specs=[smem(), vmem(), vmem()],
        out_specs=vmem(),
        scratch_shapes=[pltpu.VMEM((NVZ * TILE, CELLS // TILE * BLOCK), BF16)],
        compiler_params=pltpu.CompilerParams(vmem_limit_bytes=LIMIT),
        name="relax",
    )(place, got, mix)


def advance_kernel(
    core_ref,
    f_hbm,
    back_hbm,
    weights_hbm,
    below_hbm,
    above_hbm,
    inner_hbm,
    outer_hbm,
    out_hbm,
    f_ref,
    back_ref,
    weights_ref,
    lower_ref,
    upper_ref,
    inner_ref,
    outer_ref,
    moved_ref,
    out_ref,
    sem,
    out_sem,
):
    edge = pl.ds(below_hbm.shape[0] - 2 * COLS, 2 * COLS)
    first = [
        pltpu.make_async_copy(below_hbm.at[edge], lower_ref, sem.at[0]),
        pltpu.make_async_copy(above_hbm.at[edge], upper_ref, sem.at[1]),
        pltpu.make_async_copy(inner_hbm, inner_ref, sem.at[2]),
        pltpu.make_async_copy(outer_hbm.at[pl.ds(outer_hbm.shape[0] - 16, 16)], outer_ref, sem.at[3]),
        pltpu.make_async_copy(f_hbm, f_ref, sem.at[4]),
    ]
    second = [
        pltpu.make_async_copy(back_hbm, back_ref, sem.at[5]),
        pltpu.make_async_copy(weights_hbm, weights_ref, sem.at[6]),
    ]
    for copy in first + second:
        copy.start()
    half = NXY // 2
    vx, vy = lane_speeds((COLS, NXY), 0)
    courant_across = COURANT / (4.0 - 4.0 / NVX)
    courant_along = COURANT / (4.0 - 4.0 / NVY)
    cx = courant_across * jnp.abs(vx)
    cy = courant_along * jnp.abs(vy)
    upwind = vy > 0.0
    col = lax.broadcasted_iota(jnp.int32, (COLS, NXY), 0)
    core = core_ref[0]
    for copy in first:
        copy.wait()
    inner = inner_ref[...].astype(F32)
    outer = outer_ref[...].astype(F32)
    left_edge = jnp.where(core == 0, outer, inner)
    right_edge = jnp.where(core == 0, inner, outer)
    for p in range(PLANES):
        lanes = slice(p * NXY, (p + 1) * NXY)
        first_half = slice(p * NXY, p * NXY + half)
        second_half = slice(p * NXY + half, (p + 1) * NXY)
        rows = slice(p // 2 * COLS, (p // 2 + 1) * COLS)
        packed = slice(p % 2 * half, (p % 2 + 1) * half)
        for r in range(ROWS):
            current = f_ref[r, :, lanes].astype(F32)
            above = upper_ref[rows, packed] if r == ROWS - 1 else f_ref[r + 1, :, first_half]
            below = lower_ref[rows, packed] if r == 0 else f_ref[r - 1, :, second_half]
            across = jnp.concatenate([above, below], axis=1).astype(F32)
            left = left_edge[r * PLANES + p : r * PLANES + p + 1, :]
            right = right_edge[r * PLANES + p : r * PLANES + p + 1, :]
            left = jnp.where(col == 0, left, pltpu.roll(current, 1, 0))
            right = jnp.where(col == COLS - 1, right, pltpu.roll(current, COLS - 1, 0))
            along = jnp.where(upwind, left, right)
            start = p * CELLS + r * COLS
            moved_ref[start : start + COLS, :] = current - (
                cx * (current - across) + cy * (current - along)
            )
    for copy in second:
        copy.wait()
    mixed = jnp.concatenate([back_ref[v] for v in range(GROUP)], axis=1)
    collision = jnp.dot(mixed, weights_ref[...], preferred_element_type=F32)
    stores = []
    for p in range(PLANES):
        for r in range(ROWS):
            start = p * CELLS + r * COLS
            value = moved_ref[start : start + COLS, :] + RELAX_RATE * collision[start : start + COLS, :]
            out_ref[r, :, p * NXY : (p + 1) * NXY] = value.astype(BF16)
        lanes = pl.ds(p * NXY, NXY)
        stores.append(
            pltpu.make_async_copy(
                out_ref.at[:, :, lanes], out_hbm.at[:, :, lanes], out_sem.at[p]
            )
        )
        stores[-1].start()
    for copy in stores:
        copy.wait()


def advance(core, f, back, weights, below, above, inner, outer):
    weights = pltpu.with_memory_space_constraint(weights, pltpu.HBM)
    return pl.pallas_call(
        advance_kernel,
        out_shape=jax.ShapeDtypeStruct(f.shape, BF16),
        in_specs=[smem()] + [hbm()] * 7,
        out_specs=hbm(),
        scratch_shapes=[
            pltpu.VMEM(f.shape, BF16),
            pltpu.VMEM(back.shape, BF16),
            pltpu.VMEM(weights.shape, BF16),
            pltpu.VMEM((2 * COLS, NXY), BF16),
            pltpu.VMEM((2 * COLS, NXY), BF16),
            pltpu.VMEM(inner.shape, BF16),
            pltpu.VMEM((16, NXY), BF16),
            pltpu.VMEM((DATA, NXY), F32),
            pltpu.VMEM(f.shape, BF16),
            pltpu.SemaphoreType.DMA((7,)),
            pltpu.SemaphoreType.DMA((PLANES,)),
        ],
        compiler_params=pltpu.CompilerParams(vmem_limit_bytes=LIMIT),
        name="advance",
    )(core, f, back, weights, below, above, inner, outer)


def ring(axis, step):
    count = lax.axis_size(axis)
    return [(i, (i + step) % count) for i in range(count)]


def local(distribution, plane_weights, depth_weights):
    place = lax.axis_index("vel").astype(jnp.int32).reshape(1)
    along = lax.axis_index("sy").astype(jnp.int32)
    core = jnp.bitwise_and(along, 1).reshape(1)
    where = jnp.stack([along, lax.axis_index("sx").astype(jnp.int32)])
    flip = lambda bit: [(i, i ^ bit) for i in range(8)]
    held = jnp.concatenate([plane_weights, lax.ppermute(plane_weights, "sy", flip(2))])
    held = jnp.concatenate([held, lax.ppermute(held, "sy", flip(4))])
    send, held = lax.optimization_barrier((pack(place, distribution), held))
    got = lax.all_to_all(send, "vel", 0, 0, tiled=True)
    held = jnp.concatenate([held, lax.ppermute(held, "sx", flip(4))])
    low, high, inner, outer = edges(core, held, distribution)
    above = lax.ppermute(low, "sx", ring("sx", -1))
    below = lax.ppermute(high, "sx", ring("sx", 1))
    across = lax.ppermute(held, "sx", [(i, (i + 2) % 8 if i % 2 == 0 else (i - 2) % 8) for i in range(8)])
    outer = lax.ppermute(outer, "sy", [(i, (i + 1) % 8 if i % 2 else (i - 1) % 8) for i in range(8)])
    send = relax(place, got, spread(depth_weights))
    own = join(held, above, below, across, inner)
    other = lax.ppermute(own, "sy", flip(1))
    weights, inner = assemble(where, own, other)
    back = lax.all_to_all(send, "vel", 0, 0, tiled=True)
    return advance(core, distribution, back, weights, below, above, inner, outer)


def solution(mesh):
    return jax.shard_map(
        local,
        mesh=mesh,
        in_specs=(P("sx", "sy", "vel"), P(("sx", "sy"), None), P()),
        out_specs=P("sx", "sy", "vel"),
        check_vma=False,
    )
```

```python
import jax
import jax.numpy as jnp
import numpy as np
from jax import lax
from jax.experimental import pallas as pl
from jax.experimental.pallas import tpu as pltpu
from jax.sharding import PartitionSpec as P

NVZ = 32
NVX = 32
NVY = 32
NXY = NVX * NVY
COURANT = 0.45
RELAX_RATE = 0.3
ROWS = 3
COLS = 32
CELLS = ROWS * COLS
PLANES = 4
GROUP = 8
BLOCK = NXY // GROUP
DATA = PLANES * CELLS
CHUNK = DATA + 16
TILE = 16
LIMIT = 16 << 20
F32 = jnp.float32
BF16 = jnp.bfloat16


def speed(index, count):
    return (index.astype(F32) - (count - 1) / 2.0) * (8.0 / count)


def lane_speeds(shape, offset):
    lane = lax.broadcasted_iota(jnp.int32, shape, len(shape) - 1) + offset
    return speed(lane // NVY, NVX), speed(lane % NVY, NVY)


def vmem():
    return pl.BlockSpec(memory_space=pltpu.VMEM)


def hbm():
    return pl.BlockSpec(memory_space=pltpu.HBM)


def smem():
    return pl.BlockSpec(memory_space=pltpu.SMEM)


def moment_basis():
    lane = np.arange(NXY)
    vx = (lane // NVY - (NVX - 1) / 2.0) * (8.0 / NVX)
    vy = (lane % NVY - (NVY - 1) / 2.0) * (8.0 / NVY)
    squared = (vx * vx + vy * vy).astype(np.float32)
    rough = squared.astype(BF16).astype(np.float32)
    basis = np.zeros((NXY, 128), np.float32)
    for part in range(3):
        basis[:, part * 5] = 1.0
        basis[:, part * 5 + 1] = vx
        basis[:, part * 5 + 2] = vy
        basis[:, part * 5 + 3] = 1.0
        basis[:, part * 5 + 4] = rough
        basis[:, 16 + part * 5 + 4] = squared - rough
        basis[:, 32 + part * 5 + 4] = 1.0
    return basis.astype(BF16)


def pack_kernel(place_ref, f_ref, basis_ref, send_ref, x_ref, base_ref, out_ref, in_sem, base_sem, out_sem):
    def load(p):
        lanes = pl.ds(p * NXY, NXY)
        return pltpu.make_async_copy(f_ref.at[:, :, lanes], x_ref.at[p], in_sem.at[p])

    def store(p):
        rows = pl.ds(p * CELLS, CELLS)
        return pltpu.make_async_copy(out_ref.at[:, rows, :], send_ref.at[:, rows, :], out_sem.at[p])

    base = pltpu.make_async_copy(basis_ref, base_ref, base_sem)
    load(0).start()
    base.start()
    for p in range(1, PLANES):
        load(p).start()
    lane = lax.broadcasted_iota(jnp.int32, (1, 128), 1)
    first_plane = place_ref[0] * PLANES
    total = jnp.zeros((CELLS, 128), F32)
    for p in range(PLANES):
        load(p).wait()
        x = x_ref[p].reshape(CELLS, NXY)
        for v in range(GROUP):
            out_ref[v, p * CELLS : (p + 1) * CELLS, :] = x[:, v * BLOCK : (v + 1) * BLOCK]
        store(p).start()
        if p == 0:
            base.wait()
        sums = jnp.dot(x, base_ref[...], preferred_element_type=F32)
        vz = speed(first_plane + p, NVZ)
        factor = jnp.where(lane >= 32, vz * vz, jnp.where((lane < 16) & (lane % 5 == 3), vz, 1.0))
        total = total + sums * factor
    total = jnp.transpose(total)
    total = (total[0:16, :] + total[16:32, :]) + total[32:48, :]
    column = lax.broadcasted_iota(jnp.int32, (16, CELLS), 0)
    high = total.astype(BF16).astype(F32)
    middle = (total - high).astype(BF16).astype(F32)
    low = (total - high) - middle
    parts = jnp.where(
        column < 5, high, jnp.where(column < 10, middle, jnp.where(column < 15, low, 0.0))
    )
    parts = jnp.concatenate([parts, jnp.zeros((16, 128 - CELLS), F32)], axis=1).astype(BF16)
    for v in range(GROUP):
        out_ref[v, DATA:CHUNK, :] = parts
    tail = pl.ds(DATA, CHUNK - DATA)
    last = pltpu.make_async_copy(
        out_ref.at[:, tail, :], send_ref.at[:, tail, :], out_sem.at[PLANES]
    )
    last.start()
    for p in range(PLANES):
        store(p).wait()
    last.wait()


def pack(place, f):
    basis = jnp.asarray(moment_basis())
    f, basis = (pltpu.with_memory_space_constraint(x, pltpu.HBM) for x in (f, basis))
    return pl.pallas_call(
        pack_kernel,
        out_shape=jax.ShapeDtypeStruct((GROUP, CHUNK, BLOCK), BF16),
        in_specs=[smem(), hbm(), hbm()],
        out_specs=hbm(),
        scratch_shapes=[
            pltpu.VMEM((PLANES, ROWS, COLS, NXY), BF16),
            pltpu.VMEM((NXY, 128), BF16),
            pltpu.VMEM((GROUP, CHUNK, BLOCK), BF16),
            pltpu.SemaphoreType.DMA((PLANES,)),
            pltpu.SemaphoreType.DMA(()),
            pltpu.SemaphoreType.DMA((PLANES + 1,)),
        ],
        compiler_params=pltpu.CompilerParams(vmem_limit_bytes=LIMIT),
        name="pack",
    )(place, f, basis)


def edges_kernel(core_ref, held_ref, f_ref, low_ref, high_ref, inner_ref, outer_ref):
    half = NXY // 2
    size = held_ref.shape[0]
    low_ref[0:size, :] = held_ref[...]
    high_ref[0:size, :] = held_ref[...]
    for p in range(PLANES):
        rows = slice(size + p // 2 * COLS, size + (p // 2 + 1) * COLS)
        lanes = slice(p % 2 * half, (p % 2 + 1) * half)
        high_ref[rows, lanes] = f_ref[ROWS - 1, :, p * NXY + half : (p + 1) * NXY]
        low_ref[rows, lanes] = f_ref[0, :, p * NXY : p * NXY + half]
    edge_row = lax.broadcasted_iota(jnp.int32, (16, NXY), 0)
    first = jnp.zeros((16, NXY), F32)
    last = jnp.zeros((16, NXY), F32)
    for r in range(ROWS):
        for p in range(PLANES):
            lanes = slice(p * NXY, (p + 1) * NXY)
            a = f_ref[r, 0:8, lanes].astype(F32)[0:1, :]
            b = f_ref[r, COLS - 8 : COLS, lanes].astype(F32)[7:8, :]
            first = jnp.where(edge_row == r * PLANES + p, a, first)
            last = jnp.where(edge_row == r * PLANES + p, b, last)
    core = core_ref[0]
    inner_ref[...] = jnp.where(core == 0, last, first).astype(BF16)
    outer_ref[...] = jnp.where(core == 0, first, last).astype(BF16)


def edges(core, held, f):
    row = jax.ShapeDtypeStruct((held.shape[0] + 2 * COLS, NXY), BF16)
    column = jax.ShapeDtypeStruct((16, NXY), BF16)
    return pl.pallas_call(
        edges_kernel,
        out_shape=(row, row, column, column),
        in_specs=[smem(), vmem(), vmem()],
        out_specs=(vmem(),) * 4,
        compiler_params=pltpu.CompilerParams(vmem_limit_bytes=LIMIT),
        name="edges",
    )(core, held, f)


def join_kernel(held_ref, above_ref, below_ref, across_ref, inner_ref, out_ref, sem):
    size = held_ref.shape[0]
    copies = []
    for m, ref in enumerate((held_ref, above_ref, below_ref, across_ref)):
        copies.append(
            pltpu.make_async_copy(
                ref.at[pl.ds(0, size)], out_ref.at[pl.ds(m * size, size)], sem.at[m]
            )
        )
    copies.append(
        pltpu.make_async_copy(inner_ref, out_ref.at[pl.ds(4 * size, 16)], sem.at[4])
    )
    for copy in copies:
        copy.start()
    for copy in copies:
        copy.wait()


def join(held, above, below, across, inner):
    return pl.pallas_call(
        join_kernel,
        out_shape=pltpu.HBM((4 * held.shape[0] + 16, NXY), BF16),
        in_specs=[hbm()] * 5,
        out_specs=hbm(),
        scratch_shapes=[pltpu.SemaphoreType.DMA((5,))],
        compiler_params=pltpu.CompilerParams(vmem_limit_bytes=LIMIT),
        name="join",
    )(held, above, below, across, inner)


def spread_kernel(depth_ref, out_ref):
    size = NVZ * TILE
    row = lax.broadcasted_iota(jnp.int32, (size, NVZ), 0)
    col = lax.broadcasted_iota(jnp.int32, (size, NVZ), 1)
    pick = jnp.where(row // TILE == col, 1.0, 0.0).astype(BF16)
    left = jnp.dot(pick, depth_ref[...], preferred_element_type=F32).astype(BF16)
    full = lax.dot_general(left, pick, (((1,), (1,)), ((), ())), preferred_element_type=F32)
    i = lax.broadcasted_iota(jnp.int32, (size, size), 0)
    j = lax.broadcasted_iota(jnp.int32, (size, size), 1)
    out_ref[...] = jnp.where(i % TILE == j % TILE, full, 0.0).astype(BF16)


def spread(depth_weights):
    size = NVZ * TILE
    return pl.pallas_call(
        spread_kernel,
        out_shape=jax.ShapeDtypeStruct((size, size), BF16),
        in_specs=[vmem()],
        out_specs=vmem(),
        compiler_params=pltpu.CompilerParams(vmem_limit_bytes=LIMIT),
        name="spread",
    )(depth_weights)


def relax_kernel(place_ref, got_ref, mix_ref, send_ref, dev_ref):
    pieces = jnp.concatenate([got_ref[v, DATA:CHUNK, :] for v in range(GROUP)], axis=0)
    i = lax.broadcasted_iota(jnp.int32, (GROUP * 16, 128), 0) % 16
    j = lax.broadcasted_iota(jnp.int32, (GROUP * 16, 128), 1)
    pick = jnp.where((i % 5 == j) & (i < 15), 1.0, 0.0).astype(BF16)
    moments = lax.dot_general(pieces, pick, (((0,), (0,)), ((), ())), preferred_element_type=F32)
    moments = moments[:CELLS, :]
    density = moments[:, 0:1]
    ux = moments[:, 1:2] / density
    uy = moments[:, 2:3] / density
    uz = moments[:, 3:4] / density
    heat = (moments[:, 4:5] / density - (ux * ux + uy * uy + uz * uz)) / 3.0
    measure = (8.0 / NVX) * (8.0 / NVY) * (8.0 / NVZ)
    width = 2.0 * jnp.pi * heat
    scale = density * measure / (width * jnp.sqrt(width))
    inverse = -1.0 / (2.0 * heat)
    vx, vy = lane_speeds((CELLS, BLOCK), place_ref[0] * BLOCK)
    dx = vx - ux
    dy = vy - uy
    plane = scale * jnp.exp((dx * dx + dy * dy) * inverse)
    dz = speed(lax.broadcasted_iota(jnp.int32, (CELLS, 128), 1), NVZ) - uz
    depth = jnp.exp((dz * dz) * inverse)
    for w in range(NVZ):
        v, p = w // PLANES, w % PLANES
        f = got_ref[v, p * CELLS : (p + 1) * CELLS, :].astype(F32)
        deviation = (depth[:, w : w + 1] * plane - f).astype(BF16)
        for t in range(CELLS // TILE):
            dev_ref[w * TILE : (w + 1) * TILE, t * BLOCK : (t + 1) * BLOCK] = deviation[
                t * TILE : (t + 1) * TILE, :
            ]
    mixed = jnp.dot(mix_ref[...], dev_ref[...], preferred_element_type=F32).astype(BF16)
    for w in range(NVZ):
        v, p = w // PLANES, w % PLANES
        for t in range(CELLS // TILE):
            send_ref[v, p * CELLS + t * TILE : p * CELLS + (t + 1) * TILE, :] = mixed[
                w * TILE : (w + 1) * TILE, t * BLOCK : (t + 1) * BLOCK
            ]


def relax(place, got, mix):
    return pl.pallas_call(
        relax_kernel,
        out_shape=jax.ShapeDtypeStruct((GROUP, DATA, BLOCK), BF16),
        in_specs=[smem(), vmem(), vmem()],
        out_specs=vmem(),
        scratch_shapes=[pltpu.VMEM((NVZ * TILE, CELLS // TILE * BLOCK), BF16)],
        compiler_params=pltpu.CompilerParams(vmem_limit_bytes=LIMIT),
        name="relax",
    )(place, got, mix)


def advance_kernel(
    where_ref,
    f_hbm,
    back_hbm,
    own_hbm,
    other_hbm,
    below_hbm,
    above_hbm,
    outer_hbm,
    out_hbm,
    f_ref,
    back_ref,
    weights_ref,
    lower_ref,
    upper_ref,
    inner_ref,
    outer_ref,
    moved_ref,
    out_ref,
    sem,
    out_sem,
):
    edge = pl.ds(below_hbm.shape[0] - 2 * COLS, 2 * COLS)
    first = [
        pltpu.make_async_copy(below_hbm.at[edge], lower_ref, sem.at[0]),
        pltpu.make_async_copy(above_hbm.at[edge], upper_ref, sem.at[1]),
        pltpu.make_async_copy(other_hbm.at[pl.ds(NXY // 2, 16)], inner_ref, sem.at[2]),
        pltpu.make_async_copy(outer_hbm.at[pl.ds(outer_hbm.shape[0] - 16, 16)], outer_ref, sem.at[3]),
        pltpu.make_async_copy(f_hbm, f_ref, sem.at[4]),
    ]
    second = [pltpu.make_async_copy(back_hbm, back_ref, sem.at[5])]
    mine, y = where_ref[0], where_ref[1]
    far = jnp.where(y % 2 == 0, y + 6, y + 2)
    for side, ref in ((mine, own_hbm), (jnp.bitwise_xor(mine, 1), other_hbm)):
        for m, base in enumerate((y, y + 1, y + 7, far)):
            for i in range(2):
                row = (base + 4 * i) % 8 * 8
                for j in range(4):
                    block = pl.ds((m * 8 + i * 4 + j) * 16, 16)
                    place = row + jnp.bitwise_xor(side, 2 * j)
                    second.append(
                        pltpu.make_async_copy(
                            ref.at[block], weights_ref.at[place], sem.at[5 + len(second)]
                        )
                    )
    for copy in first + second:
        copy.start()
    half = NXY // 2
    vx, vy = lane_speeds((COLS, NXY), 0)
    courant_across = COURANT / (4.0 - 4.0 / NVX)
    courant_along = COURANT / (4.0 - 4.0 / NVY)
    cx = courant_across * jnp.abs(vx)
    cy = courant_along * jnp.abs(vy)
    upwind = vy > 0.0
    col = lax.broadcasted_iota(jnp.int32, (COLS, NXY), 0)
    core = mine % 2
    for copy in first:
        copy.wait()
    inner = inner_ref[...].astype(F32)
    outer = outer_ref[...].astype(F32)
    left_edge = jnp.where(core == 0, outer, inner)
    right_edge = jnp.where(core == 0, inner, outer)
    for p in range(PLANES):
        lanes = slice(p * NXY, (p + 1) * NXY)
        first_half = slice(p * NXY, p * NXY + half)
        second_half = slice(p * NXY + half, (p + 1) * NXY)
        rows = slice(p // 2 * COLS, (p // 2 + 1) * COLS)
        packed = slice(p % 2 * half, (p % 2 + 1) * half)
        for r in range(ROWS):
            current = f_ref[r, :, lanes].astype(F32)
            above = upper_ref[rows, packed] if r == ROWS - 1 else f_ref[r + 1, :, first_half]
            below = lower_ref[rows, packed] if r == 0 else f_ref[r - 1, :, second_half]
            across = jnp.concatenate([above, below], axis=1).astype(F32)
            left = left_edge[r * PLANES + p : r * PLANES + p + 1, :]
            right = right_edge[r * PLANES + p : r * PLANES + p + 1, :]
            left = jnp.where(col == 0, left, pltpu.roll(current, 1, 0))
            right = jnp.where(col == COLS - 1, right, pltpu.roll(current, COLS - 1, 0))
            along = jnp.where(upwind, left, right)
            start = p * CELLS + r * COLS
            moved_ref[start : start + COLS, :] = current - (
                cx * (current - across) + cy * (current - along)
            )
    for copy in second:
        copy.wait()
    mixed = jnp.concatenate([back_ref[v] for v in range(GROUP)], axis=1)
    weights = weights_ref[...].reshape(NXY, NXY)
    collision = lax.dot_general(
        mixed, weights, (((1,), (1,)), ((), ())), preferred_element_type=F32
    )
    stores = []
    for p in range(PLANES):
        for r in range(ROWS):
            start = p * CELLS + r * COLS
            value = moved_ref[start : start + COLS, :] + RELAX_RATE * collision[start : start + COLS, :]
            out_ref[r, :, p * NXY : (p + 1) * NXY] = value.astype(BF16)
        lanes = pl.ds(p * NXY, NXY)
        stores.append(
            pltpu.make_async_copy(
                out_ref.at[:, :, lanes], out_hbm.at[:, :, lanes], out_sem.at[p]
            )
        )
        stores[-1].start()
    for copy in stores:
        copy.wait()


def advance(where, f, back, own, other, below, above, outer):
    own, other = (pltpu.with_memory_space_constraint(x, pltpu.HBM) for x in (own, other))
    return pl.pallas_call(
        advance_kernel,
        out_shape=jax.ShapeDtypeStruct(f.shape, BF16),
        in_specs=[smem()] + [hbm()] * 7,
        out_specs=hbm(),
        scratch_shapes=[
            pltpu.VMEM(f.shape, BF16),
            pltpu.VMEM(back.shape, BF16),
            pltpu.VMEM((NXY // 16, 16, NXY), BF16),
            pltpu.VMEM((2 * COLS, NXY), BF16),
            pltpu.VMEM((2 * COLS, NXY), BF16),
            pltpu.VMEM((16, NXY), BF16),
            pltpu.VMEM((16, NXY), BF16),
            pltpu.VMEM((DATA, NXY), F32),
            pltpu.VMEM(f.shape, BF16),
            pltpu.SemaphoreType.DMA((6 + NXY // 16,)),
            pltpu.SemaphoreType.DMA((PLANES,)),
        ],
        compiler_params=pltpu.CompilerParams(vmem_limit_bytes=LIMIT),
        name="advance",
    )(where, f, back, own, other, below, above, outer)


def ring(axis, step):
    count = lax.axis_size(axis)
    return [(i, (i + step) % count) for i in range(count)]


def local(distribution, plane_weights, depth_weights):
    place = lax.axis_index("vel").astype(jnp.int32).reshape(1)
    along = lax.axis_index("sy").astype(jnp.int32)
    core = jnp.bitwise_and(along, 1).reshape(1)
    where = jnp.stack([along, lax.axis_index("sx").astype(jnp.int32)])
    flip = lambda bit: [(i, i ^ bit) for i in range(8)]
    held = jnp.concatenate([plane_weights, lax.ppermute(plane_weights, "sy", flip(2))])
    held = jnp.concatenate([held, lax.ppermute(held, "sy", flip(4))])
    send, held = lax.optimization_barrier((pack(place, distribution), held))
    got = lax.all_to_all(send, "vel", 0, 0, tiled=True)
    held = jnp.concatenate([held, lax.ppermute(held, "sx", flip(4))])
    low, high, inner, outer = edges(core, held, distribution)
    above = lax.ppermute(low, "sx", ring("sx", -1))
    below = lax.ppermute(high, "sx", ring("sx", 1))
    across = lax.ppermute(held, "sx", [(i, (i + 2) % 8 if i % 2 == 0 else (i - 2) % 8) for i in range(8)])
    outer = lax.ppermute(outer, "sy", [(i, (i + 1) % 8 if i % 2 else (i - 1) % 8) for i in range(8)])
    send = relax(place, got, spread(depth_weights))
    own = join(held, above, below, across, inner)
    other = lax.ppermute(own, "sy", flip(1))
    back = lax.all_to_all(send, "vel", 0, 0, tiled=True)
    return advance(where, distribution, back, own, other, below, above, outer)


def solution(mesh):
    return jax.shard_map(
        local,
        mesh=mesh,
        in_specs=(P("sx", "sy", "vel"), P(("sx", "sy"), None), P()),
        out_specs=P("sx", "sy", "vel"),
        check_vma=False,
    )
```

```python
import jax
import jax.numpy as jnp
import numpy as np
from jax import lax
from jax.experimental import pallas as pl
from jax.experimental.pallas import tpu as pltpu
from jax.sharding import PartitionSpec as P

NVZ = 32
NVX = 32
NVY = 32
NXY = NVX * NVY
COURANT = 0.45
RELAX_RATE = 0.3
ROWS = 3
COLS = 32
CELLS = ROWS * COLS
PLANES = 4
GROUP = 8
BLOCK = NXY // GROUP
DATA = PLANES * CELLS
CHUNK = DATA + 16
TILE = 16
LIMIT = 16 << 20
F32 = jnp.float32
BF16 = jnp.bfloat16


def speed(index, count):
    return (index.astype(F32) - (count - 1) / 2.0) * (8.0 / count)


def lane_speeds(shape, offset):
    lane = lax.broadcasted_iota(jnp.int32, shape, len(shape) - 1) + offset
    return speed(lane // NVY, NVX), speed(lane % NVY, NVY)


def vmem():
    return pl.BlockSpec(memory_space=pltpu.VMEM)


def hbm():
    return pl.BlockSpec(memory_space=pltpu.HBM)


def smem():
    return pl.BlockSpec(memory_space=pltpu.SMEM)


def moment_basis():
    lane = np.arange(NXY)
    vx = (lane // NVY - (NVX - 1) / 2.0) * (8.0 / NVX)
    vy = (lane % NVY - (NVY - 1) / 2.0) * (8.0 / NVY)
    squared = (vx * vx + vy * vy).astype(np.float32)
    rough = squared.astype(BF16).astype(np.float32)
    basis = np.zeros((NXY, 128), np.float32)
    for part in range(3):
        basis[:, part * 5] = 1.0
        basis[:, part * 5 + 1] = vx
        basis[:, part * 5 + 2] = vy
        basis[:, part * 5 + 3] = 1.0
        basis[:, part * 5 + 4] = rough
        basis[:, 16 + part * 5 + 4] = squared - rough
        basis[:, 32 + part * 5 + 4] = 1.0
    return basis.astype(BF16)


def pack_kernel(place_ref, f_ref, basis_ref, send_ref, x_ref, base_ref, out_ref, in_sem, base_sem, out_sem):
    def load(p):
        lanes = pl.ds(p * NXY, NXY)
        return pltpu.make_async_copy(f_ref.at[:, :, lanes], x_ref.at[p], in_sem.at[p])

    def store(p):
        rows = pl.ds(p * CELLS, CELLS)
        return pltpu.make_async_copy(out_ref.at[:, rows, :], send_ref.at[:, rows, :], out_sem.at[p])

    base = pltpu.make_async_copy(basis_ref, base_ref, base_sem)
    load(0).start()
    base.start()
    for p in range(1, PLANES):
        load(p).start()
    lane = lax.broadcasted_iota(jnp.int32, (1, 128), 1)
    first_plane = place_ref[0] * PLANES
    total = jnp.zeros((CELLS, 128), F32)
    for p in range(PLANES):
        load(p).wait()
        x = x_ref[p].reshape(CELLS, NXY)
        for v in range(GROUP):
            out_ref[v, p * CELLS : (p + 1) * CELLS, :] = x[:, v * BLOCK : (v + 1) * BLOCK]
        store(p).start()
        if p == 0:
            base.wait()
        sums = jnp.dot(x, base_ref[...], preferred_element_type=F32)
        vz = speed(first_plane + p, NVZ)
        factor = jnp.where(lane >= 32, vz * vz, jnp.where((lane < 16) & (lane % 5 == 3), vz, 1.0))
        total = total + sums * factor
    total = jnp.transpose(total)
    total = (total[0:16, :] + total[16:32, :]) + total[32:48, :]
    column = lax.broadcasted_iota(jnp.int32, (16, CELLS), 0)
    high = total.astype(BF16).astype(F32)
    middle = (total - high).astype(BF16).astype(F32)
    low = (total - high) - middle
    parts = jnp.where(
        column < 5, high, jnp.where(column < 10, middle, jnp.where(column < 15, low, 0.0))
    )
    parts = jnp.concatenate([parts, jnp.zeros((16, 128 - CELLS), F32)], axis=1).astype(BF16)
    for v in range(GROUP):
        out_ref[v, DATA:CHUNK, :] = parts
    tail = pl.ds(DATA, CHUNK - DATA)
    last = pltpu.make_async_copy(
        out_ref.at[:, tail, :], send_ref.at[:, tail, :], out_sem.at[PLANES]
    )
    last.start()
    for p in range(PLANES):
        store(p).wait()
    last.wait()


def pack(place, f):
    basis = jnp.asarray(moment_basis())
    f, basis = (pltpu.with_memory_space_constraint(x, pltpu.HBM) for x in (f, basis))
    return pl.pallas_call(
        pack_kernel,
        out_shape=jax.ShapeDtypeStruct((GROUP, CHUNK, BLOCK), BF16),
        in_specs=[smem(), hbm(), hbm()],
        out_specs=hbm(),
        scratch_shapes=[
            pltpu.VMEM((PLANES, ROWS, COLS, NXY), BF16),
            pltpu.VMEM((NXY, 128), BF16),
            pltpu.VMEM((GROUP, CHUNK, BLOCK), BF16),
            pltpu.SemaphoreType.DMA((PLANES,)),
            pltpu.SemaphoreType.DMA(()),
            pltpu.SemaphoreType.DMA((PLANES + 1,)),
        ],
        compiler_params=pltpu.CompilerParams(vmem_limit_bytes=LIMIT),
        name="pack",
    )(place, f, basis)


def columns_kernel(core_ref, f_hbm, shard_hbm, pack_ref, inner_ref, first_ref, last_ref, sem):
    shard = shard_hbm.shape[0]
    copies = [
        pltpu.make_async_copy(f_hbm.at[:, pl.ds(0, 8), :], first_ref, sem.at[0]),
        pltpu.make_async_copy(f_hbm.at[:, pl.ds(COLS - 8, 8), :], last_ref, sem.at[1]),
        pltpu.make_async_copy(shard_hbm, pack_ref.at[pl.ds(0, shard)], sem.at[2]),
    ]
    for copy in copies:
        copy.start()
    edge_row = lax.broadcasted_iota(jnp.int32, (16, NXY), 0)
    first = jnp.zeros((16, NXY), F32)
    last = jnp.zeros((16, NXY), F32)
    for copy in copies:
        copy.wait()
    for r in range(ROWS):
        for p in range(PLANES):
            lanes = slice(p * NXY, (p + 1) * NXY)
            a = first_ref[r, :, lanes].astype(F32)[0:1, :]
            b = last_ref[r, :, lanes].astype(F32)[7:8, :]
            first = jnp.where(edge_row == r * PLANES + p, a, first)
            last = jnp.where(edge_row == r * PLANES + p, b, last)
    core = core_ref[0]
    inner_ref[...] = jnp.where(core == 0, last, first).astype(BF16)
    pack_ref[shard : shard + 16, :] = jnp.where(core == 0, first, last).astype(BF16)


def columns(core, f, shard):
    f, shard = (pltpu.with_memory_space_constraint(x, pltpu.HBM) for x in (f, shard))
    return pl.pallas_call(
        columns_kernel,
        out_shape=(
            jax.ShapeDtypeStruct((shard.shape[0] + 16, NXY), BF16),
            jax.ShapeDtypeStruct((16, NXY), BF16),
        ),
        in_specs=[smem(), hbm(), hbm()],
        out_specs=(vmem(), vmem()),
        scratch_shapes=[
            pltpu.VMEM((ROWS, 8, PLANES * NXY), BF16),
            pltpu.VMEM((ROWS, 8, PLANES * NXY), BF16),
            pltpu.SemaphoreType.DMA((3,)),
        ],
        compiler_params=pltpu.CompilerParams(vmem_limit_bytes=LIMIT),
        name="columns",
    )(core, f, shard)


def edges_kernel(held_ref, f_ref, low_ref, high_ref):
    half = NXY // 2
    size = held_ref.shape[0]
    low_ref[0:size, :] = held_ref[...]
    high_ref[0:size, :] = held_ref[...]
    for p in range(PLANES):
        rows = slice(size + p // 2 * COLS, size + (p // 2 + 1) * COLS)
        lanes = slice(p % 2 * half, (p % 2 + 1) * half)
        high_ref[rows, lanes] = f_ref[ROWS - 1, :, p * NXY + half : (p + 1) * NXY]
        low_ref[rows, lanes] = f_ref[0, :, p * NXY : p * NXY + half]


def edges(held, f):
    row = jax.ShapeDtypeStruct((held.shape[0] + 2 * COLS, NXY), BF16)
    return pl.pallas_call(
        edges_kernel,
        out_shape=(row, row),
        in_specs=[vmem(), vmem()],
        out_specs=(vmem(), vmem()),
        compiler_params=pltpu.CompilerParams(vmem_limit_bytes=LIMIT),
        name="edges",
    )(held, f)


def join_kernel(held_ref, above_ref, below_ref, across_ref, inner_ref, out_ref, sem):
    size = held_ref.shape[0]
    copies = []
    for m, ref in enumerate((held_ref, above_ref, below_ref, across_ref)):
        copies.append(
            pltpu.make_async_copy(
                ref.at[pl.ds(0, size)], out_ref.at[pl.ds(m * size, size)], sem.at[m]
            )
        )
    copies.append(
        pltpu.make_async_copy(inner_ref, out_ref.at[pl.ds(4 * size, 16)], sem.at[4])
    )
    for copy in copies:
        copy.start()
    for copy in copies:
        copy.wait()


def join(held, above, below, across, inner):
    return pl.pallas_call(
        join_kernel,
        out_shape=pltpu.HBM((4 * held.shape[0] + 16, NXY), BF16),
        in_specs=[hbm()] * 5,
        out_specs=hbm(),
        scratch_shapes=[pltpu.SemaphoreType.DMA((5,))],
        compiler_params=pltpu.CompilerParams(vmem_limit_bytes=LIMIT),
        name="join",
    )(held, above, below, across, inner)


def spread_kernel(depth_ref, out_ref):
    size = NVZ * TILE
    row = lax.broadcasted_iota(jnp.int32, (size, NVZ), 0)
    col = lax.broadcasted_iota(jnp.int32, (size, NVZ), 1)
    pick = jnp.where(row // TILE == col, 1.0, 0.0).astype(BF16)
    left = jnp.dot(pick, depth_ref[...], preferred_element_type=F32).astype(BF16)
    full = lax.dot_general(left, pick, (((1,), (1,)), ((), ())), preferred_element_type=F32)
    i = lax.broadcasted_iota(jnp.int32, (size, size), 0)
    j = lax.broadcasted_iota(jnp.int32, (size, size), 1)
    out_ref[...] = jnp.where(i % TILE == j % TILE, full, 0.0).astype(BF16)


def spread(depth_weights):
    size = NVZ * TILE
    return pl.pallas_call(
        spread_kernel,
        out_shape=jax.ShapeDtypeStruct((size, size), BF16),
        in_specs=[vmem()],
        out_specs=vmem(),
        compiler_params=pltpu.CompilerParams(vmem_limit_bytes=LIMIT),
        name="spread",
    )(depth_weights)


def relax_kernel(place_ref, got_ref, mix_ref, send_ref, dev_ref):
    pieces = jnp.concatenate([got_ref[v, DATA:CHUNK, :] for v in range(GROUP)], axis=0)
    i = lax.broadcasted_iota(jnp.int32, (GROUP * 16, 128), 0) % 16
    j = lax.broadcasted_iota(jnp.int32, (GROUP * 16, 128), 1)
    pick = jnp.where((i % 5 == j) & (i < 15), 1.0, 0.0).astype(BF16)
    moments = lax.dot_general(pieces, pick, (((0,), (0,)), ((), ())), preferred_element_type=F32)
    moments = moments[:CELLS, :]
    density = moments[:, 0:1]
    ux = moments[:, 1:2] / density
    uy = moments[:, 2:3] / density
    uz = moments[:, 3:4] / density
    heat = (moments[:, 4:5] / density - (ux * ux + uy * uy + uz * uz)) / 3.0
    measure = (8.0 / NVX) * (8.0 / NVY) * (8.0 / NVZ)
    width = 2.0 * jnp.pi * heat
    scale = density * measure / (width * jnp.sqrt(width))
    inverse = -1.0 / (2.0 * heat)
    vx, vy = lane_speeds((CELLS, BLOCK), place_ref[0] * BLOCK)
    dx = vx - ux
    dy = vy - uy
    plane = scale * jnp.exp((dx * dx + dy * dy) * inverse)
    dz = speed(lax.broadcasted_iota(jnp.int32, (CELLS, 128), 1), NVZ) - uz
    depth = jnp.exp((dz * dz) * inverse)
    for w in range(NVZ):
        v, p = w // PLANES, w % PLANES
        f = got_ref[v, p * CELLS : (p + 1) * CELLS, :].astype(F32)
        deviation = (depth[:, w : w + 1] * plane - f).astype(BF16)
        for t in range(CELLS // TILE):
            dev_ref[w * TILE : (w + 1) * TILE, t * BLOCK : (t + 1) * BLOCK] = deviation[
                t * TILE : (t + 1) * TILE, :
            ]
    mixed = jnp.dot(mix_ref[...], dev_ref[...], preferred_element_type=F32).astype(BF16)
    for w in range(NVZ):
        v, p = w // PLANES, w % PLANES
        for t in range(CELLS // TILE):
            send_ref[v, p * CELLS + t * TILE : p * CELLS + (t + 1) * TILE, :] = mixed[
                w * TILE : (w + 1) * TILE, t * BLOCK : (t + 1) * BLOCK
            ]


def relax(place, got, mix):
    return pl.pallas_call(
        relax_kernel,
        out_shape=jax.ShapeDtypeStruct((GROUP, DATA, BLOCK), BF16),
        in_specs=[smem(), vmem(), vmem()],
        out_specs=vmem(),
        scratch_shapes=[pltpu.VMEM((NVZ * TILE, CELLS // TILE * BLOCK), BF16)],
        compiler_params=pltpu.CompilerParams(vmem_limit_bytes=LIMIT),
        name="relax",
    )(place, got, mix)


def advance_kernel(
    where_ref,
    f_hbm,
    back_hbm,
    own_hbm,
    other_hbm,
    below_hbm,
    above_hbm,
    outer_hbm,
    out_hbm,
    f_ref,
    back_ref,
    weights_ref,
    lower_ref,
    upper_ref,
    inner_ref,
    outer_ref,
    moved_ref,
    out_ref,
    sem,
    out_sem,
):
    edge = pl.ds(below_hbm.shape[0] - 2 * COLS, 2 * COLS)
    first = [
        pltpu.make_async_copy(below_hbm.at[edge], lower_ref, sem.at[0]),
        pltpu.make_async_copy(above_hbm.at[edge], upper_ref, sem.at[1]),
        pltpu.make_async_copy(other_hbm.at[pl.ds(NXY // 2, 16)], inner_ref, sem.at[2]),
        pltpu.make_async_copy(outer_hbm.at[pl.ds(outer_hbm.shape[0] - 16, 16)], outer_ref, sem.at[3]),
        pltpu.make_async_copy(f_hbm, f_ref, sem.at[4]),
    ]
    second = [pltpu.make_async_copy(back_hbm, back_ref, sem.at[5])]
    mine, y = where_ref[0], where_ref[1]
    far = jnp.where(y % 2 == 0, y + 6, y + 2)
    for side, ref in ((mine, own_hbm), (jnp.bitwise_xor(mine, 1), other_hbm)):
        turn = jnp.bitwise_xor(side, 4)
        step = jnp.where(side % 2 == 1, 1, 7)
        places = (side, (side + step) % 8, turn, (turn + step) % 8)
        for m, base in enumerate((y, y + 1, y + 7, far)):
            for i in range(2):
                row = (base + 4 * i) % 8 * 8
                for j in range(4):
                    block = pl.ds((m * 8 + i * 4 + j) * 16, 16)
                    place = row + places[j]
                    second.append(
                        pltpu.make_async_copy(
                            ref.at[block], weights_ref.at[place], sem.at[5 + len(second)]
                        )
                    )
    for copy in first + second:
        copy.start()
    half = NXY // 2
    vx, vy = lane_speeds((COLS, NXY), 0)
    courant_across = COURANT / (4.0 - 4.0 / NVX)
    courant_along = COURANT / (4.0 - 4.0 / NVY)
    cx = courant_across * jnp.abs(vx)
    cy = courant_along * jnp.abs(vy)
    upwind = vy > 0.0
    col = lax.broadcasted_iota(jnp.int32, (COLS, NXY), 0)
    core = mine % 2
    for copy in first:
        copy.wait()
    inner = inner_ref[...].astype(F32)
    outer = outer_ref[...].astype(F32)
    left_edge = jnp.where(core == 0, outer, inner)
    right_edge = jnp.where(core == 0, inner, outer)
    for p in range(PLANES):
        lanes = slice(p * NXY, (p + 1) * NXY)
        first_half = slice(p * NXY, p * NXY + half)
        second_half = slice(p * NXY + half, (p + 1) * NXY)
        rows = slice(p // 2 * COLS, (p // 2 + 1) * COLS)
        packed = slice(p % 2 * half, (p % 2 + 1) * half)
        for r in range(ROWS):
            current = f_ref[r, :, lanes].astype(F32)
            above = upper_ref[rows, packed] if r == ROWS - 1 else f_ref[r + 1, :, first_half]
            below = lower_ref[rows, packed] if r == 0 else f_ref[r - 1, :, second_half]
            across = jnp.concatenate([above, below], axis=1).astype(F32)
            left = left_edge[r * PLANES + p : r * PLANES + p + 1, :]
            right = right_edge[r * PLANES + p : r * PLANES + p + 1, :]
            left = jnp.where(col == 0, left, pltpu.roll(current, 1, 0))
            right = jnp.where(col == COLS - 1, right, pltpu.roll(current, COLS - 1, 0))
            along = jnp.where(upwind, left, right)
            start = p * CELLS + r * COLS
            moved_ref[start : start + COLS, :] = current - (
                cx * (current - across) + cy * (current - along)
            )
    for copy in second:
        copy.wait()
    mixed = jnp.concatenate([back_ref[v] for v in range(GROUP)], axis=1)
    weights = weights_ref[...].reshape(NXY, NXY)
    collision = lax.dot_general(
        mixed, weights, (((1,), (1,)), ((), ())), preferred_element_type=F32
    )
    stores = []
    for p in range(PLANES):
        for r in range(ROWS):
            start = p * CELLS + r * COLS
            value = moved_ref[start : start + COLS, :] + RELAX_RATE * collision[start : start + COLS, :]
            out_ref[r, :, p * NXY : (p + 1) * NXY] = value.astype(BF16)
        lanes = pl.ds(p * NXY, NXY)
        stores.append(
            pltpu.make_async_copy(
                out_ref.at[:, :, lanes], out_hbm.at[:, :, lanes], out_sem.at[p]
            )
        )
        stores[-1].start()
    for copy in stores:
        copy.wait()


def advance(where, f, back, own, other, below, above, outer):
    own, other = (pltpu.with_memory_space_constraint(x, pltpu.HBM) for x in (own, other))
    return pl.pallas_call(
        advance_kernel,
        out_shape=jax.ShapeDtypeStruct(f.shape, BF16),
        in_specs=[smem()] + [hbm()] * 7,
        out_specs=hbm(),
        scratch_shapes=[
            pltpu.VMEM(f.shape, BF16),
            pltpu.VMEM(back.shape, BF16),
            pltpu.VMEM((NXY // 16, 16, NXY), BF16),
            pltpu.VMEM((2 * COLS, NXY), BF16),
            pltpu.VMEM((2 * COLS, NXY), BF16),
            pltpu.VMEM((16, NXY), BF16),
            pltpu.VMEM((16, NXY), BF16),
            pltpu.VMEM((DATA, NXY), F32),
            pltpu.VMEM(f.shape, BF16),
            pltpu.SemaphoreType.DMA((6 + NXY // 16,)),
            pltpu.SemaphoreType.DMA((PLANES,)),
        ],
        compiler_params=pltpu.CompilerParams(vmem_limit_bytes=LIMIT),
        name="advance",
    )(where, f, back, own, other, below, above, outer)


def ring(axis, step):
    count = lax.axis_size(axis)
    return [(i, (i + step) % count) for i in range(count)]


def local(distribution, plane_weights, depth_weights):
    place = lax.axis_index("vel").astype(jnp.int32).reshape(1)
    along = lax.axis_index("sy").astype(jnp.int32)
    core = jnp.bitwise_and(along, 1).reshape(1)
    where = jnp.stack([along, lax.axis_index("sx").astype(jnp.int32)])
    flip = lambda bit: [(i, i ^ bit) for i in range(8)]
    bundle, inner = columns(core, distribution, plane_weights)
    outer = lax.ppermute(bundle, "sy", [(i, (i + 1) % 8 if i % 2 else (i - 1) % 8) for i in range(8)])
    held = jnp.concatenate([plane_weights, outer[: plane_weights.shape[0]]])
    held = jnp.concatenate([held, lax.ppermute(held, "sy", flip(4))])
    send, held = lax.optimization_barrier((pack(place, distribution), held))
    got = lax.all_to_all(send, "vel", 0, 0, tiled=True)
    held = jnp.concatenate([held, lax.ppermute(held, "sx", flip(4))])
    low, high = edges(held, distribution)
    above = lax.ppermute(low, "sx", ring("sx", -1))
    below = lax.ppermute(high, "sx", ring("sx", 1))
    across = lax.ppermute(held, "sx", [(i, (i + 2) % 8 if i % 2 == 0 else (i - 2) % 8) for i in range(8)])
    send = relax(place, got, spread(depth_weights))
    own = join(held, above, below, across, inner)
    other = lax.ppermute(own, "sy", flip(1))
    back = lax.all_to_all(send, "vel", 0, 0, tiled=True)
    return advance(where, distribution, back, own, other, below, above, outer)


def solution(mesh):
    return jax.shard_map(
        local,
        mesh=mesh,
        in_specs=(P("sx", "sy", "vel"), P(("sx", "sy"), None), P()),
        out_specs=P("sx", "sy", "vel"),
        check_vma=False,
    )
```

```python
import jax
import jax.numpy as jnp
import numpy as np
from jax import lax
from jax.experimental import pallas as pl
from jax.experimental.pallas import tpu as pltpu
from jax.sharding import PartitionSpec as P

NVZ = 32
NVX = 32
NVY = 32
NXY = NVX * NVY
COURANT = 0.45
RELAX_RATE = 0.3
ROWS = 3
COLS = 32
CELLS = ROWS * COLS
PLANES = 4
GROUP = 8
BLOCK = NXY // GROUP
DATA = PLANES * CELLS
CHUNK = DATA + 16
TILE = 16
LIMIT = 16 << 20
F32 = jnp.float32
BF16 = jnp.bfloat16


def speed(index, count):
    return (index.astype(F32) - (count - 1) / 2.0) * (8.0 / count)


def lane_speeds(shape, offset):
    lane = lax.broadcasted_iota(jnp.int32, shape, len(shape) - 1) + offset
    return speed(lane // NVY, NVX), speed(lane % NVY, NVY)


def vmem():
    return pl.BlockSpec(memory_space=pltpu.VMEM)


def hbm():
    return pl.BlockSpec(memory_space=pltpu.HBM)


def smem():
    return pl.BlockSpec(memory_space=pltpu.SMEM)


def moment_basis():
    lane = np.arange(NXY)
    vx = (lane // NVY - (NVX - 1) / 2.0) * (8.0 / NVX)
    vy = (lane % NVY - (NVY - 1) / 2.0) * (8.0 / NVY)
    squared = (vx * vx + vy * vy).astype(np.float32)
    rough = squared.astype(BF16).astype(np.float32)
    basis = np.zeros((NXY, 128), np.float32)
    for part in range(3):
        basis[:, part * 5] = 1.0
        basis[:, part * 5 + 1] = vx
        basis[:, part * 5 + 2] = vy
        basis[:, part * 5 + 3] = 1.0
        basis[:, part * 5 + 4] = rough
        basis[:, 16 + part * 5 + 4] = squared - rough
        basis[:, 32 + part * 5 + 4] = 1.0
    return basis.astype(BF16)


def pack_kernel(place_ref, f_ref, basis_ref, send_ref, x_ref, base_ref, out_ref, in_sem, base_sem, out_sem):
    def load(p):
        lanes = pl.ds(p * NXY, NXY)
        return pltpu.make_async_copy(f_ref.at[:, :, lanes], x_ref.at[p], in_sem.at[p])

    def store(p):
        rows = pl.ds(p * CELLS, CELLS)
        return pltpu.make_async_copy(out_ref.at[:, rows, :], send_ref.at[:, rows, :], out_sem.at[p])

    base = pltpu.make_async_copy(basis_ref, base_ref, base_sem)
    load(0).start()
    base.start()
    for p in range(1, PLANES):
        load(p).start()
    lane = lax.broadcasted_iota(jnp.int32, (1, 128), 1)
    first_plane = place_ref[0] * PLANES
    total = jnp.zeros((CELLS, 128), F32)
    for p in range(PLANES):
        load(p).wait()
        x = x_ref[p].reshape(CELLS, NXY)
        for v in range(GROUP):
            out_ref[v, p * CELLS : (p + 1) * CELLS, :] = x[:, v * BLOCK : (v + 1) * BLOCK]
        store(p).start()
        if p == 0:
            base.wait()
        sums = jnp.dot(x, base_ref[...], preferred_element_type=F32)
        vz = speed(first_plane + p, NVZ)
        factor = jnp.where(lane >= 32, vz * vz, jnp.where((lane < 16) & (lane % 5 == 3), vz, 1.0))
        total = total + sums * factor
    total = jnp.transpose(total)
    total = (total[0:16, :] + total[16:32, :]) + total[32:48, :]
    column = lax.broadcasted_iota(jnp.int32, (16, CELLS), 0)
    high = total.astype(BF16).astype(F32)
    middle = (total - high).astype(BF16).astype(F32)
    low = (total - high) - middle
    parts = jnp.where(
        column < 5, high, jnp.where(column < 10, middle, jnp.where(column < 15, low, 0.0))
    )
    parts = jnp.concatenate([parts, jnp.zeros((16, 128 - CELLS), F32)], axis=1).astype(BF16)
    for v in range(GROUP):
        out_ref[v, DATA:CHUNK, :] = parts
    tail = pl.ds(DATA, CHUNK - DATA)
    last = pltpu.make_async_copy(
        out_ref.at[:, tail, :], send_ref.at[:, tail, :], out_sem.at[PLANES]
    )
    last.start()
    for p in range(PLANES):
        store(p).wait()
    last.wait()


def pack(place, f):
    basis = jnp.asarray(moment_basis())
    f, basis = (pltpu.with_memory_space_constraint(x, pltpu.HBM) for x in (f, basis))
    return pl.pallas_call(
        pack_kernel,
        out_shape=jax.ShapeDtypeStruct((GROUP, CHUNK, BLOCK), BF16),
        in_specs=[smem(), hbm(), hbm()],
        out_specs=hbm(),
        scratch_shapes=[
            pltpu.VMEM((PLANES, ROWS, COLS, NXY), BF16),
            pltpu.VMEM((NXY, 128), BF16),
            pltpu.VMEM((GROUP, CHUNK, BLOCK), BF16),
            pltpu.SemaphoreType.DMA((PLANES,)),
            pltpu.SemaphoreType.DMA(()),
            pltpu.SemaphoreType.DMA((PLANES + 1,)),
        ],
        compiler_params=pltpu.CompilerParams(vmem_limit_bytes=LIMIT),
        name="pack",
    )(place, f, basis)


def edges_kernel(core_ref, held_ref, f_ref, low_ref, high_ref, inner_ref, outer_ref):
    half = NXY // 2
    size = held_ref.shape[0]
    low_ref[0:size, :] = held_ref[...]
    high_ref[0:size, :] = held_ref[...]
    for p in range(PLANES):
        rows = slice(size + p // 2 * COLS, size + (p // 2 + 1) * COLS)
        lanes = slice(p % 2 * half, (p % 2 + 1) * half)
        high_ref[rows, lanes] = f_ref[ROWS - 1, :, p * NXY + half : (p + 1) * NXY]
        low_ref[rows, lanes] = f_ref[0, :, p * NXY : p * NXY + half]
    edge_row = lax.broadcasted_iota(jnp.int32, (16, NXY), 0)
    first = jnp.zeros((16, NXY), F32)
    last = jnp.zeros((16, NXY), F32)
    for r in range(ROWS):
        for p in range(PLANES):
            lanes = slice(p * NXY, (p + 1) * NXY)
            a = f_ref[r, 0:8, lanes].astype(F32)[0:1, :]
            b = f_ref[r, COLS - 8 : COLS, lanes].astype(F32)[7:8, :]
            first = jnp.where(edge_row == r * PLANES + p, a, first)
            last = jnp.where(edge_row == r * PLANES + p, b, last)
    core = core_ref[0]
    inner_ref[...] = jnp.where(core == 0, last, first).astype(BF16)
    outer_ref[...] = jnp.where(core == 0, first, last).astype(BF16)


def edges(core, held, f):
    row = jax.ShapeDtypeStruct((held.shape[0] + 2 * COLS, NXY), BF16)
    column = jax.ShapeDtypeStruct((16, NXY), BF16)
    return pl.pallas_call(
        edges_kernel,
        out_shape=(row, row, column, column),
        in_specs=[smem(), vmem(), vmem()],
        out_specs=(vmem(),) * 4,
        compiler_params=pltpu.CompilerParams(vmem_limit_bytes=LIMIT),
        name="edges",
    )(core, held, f)


def join_kernel(held_ref, above_ref, below_ref, across_ref, inner_ref, out_ref, sem):
    size = held_ref.shape[0]
    copies = []
    for m, ref in enumerate((held_ref, above_ref, below_ref, across_ref)):
        copies.append(
            pltpu.make_async_copy(
                ref.at[pl.ds(0, size)], out_ref.at[pl.ds(m * size, size)], sem.at[m]
            )
        )
    copies.append(
        pltpu.make_async_copy(inner_ref, out_ref.at[pl.ds(4 * size, 16)], sem.at[4])
    )
    for copy in copies:
        copy.start()
    for copy in copies:
        copy.wait()


def join(held, above, below, across, inner):
    return pl.pallas_call(
        join_kernel,
        out_shape=pltpu.HBM((4 * held.shape[0] + 16, NXY), BF16),
        in_specs=[hbm()] * 5,
        out_specs=hbm(),
        scratch_shapes=[pltpu.SemaphoreType.DMA((5,))],
        compiler_params=pltpu.CompilerParams(vmem_limit_bytes=LIMIT),
        name="join",
    )(held, above, below, across, inner)


def spread_kernel(depth_ref, out_ref):
    size = NVZ * TILE
    row = lax.broadcasted_iota(jnp.int32, (size, NVZ), 0)
    col = lax.broadcasted_iota(jnp.int32, (size, NVZ), 1)
    pick = jnp.where(row // TILE == col, 1.0, 0.0).astype(BF16)
    left = jnp.dot(pick, depth_ref[...], preferred_element_type=F32).astype(BF16)
    full = lax.dot_general(left, pick, (((1,), (1,)), ((), ())), preferred_element_type=F32)
    i = lax.broadcasted_iota(jnp.int32, (size, size), 0)
    j = lax.broadcasted_iota(jnp.int32, (size, size), 1)
    out_ref[...] = jnp.where(i % TILE == j % TILE, full, 0.0).astype(BF16)


def spread(depth_weights):
    size = NVZ * TILE
    return pl.pallas_call(
        spread_kernel,
        out_shape=jax.ShapeDtypeStruct((size, size), BF16),
        in_specs=[vmem()],
        out_specs=vmem(),
        compiler_params=pltpu.CompilerParams(vmem_limit_bytes=LIMIT),
        name="spread",
    )(depth_weights)


def relax_kernel(place_ref, got_ref, mix_ref, send_ref, dev_ref):
    pieces = jnp.concatenate([got_ref[v, DATA:CHUNK, :] for v in range(GROUP)], axis=0)
    i = lax.broadcasted_iota(jnp.int32, (GROUP * 16, 128), 0) % 16
    j = lax.broadcasted_iota(jnp.int32, (GROUP * 16, 128), 1)
    pick = jnp.where((i % 5 == j) & (i < 15), 1.0, 0.0).astype(BF16)
    moments = lax.dot_general(pieces, pick, (((0,), (0,)), ((), ())), preferred_element_type=F32)
    moments = moments[:CELLS, :]
    density = moments[:, 0:1]
    ux = moments[:, 1:2] / density
    uy = moments[:, 2:3] / density
    uz = moments[:, 3:4] / density
    heat = (moments[:, 4:5] / density - (ux * ux + uy * uy + uz * uz)) / 3.0
    measure = (8.0 / NVX) * (8.0 / NVY) * (8.0 / NVZ)
    width = 2.0 * jnp.pi * heat
    scale = density * measure / (width * jnp.sqrt(width))
    inverse = -1.0 / (2.0 * heat)
    vx, vy = lane_speeds((CELLS, BLOCK), place_ref[0] * BLOCK)
    dx = vx - ux
    dy = vy - uy
    plane = scale * jnp.exp((dx * dx + dy * dy) * inverse)
    dz = speed(lax.broadcasted_iota(jnp.int32, (CELLS, 128), 1), NVZ) - uz
    depth = jnp.exp((dz * dz) * inverse)
    for w in range(NVZ):
        v, p = w // PLANES, w % PLANES
        f = got_ref[v, p * CELLS : (p + 1) * CELLS, :].astype(F32)
        deviation = (depth[:, w : w + 1] * plane - f).astype(BF16)
        for t in range(CELLS // TILE):
            dev_ref[w * TILE : (w + 1) * TILE, t * BLOCK : (t + 1) * BLOCK] = deviation[
                t * TILE : (t + 1) * TILE, :
            ]
    mixed = jnp.dot(mix_ref[...], dev_ref[...], preferred_element_type=F32).astype(BF16)
    for w in range(NVZ):
        v, p = w // PLANES, w % PLANES
        for t in range(CELLS // TILE):
            send_ref[v, p * CELLS + t * TILE : p * CELLS + (t + 1) * TILE, :] = mixed[
                w * TILE : (w + 1) * TILE, t * BLOCK : (t + 1) * BLOCK
            ]


def relax(place, got, mix):
    return pl.pallas_call(
        relax_kernel,
        out_shape=jax.ShapeDtypeStruct((GROUP, DATA, BLOCK), BF16),
        in_specs=[smem(), vmem(), vmem()],
        out_specs=vmem(),
        scratch_shapes=[pltpu.VMEM((NVZ * TILE, CELLS // TILE * BLOCK), BF16)],
        compiler_params=pltpu.CompilerParams(vmem_limit_bytes=LIMIT),
        name="relax",
    )(place, got, mix)


def advance_kernel(
    where_ref,
    f_hbm,
    back_hbm,
    own_hbm,
    other_hbm,
    below_hbm,
    above_hbm,
    outer_hbm,
    out_hbm,
    f_ref,
    back_ref,
    weights_ref,
    lower_ref,
    upper_ref,
    inner_ref,
    outer_ref,
    moved_ref,
    out_ref,
    sem,
    out_sem,
):
    edge = pl.ds(below_hbm.shape[0] - 2 * COLS, 2 * COLS)
    first = [
        pltpu.make_async_copy(below_hbm.at[edge], lower_ref, sem.at[0]),
        pltpu.make_async_copy(above_hbm.at[edge], upper_ref, sem.at[1]),
        pltpu.make_async_copy(other_hbm.at[pl.ds(NXY // 2, 16)], inner_ref, sem.at[2]),
        pltpu.make_async_copy(outer_hbm.at[pl.ds(outer_hbm.shape[0] - 16, 16)], outer_ref, sem.at[3]),
        pltpu.make_async_copy(f_hbm, f_ref, sem.at[4]),
    ]
    second = [pltpu.make_async_copy(back_hbm, back_ref, sem.at[5])]
    mine, y = where_ref[0], where_ref[1]
    far = jnp.where(y % 2 == 0, y + 6, y + 2)
    for side, ref in ((mine, own_hbm), (jnp.bitwise_xor(mine, 1), other_hbm)):
        for m, base in enumerate((y, y + 1, y + 7, far)):
            for i in range(2):
                row = (base + 4 * i) % 8 * 8
                for j in range(4):
                    block = pl.ds((m * 8 + i * 4 + j) * 16, 16)
                    place = row + jnp.bitwise_xor(side, 2 * j)
                    second.append(
                        pltpu.make_async_copy(
                            ref.at[block], weights_ref.at[place], sem.at[5 + len(second)]
                        )
                    )
    for copy in first + second:
        copy.start()
    half = NXY // 2
    vx, vy = lane_speeds((COLS, NXY), 0)
    courant_across = COURANT / (4.0 - 4.0 / NVX)
    courant_along = COURANT / (4.0 - 4.0 / NVY)
    cx = courant_across * jnp.abs(vx)
    cy = courant_along * jnp.abs(vy)
    upwind = vy > 0.0
    col = lax.broadcasted_iota(jnp.int32, (COLS, NXY), 0)
    core = mine % 2
    for copy in first:
        copy.wait()
    inner = inner_ref[...].astype(F32)
    outer = outer_ref[...].astype(F32)
    left_edge = jnp.where(core == 0, outer, inner)
    right_edge = jnp.where(core == 0, inner, outer)
    for p in range(PLANES):
        lanes = slice(p * NXY, (p + 1) * NXY)
        first_half = slice(p * NXY, p * NXY + half)
        second_half = slice(p * NXY + half, (p + 1) * NXY)
        rows = slice(p // 2 * COLS, (p // 2 + 1) * COLS)
        packed = slice(p % 2 * half, (p % 2 + 1) * half)
        for r in range(ROWS):
            current = f_ref[r, :, lanes].astype(F32)
            above = upper_ref[rows, packed] if r == ROWS - 1 else f_ref[r + 1, :, first_half]
            below = lower_ref[rows, packed] if r == 0 else f_ref[r - 1, :, second_half]
            across = jnp.concatenate([above, below], axis=1).astype(F32)
            left = left_edge[r * PLANES + p : r * PLANES + p + 1, :]
            right = right_edge[r * PLANES + p : r * PLANES + p + 1, :]
            left = jnp.where(col == 0, left, pltpu.roll(current, 1, 0))
            right = jnp.where(col == COLS - 1, right, pltpu.roll(current, COLS - 1, 0))
            along = jnp.where(upwind, left, right)
            start = p * CELLS + r * COLS
            moved_ref[start : start + COLS, :] = current - (
                cx * (current - across) + cy * (current - along)
            )
    for copy in second:
        copy.wait()
    mixed = jnp.concatenate([back_ref[v] for v in range(GROUP)], axis=1)
    weights = weights_ref[...].reshape(NXY, NXY)
    collision = lax.dot_general(
        mixed, weights, (((1,), (1,)), ((), ())), preferred_element_type=F32
    )
    stores = []
    for p in range(PLANES):
        for r in range(ROWS):
            start = p * CELLS + r * COLS
            value = moved_ref[start : start + COLS, :] + RELAX_RATE * collision[start : start + COLS, :]
            out_ref[r, :, p * NXY : (p + 1) * NXY] = value.astype(BF16)
        lanes = pl.ds(p * NXY, NXY)
        stores.append(
            pltpu.make_async_copy(
                out_ref.at[:, :, lanes], out_hbm.at[:, :, lanes], out_sem.at[p]
            )
        )
        stores[-1].start()
    for copy in stores:
        copy.wait()


def advance(where, f, back, own, other, below, above, outer):
    own, other = (pltpu.with_memory_space_constraint(x, pltpu.HBM) for x in (own, other))
    return pl.pallas_call(
        advance_kernel,
        out_shape=jax.ShapeDtypeStruct(f.shape, BF16),
        in_specs=[smem()] + [hbm()] * 7,
        out_specs=hbm(),
        scratch_shapes=[
            pltpu.VMEM(f.shape, BF16),
            pltpu.VMEM(back.shape, BF16),
            pltpu.VMEM((NXY // 16, 16, NXY), BF16),
            pltpu.VMEM((2 * COLS, NXY), BF16),
            pltpu.VMEM((2 * COLS, NXY), BF16),
            pltpu.VMEM((16, NXY), BF16),
            pltpu.VMEM((16, NXY), BF16),
            pltpu.VMEM((DATA, NXY), F32),
            pltpu.VMEM(f.shape, BF16),
            pltpu.SemaphoreType.DMA((6 + NXY // 16,)),
            pltpu.SemaphoreType.DMA((PLANES,)),
        ],
        compiler_params=pltpu.CompilerParams(vmem_limit_bytes=LIMIT),
        name="advance",
    )(where, f, back, own, other, below, above, outer)


def ring(axis, step):
    count = lax.axis_size(axis)
    return [(i, (i + step) % count) for i in range(count)]


def local(distribution, plane_weights, depth_weights):
    place = lax.axis_index("vel").astype(jnp.int32).reshape(1)
    along = lax.axis_index("sy").astype(jnp.int32)
    core = jnp.bitwise_and(along, 1).reshape(1)
    where = jnp.stack([along, lax.axis_index("sx").astype(jnp.int32)])
    flip = lambda bit: [(i, i ^ bit) for i in range(8)]
    held = jnp.concatenate([plane_weights, lax.ppermute(plane_weights, "sy", flip(2))])
    held = jnp.concatenate([held, lax.ppermute(held, "sy", flip(4))])
    send, held = lax.optimization_barrier((pack(place, distribution), held))
    got = lax.all_to_all(send, "vel", 0, 0, tiled=True)
    held = jnp.concatenate([held, lax.ppermute(held, "sx", flip(4))])
    low, high, inner, outer = edges(core, held, distribution)
    above = lax.ppermute(low, "sx", ring("sx", -1))
    below = lax.ppermute(high, "sx", ring("sx", 1))
    across = lax.ppermute(held, "sx", [(i, (i + 2) % 8 if i % 2 == 0 else (i - 2) % 8) for i in range(8)])
    outer = lax.ppermute(outer, "sy", [(i, (i + 1) % 8 if i % 2 else (i - 1) % 8) for i in range(8)])
    send = relax(place, got, spread(depth_weights))
    send, outer = lax.optimization_barrier((send, outer))
    own = join(held, above, below, across, inner)
    other = lax.ppermute(own, "sy", flip(1))
    back = lax.all_to_all(send, "vel", 0, 0, tiled=True)
    return advance(where, distribution, back, own, other, below, above, outer)


def solution(mesh):
    return jax.shard_map(
        local,
        mesh=mesh,
        in_specs=(P("sx", "sy", "vel"), P(("sx", "sy"), None), P()),
        out_specs=P("sx", "sy", "vel"),
        check_vma=False,
    )
```
